32 devices in a mesh: mem: 16 (over z, y, x), row: 2 (over core).
Axes of the slice: x: 2, y: 2, z: 4, core: 2. Of those that a mesh axis runs over, the one named last changes fastest.
Arguments:
- realization_stack: float32 [16, 5, 32, 256], P('mem', None, 'row'), may hold values from -6 to 6
- velocity: float32 [2, 32, 256], P(None, 'row'), may hold values from -0.25 to 0.25
- diffusion: float32 [5], replicated, may hold values from 0.04 to 0.12
- obs_cell: int32 [2048], replicated, may hold values from 0 to 40959
- obs_order: int32 [2048], replicated, may hold values from 0 to 2047, each once
- obs_value: float32 [2048], replicated, may hold values from -6 to 6
- obs_var: float32 [2048], replicated, may hold values from 0.2 to 2
- field_mask: int32 [5, 5], replicated, may hold values 0 or 1
Outputs:
- analysis: float32 [16, 5, 2, 16, 256], P(None, None, 'row', 'mem')
The draws below stay inside these ranges and needn't reach their ends.
Inputs may be any that keep to these rules, and one draw needn't show every extreme that they name: `obs_cell`: a flat index field * 32 * 256 + row * 256 + column. `obs_order`: each of 0 to 2047 exactly once.
All inputs are finite; a program needn't handle non-finite values.
Results may differ from the reference program's by a relative error of at most 0.0003.
Values sent between devices are 32-bit elements; how exact they have to be, the bound alone decides.
No kernel may reach another device: no remote copies, remote signals or barrier semaphores. Data moves between devices by JAX's collectives and lax.ppermute only.
A program may use at most 64 MiB of HBM per device.

```python
import math
import jax
import jax.numpy as jnp
from jax import lax

LEVEL_VARIABLES = 5
TILE_LONGITUDES = 256
SHARD_LATITUDES = 1
SUBSTEPS = 4
OBS_BATCH = 1024
BATCHES = 2
LOC_HALF = 32
REALIZATIONS = 16
ROWS_DEV = 16
SLABS = 2
NR = 32
OBS = 2048
CELLS = 40960


def touch_ends(entries, rng, least, top_value):
    longest = entries.shape.index(max(entries.shape))
    spots = []
    for shift in (0, 1):
        where = [jax.random.randint(jax.random.fold_in(rng, axis), (), 0, length) for axis, length in enumerate(entries.shape)]
        where[longest] = (where[longest] + shift) % entries.shape[longest]
        spots.append(tuple(where))
    return entries.at[spots[0]].set(least).at[spots[1]].set(top_value)


def level_of(own_key, shape, split, least, top_value):
    loudness = 1.0
    for dim, parts in split:
        steps = jax.random.uniform(jax.random.fold_in(jax.random.fold_in(own_key, 6), dim), (parts,), jnp.float32, least / len(split), top_value / len(split))
        loudness = loudness * jnp.repeat(jnp.exp(steps), shape[dim] // parts).reshape((-1,) + (1,) * (len(shape) - 1 - dim))
    return loudness


def bell_draw(stream_key, shape, scale, most, shards=(), kind=jnp.bfloat16):
    gain = level_of(stream_key, shape, shards, -0.22, 0.18) if shards else 1.0
    drawn = jax.random.normal(stream_key, shape, jnp.float32) * scale * gain
    return jnp.minimum(jnp.maximum(drawn, -most), most).astype(kind)


def setup_inputs(seed: int = 0) -> dict:
    seeds = jax.random.split(jax.random.key(seed), 9)
    realization_stack = bell_draw(seeds[0], (REALIZATIONS, LEVEL_VARIABLES, NR, TILE_LONGITUDES), 1.0, 6.0, ((0, 16), (2, 2)), jnp.float32)
    velocity = jnp.clip(jax.random.uniform(seeds[1], (2, NR, TILE_LONGITUDES), jnp.float32, -0.25, 0.25) * level_of(seeds[1], (2, NR, TILE_LONGITUDES), ((1, 2),), -0.4, 0.0), -0.25, 0.25)
    diffusion = jnp.clip(jnp.exp(jax.random.uniform(seeds[2], (LEVEL_VARIABLES,), jnp.float32, math.log(0.04), math.log(0.12))), 0.04, 0.12)
    obs_cell = touch_ends(jax.random.randint(seeds[3], (OBS,), 0, CELLS), jax.random.fold_in(seeds[3], 1), 0, CELLS - 1).astype(jnp.int32)
    obs_order = jax.random.permutation(seeds[4], OBS).astype(jnp.int32)
    obs_value = bell_draw(seeds[5], (OBS,), 1.5, 6.0, (), jnp.float32)
    obs_var = jnp.clip(jnp.exp(jax.random.uniform(seeds[6], (OBS,), jnp.float32, math.log(0.2), math.log(2.0))), 0.2, 2.0)
    field_mask = touch_ends((jax.random.randint(seeds[7], (LEVEL_VARIABLES, LEVEL_VARIABLES), 0, 4) < 3).astype(jnp.int32), jax.random.fold_in(seeds[7], 1), 0, 1)
    return {"realization_stack": realization_stack, "velocity": velocity, "diffusion": diffusion, "obs_cell": obs_cell, "obs_order": obs_order, "obs_value": obs_value, "obs_var": obs_var, "field_mask": field_mask}


precise = lax.Precision.HIGHEST

def advance(padded, velocity, diffusion):
    spec_pad = ((0, 0),) * (padded.ndim - 1) + ((1, 1),)
    col_padded = jnp.pad(padded, spec_pad)
    centre = col_padded[..., 1:-1, 1:-1]
    north_cell = col_padded[..., :-2, 1:-1]
    south_cell = col_padded[..., 2:, 1:-1]
    west_cell = col_padded[..., 1:-1, :-2]
    east_cell = col_padded[..., 1:-1, 2:]
    along_col = velocity[0]
    along_row = velocity[1]
    spread = north_cell + south_cell + west_cell + east_cell - 4.0 * centre
    carried = jnp.maximum(along_col, 0.0) * (centre - west_cell) + jnp.minimum(along_col, 0.0) * (east_cell - centre) + jnp.maximum(along_row, 0.0) * (centre - north_cell) + jnp.minimum(along_row, 0.0) * (south_cell - centre)
    return centre + diffusion[:, None, None] * spread - carried

def gaspari(dist_sq):
    scaled = jnp.sqrt(dist_sq) / LOC_HALF
    clipped = jnp.maximum(scaled, 1.0)
    inner_part = (((-0.25 * scaled + 0.5) * scaled + 0.625) * scaled - 5.0 / 3.0) * scaled * scaled + 1.0
    outer_part = ((((scaled / 12.0 - 0.5) * scaled + 0.625) * scaled + 5.0 / 3.0) * scaled - 5.0) * scaled + 4.0 - 2.0 / (3.0 * clipped)
    return jnp.where(scaled <= 1.0, inner_part, jnp.where(scaled <= 2.0, outer_part, 0.0))

def decode(flat_cells, total_rows, n_cols):
    field_ids = flat_cells // (total_rows * n_cols)
    row_ids = flat_cells // n_cols % total_rows
    col_ids = flat_cells % n_cols
    return (field_ids, row_ids, col_ids)

def innovations(priors, obs_values, obs_noise):
    members = priors.shape[0]
    average = lax.optimization_barrier(jnp.mean(priors, axis=0))
    anomaly = priors - average
    spread = lax.optimization_barrier(jnp.sum(anomaly * anomaly, axis=0)) / (members - 1)
    variance_sum = spread + obs_noise
    root_sum = jnp.sqrt(variance_sum)
    shrink = 1.0 / (root_sum * (jnp.sqrt(obs_noise) + root_sum))
    adjust = (obs_values - average) / variance_sum - shrink * anomaly
    return (anomaly, adjust)

def regress(ensemble_now, base_row, obs_field, obs_row, obs_col, anomaly, adjust, field_mask, n_cols):
    members, n_cells = ensemble_now.shape
    n_fields = field_mask.shape[0]
    per_field = n_cells // n_fields
    local_ids = lax.iota(jnp.int32, per_field)
    cell_row = (base_row + local_ids // n_cols).astype(jnp.float32)
    cell_col = (local_ids % n_cols).astype(jnp.float32)
    centred = ensemble_now - lax.optimization_barrier(jnp.mean(ensemble_now, axis=0))
    mask_float = field_mask.astype(jnp.float32)
    total_obs = obs_field.shape[0]
    obs_block = min(256, total_obs)
    increment = jnp.zeros_like(ensemble_now)
    for offset in range(0, total_obs, obs_block):
        row_gap = cell_row[:, None] - obs_row[None, offset:offset + obs_block].astype(jnp.float32)
        col_gap = cell_col[:, None] - obs_col[None, offset:offset + obs_block].astype(jnp.float32)
        closeness = gaspari(row_gap * row_gap + col_gap * col_gap)
        field_hot = (obs_field[None, offset:offset + obs_block] == lax.iota(jnp.int32, n_fields)[:, None]).astype(jnp.float32)
        allowed = jnp.dot(mask_float, field_hot, precision=precise)
        covariance = lax.dot_general(centred, anomaly[:, offset:offset + obs_block], (((0,), (0,)), ((), ())), precision=precise)
        weights = covariance.reshape(n_fields, per_field, obs_block) * (closeness[None] * allowed[:, None, :]) / (members - 1)
        increment = increment + lax.dot_general(adjust[:, offset:offset + obs_block], weights.reshape(n_cells, obs_block), (((1,), (1,)), ((), ())), precision=precise)
    return ensemble_now + increment

def reference(realization_stack, velocity, diffusion, obs_cell, obs_order, obs_value, obs_var, field_mask):

    def realization_prediction(variables_each_realization):
        current = variables_each_realization
        for substep in range(SUBSTEPS):
            padded = jnp.pad(current, ((0, 0), (1, 1), (0, 0)))
            current = advance(padded, velocity, diffusion)
        return current
    predicted_background = lax.map(realization_prediction, realization_stack)
    tile_piece_total = NR // SHARD_LATITUDES
    tile_piece_arrangement = predicted_background.reshape(REALIZATIONS, LEVEL_VARIABLES, tile_piece_total, SHARD_LATITUDES, TILE_LONGITUDES)
    tile_piece_arrangement = jnp.transpose(tile_piece_arrangement, (2, 0, 1, 3, 4)).reshape(tile_piece_total, REALIZATIONS, LEVEL_VARIABLES * SHARD_LATITUDES * TILE_LONGITUDES)
    bases = jnp.arange(tile_piece_total, dtype=jnp.int32) * SHARD_LATITUDES
    field_all, row_all, col_all = decode(obs_cell, NR, TILE_LONGITUDES)
    for batch_num in range(BATCHES):
        picked = obs_order[batch_num * OBS_BATCH:(batch_num + 1) * OBS_BATCH]
        obs_field = field_all[picked]
        obs_row = row_all[picked]
        obs_col = col_all[picked]
        block_ids = (obs_row // SHARD_LATITUDES).astype(jnp.int32)
        within_ids = (obs_field * SHARD_LATITUDES * TILE_LONGITUDES + obs_row % SHARD_LATITUDES * TILE_LONGITUDES + obs_col).astype(jnp.int32)
        priors = tile_piece_arrangement[block_ids, :, within_ids].T
        anomaly, adjust = innovations(priors, obs_value[picked], obs_var[picked])

        def update_block(operands):
            return regress(operands[0], operands[1], obs_field, obs_row, obs_col, anomaly, adjust, field_mask, TILE_LONGITUDES)
        tile_piece_arrangement = lax.map(update_block, (tile_piece_arrangement, bases))
    result = tile_piece_arrangement.reshape(tile_piece_total, REALIZATIONS, LEVEL_VARIABLES, SHARD_LATITUDES, TILE_LONGITUDES)
    result = jnp.transpose(result, (1, 2, 0, 3, 4))
    return result.reshape(REALIZATIONS, LEVEL_VARIABLES, SLABS, ROWS_DEV, TILE_LONGITUDES)
```

```python
import functools

import jax
import jax.numpy as jnp
from jax import lax
from jax.experimental import pallas as pl
from jax.experimental.pallas import tpu as pltpu
from jax.sharding import PartitionSpec as P

SUBSTEPS = 4
BATCHES = 2
LOC_HALF = 32


precise = lax.Precision.HIGHEST


def extended(shard, sides, width):
    for axis, dim in sides:
        count, length = (lax.axis_size(axis), shard.shape[dim])
        up = [(i, (i + 1) % count) for i in range(count - 1)]
        down = [(j, i) for i, j in up]
        last = lax.slice_in_dim(shard, length - width, length, axis=dim)
        initial = lax.slice_in_dim(shard, 0, width, axis=dim)
        before = lax.ppermute(last, axis, up)
        after = lax.ppermute(initial, axis, down)
        shard = jnp.concatenate([before, shard, after], axis=dim)
    return shard


def advance(padded, velocity, diffusion):
    spec_pad = ((0, 0),) * (padded.ndim - 1) + ((1, 1),)
    col_padded = jnp.pad(padded, spec_pad)
    centre = col_padded[..., 1:-1, 1:-1]
    north_cell = col_padded[..., :-2, 1:-1]
    south_cell = col_padded[..., 2:, 1:-1]
    west_cell = col_padded[..., 1:-1, :-2]
    east_cell = col_padded[..., 1:-1, 2:]
    along_col = velocity[0]
    along_row = velocity[1]
    spread = north_cell + south_cell + west_cell + east_cell - 4.0 * centre
    carried = (
        jnp.maximum(along_col, 0.0) * (centre - west_cell)
        + jnp.minimum(along_col, 0.0) * (east_cell - centre)
        + jnp.maximum(along_row, 0.0) * (centre - north_cell)
        + jnp.minimum(along_row, 0.0) * (south_cell - centre)
    )
    return centre + diffusion[:, None, None] * spread - carried


def gaspari(dist_sq):
    scaled = jnp.sqrt(dist_sq) / LOC_HALF
    clipped = jnp.maximum(scaled, 1.0)
    inner_part = (
        ((-0.25 * scaled + 0.5) * scaled + 0.625) * scaled - 5.0 / 3.0
    ) * scaled * scaled + 1.0
    outer_part = (
        ((((scaled / 12.0 - 0.5) * scaled + 0.625) * scaled + 5.0 / 3.0) * scaled - 5.0) * scaled
        + 4.0
        - 2.0 / (3.0 * clipped)
    )
    return jnp.where(scaled <= 1.0, inner_part, jnp.where(scaled <= 2.0, outer_part, 0.0))


def decode(flat_cells, total_rows, n_cols):
    field_ids = flat_cells // (total_rows * n_cols)
    row_ids = flat_cells // n_cols % total_rows
    col_ids = flat_cells % n_cols
    return (field_ids, row_ids, col_ids)


def innovations(priors, obs_values, obs_noise):
    members = priors.shape[0]
    average = jnp.mean(priors, axis=0)
    anomaly = priors - average
    spread = jnp.sum(anomaly * anomaly, axis=0) / (members - 1)
    variance_sum = spread + obs_noise
    root_sum = jnp.sqrt(variance_sum)
    shrink = 1.0 / (root_sum * (jnp.sqrt(obs_noise) + root_sum))
    adjust = (obs_values - average) / variance_sum - shrink * anomaly
    return (anomaly, adjust)


def regress(
    ensemble_now, base_row, obs_field, obs_row, obs_col, anomaly, adjust, field_mask, n_cols
):
    members, n_cells = ensemble_now.shape
    n_fields = field_mask.shape[0]
    per_field = n_cells // n_fields
    local_ids = lax.iota(jnp.int32, per_field)
    cell_row = (base_row + local_ids // n_cols).astype(jnp.float32)
    cell_col = (local_ids % n_cols).astype(jnp.float32)
    centred = ensemble_now - jnp.mean(ensemble_now, axis=0)
    mask_float = field_mask.astype(jnp.float32)
    total_obs = obs_field.shape[0]
    obs_block = min(256, total_obs)
    increment = jnp.zeros_like(ensemble_now)
    for offset in range(0, total_obs, obs_block):
        row_gap = cell_row[:, None] - obs_row[None, offset : offset + obs_block].astype(jnp.float32)
        col_gap = cell_col[:, None] - obs_col[None, offset : offset + obs_block].astype(jnp.float32)
        closeness = gaspari(row_gap * row_gap + col_gap * col_gap)
        field_hot = (
            obs_field[None, offset : offset + obs_block] == lax.iota(jnp.int32, n_fields)[:, None]
        ).astype(jnp.float32)
        allowed = jnp.dot(mask_float, field_hot, precision=precise)
        covariance = lax.dot_general(
            centred,
            anomaly[:, offset : offset + obs_block],
            (((0,), (0,)), ((), ())),
            precision=precise,
        )
        weights = (
            covariance.reshape(n_fields, per_field, obs_block)
            * (closeness[None] * allowed[:, None, :])
            / (members - 1)
        )
        increment = increment + lax.dot_general(
            adjust[:, offset : offset + obs_block],
            weights.reshape(n_cells, obs_block),
            (((1,), (1,)), ((), ())),
            precision=precise,
        )
    return ensemble_now + increment


LANES = 128
MEGA = 1 << 20


def split_two(x):
    high = x.astype(jnp.bfloat16)
    low = (x - high.astype(jnp.float32)).astype(jnp.bfloat16)
    return high, low


def split_three(x):
    high = x.astype(jnp.bfloat16)
    rest = x - high.astype(jnp.float32)
    mid = rest.astype(jnp.bfloat16)
    low = (rest - mid.astype(jnp.float32)).astype(jnp.bfloat16)
    return high, mid, low


def bdot(a, b):
    return jnp.dot(a, b, preferred_element_type=jnp.float32)


def log2(n):
    return n.bit_length() - 1


def prep_kernel(order_ref, cell_ref, value_ref, var_ref, info_ref, infot_ref, *, total_rows, n_cols):
    table_rows = cell_ref.shape[0]
    order = order_ref[...]
    n_obs = order.shape[1]
    table = jnp.concatenate(
        [cell_ref[...].astype(jnp.float32), value_ref[...], var_ref[...]], axis=0
    )
    parts = jnp.concatenate(split_three(table), axis=0)
    lane_hot = (
        lax.broadcasted_iota(jnp.int32, (LANES, n_obs), 0) == (order & (LANES - 1))
    ).astype(jnp.float32).astype(jnp.bfloat16)
    found = bdot(parts, lane_hot)
    size = 3 * table_rows
    found = (found[:size] + found[size : 2 * size]) + found[2 * size :]
    row_hot = lax.broadcasted_iota(jnp.int32, (table_rows, n_obs), 0) == (order >> log2(LANES))

    def take(i):
        rows = found[i * table_rows : (i + 1) * table_rows]
        return jnp.sum(jnp.where(row_hot, rows, 0.0), axis=0, keepdims=True)

    cell = take(0).astype(jnp.int32)
    strip = cell >> log2(n_cols)
    field = strip >> log2(total_rows)
    row = strip & (total_rows - 1)
    col = cell & (n_cols - 1)
    as_float = lambda x: x.astype(jnp.float32)
    zero = jnp.zeros((1, n_obs), jnp.float32)
    info = jnp.concatenate(
        [as_float(field), as_float(row), as_float(col), take(1), take(2), as_float(strip), zero, zero],
        axis=0,
    )
    info_ref[...] = info
    infot_ref[...] = info.T


def forecast_kernel(
    place_ref, diffusion_ref, own_ref, other_ref, vel_own_ref, vel_other_ref, info_ref,
    send_ref, field_buf, vel_buf, prior_buf,
):
    n_fields, n_rows, n_cols = field_buf.shape
    half = n_rows // 2
    n_dest = half
    chunk = send_ref.shape[0] // n_dest
    mine = pl.multiple_of(place_ref[0] * half, half)
    theirs = pl.multiple_of((1 - place_ref[0]) * half, half)
    vel_buf[:, pl.ds(mine, half), :] = vel_own_ref[...]
    vel_buf[:, pl.ds(theirs, half), :] = vel_other_ref[...]
    field_buf[:, pl.ds(mine, half), :] = own_ref[0]
    field_buf[:, pl.ds(theirs, half), :] = other_ref[0]
    u = vel_buf[0]
    v = vel_buf[1]
    row = lax.broadcasted_iota(jnp.int32, (n_rows, n_cols), 0)
    col = lax.broadcasted_iota(jnp.int32, (n_rows, n_cols), 1)
    u_pos, u_neg = jnp.maximum(u, 0.0), jnp.minimum(u, 0.0)
    v_pos, v_neg = jnp.maximum(v, 0.0), jnp.minimum(v, 0.0)
    outflow = (u_neg - u_pos) + (v_neg - v_pos)
    for f in range(n_fields):
        kappa = diffusion_ref[f]
        k_c = (1.0 - 4.0 * kappa) + outflow
        k_n = jnp.where(row == 0, 0.0, kappa + v_pos)
        k_s = jnp.where(row == n_rows - 1, 0.0, kappa - v_neg)
        k_w = jnp.where(col == 0, 0.0, kappa + u_pos)
        k_e = jnp.where(col == n_cols - 1, 0.0, kappa - u_neg)
        c = field_buf[f]
        for _ in range(SUBSTEPS):
            c = (
                (c * k_c + pltpu.roll(c, 1, 0) * k_n)
                + (pltpu.roll(c, n_rows - 1, 0) * k_s + pltpu.roll(c, 1, 1) * k_w)
                + pltpu.roll(c, n_cols - 1, 1) * k_e
            )
        field_buf[f] = c
    whole = field_buf[...].reshape(n_fields * n_rows, n_cols)
    strips = n_fields * n_rows
    parts = jnp.concatenate(split_three(whole), axis=0)
    n_obs = info_ref.shape[1]
    width = 2 * LANES
    strip_ids = lax.broadcasted_iota(jnp.int32, (strips, width), 0)
    col_ids = lax.broadcasted_iota(jnp.int32, (n_cols, width), 0)
    for q in range(n_obs // width):
        cols = info_ref[2:3, q * width : (q + 1) * width].astype(jnp.int32)
        strip = info_ref[5:6, q * width : (q + 1) * width].astype(jnp.int32)
        hot = (col_ids == cols).astype(jnp.float32).astype(jnp.bfloat16)
        found = bdot(parts, hot)
        found = (found[:strips] + found[strips : 2 * strips]) + found[2 * strips :]
        values = jnp.sum(jnp.where(strip_ids == strip, found, 0.0), axis=0, keepdims=True)
        for h in range(width // LANES):
            at = q * (width // LANES) + h
            prior_buf[at : at + 1, :] = values[:, h * LANES : (h + 1) * LANES]
    priors = prior_buf[...]
    lead = chunk - n_obs // LANES
    for d in range(n_dest):
        send_ref[d * chunk + lead : (d + 1) * chunk, :] = priors
    pieces = n_cols // LANES
    for f in range(n_fields):
        rows = field_buf[f, pl.ds(mine, half), :]
        for h in range(pieces):
            send_ref[pl.ds(f * pieces + h, n_dest, stride=chunk), :] = rows[
                :, h * LANES : (h + 1) * LANES
            ]
    for i in range(n_fields * pieces, lead):
        send_ref[pl.ds(i, n_dest, stride=chunk), :] = jnp.zeros((n_dest, LANES), jnp.float32)


def closeness_of(dist_sq):
    inverse = lax.rsqrt(jnp.maximum(dist_sq, 1e-12))
    z = dist_sq * inverse
    half_sq = 0.5 * dist_sq
    inner = 1.0 + dist_sq * ((half_sq - 5.0 / 3.0) + z * (0.625 - 0.5 * half_sq))
    outer = (
        (4.0 + dist_sq * (5.0 / 3.0 - half_sq))
        + z * (dist_sq * (dist_sq * (1.0 / 12.0) + 0.625) - 5.0)
        - (2.0 / 3.0) * inverse
    )
    return jnp.where(dist_sq <= 1.0, inner, jnp.where(dist_sq <= 4.0, outer, 0.0))


def loc_kernel(
    place_ref, mask_ref, info_ref, infot_ref,
    pair_hi_ref, pair_lo_ref, cell_hi_ref, cell_lo_ref, allow_buf,
):
    n_obs = info_ref.shape[1]
    batch = n_obs // BATCHES
    n_fields = mask_ref.shape[0]
    n_cols = cell_hi_ref.shape[1]
    scale = 1.0 / LOC_HALF
    step = 16
    field_j = info_ref[0:1, batch:].astype(jnp.int32)
    hot_j = (lax.broadcasted_iota(jnp.int32, (8, n_obs - batch), 0) == field_j).astype(jnp.float32)
    field_k = infot_ref[0:batch, 0:1].astype(jnp.int32)
    lane = lax.broadcasted_iota(jnp.int32, (1, 8), 1)
    reach = jnp.zeros((batch, 8), jnp.float32)
    for b in range(n_fields):
        line = jnp.zeros((1, 8), jnp.float32)
        for a in range(n_fields):
            line = jnp.where(lane == a, mask_ref[a, b].astype(jnp.float32), line)
        reach = jnp.where(field_k == b, line, reach)
    allow_buf[...] = bdot(reach.astype(jnp.bfloat16), hot_j.astype(jnp.bfloat16))

    half = 512

    def pair_body(i, carry):
        at = pl.multiple_of(i * step, step)
        row_k = infot_ref[pl.ds(at, step), 1:2] * scale
        col_k = infot_ref[pl.ds(at, step), 2:3] * scale
        for h in range((n_obs - batch) // half):
            here = slice(h * half, (h + 1) * half)
            there = slice(batch + h * half, batch + (h + 1) * half)
            d_row = info_ref[1:2, there] * scale - row_k
            d_col = info_ref[2:3, there] * scale - col_k
            loc = closeness_of(d_row * d_row + d_col * d_col) * allow_buf[pl.ds(at, step), here]
            high, low = split_two(loc)
            pair_hi_ref[pl.ds(at, step), here] = high
            pair_lo_ref[pl.ds(at, step), here] = low
        return carry

    lax.fori_loop(0, batch // step, pair_body, 0)

    own_row = place_ref[1].astype(jnp.float32) * scale
    col_j = lax.broadcasted_iota(jnp.int32, (step, n_cols), 1).astype(jnp.float32) * scale

    def cell_body(i, carry):
        for h in range(2):
            at = pl.multiple_of(i * (2 * step) + h * step, step)
            d_row = infot_ref[pl.ds(at, step), 1:2] * scale - own_row
            d_col = col_j - infot_ref[pl.ds(at, step), 2:3] * scale
            high, low = split_two(closeness_of(d_row * d_row + d_col * d_col))
            cell_hi_ref[pl.ds(at, step), :] = high
            cell_lo_ref[pl.ds(at, step), :] = low
        return carry

    lax.fori_loop(0, n_obs // (2 * step), cell_body, 0)


def member_roll(x, shift):
    shift = shift % x.shape[0]
    return pltpu.roll(x, shift, 0) if shift else x


def factors(priors, value, var):
    members = priors.shape[0]
    average = jnp.sum(priors, axis=0, keepdims=True) * (1.0 / members)
    anomaly = priors - average
    variance = jnp.sum(anomaly * anomaly, axis=0, keepdims=True) * (1.0 / (members - 1)) + var
    root = jnp.sqrt(variance)
    shrunk = anomaly * (1.0 / ((members - 1) * (root * (jnp.sqrt(var) + root))))
    rows = [shrunk * member_roll(anomaly, -d) for d in range(members // 2 + 1)]
    rows.append(anomaly * ((value - average) / ((members - 1) * variance)))
    return rows


def combined(state, sums):
    members = state.shape[0]
    centred = state - jnp.sum(state, axis=0, keepdims=True) * (1.0 / members)
    offsets = members // 2
    block = lambda d: sums[d * members : (d + 1) * members]
    move = centred * block(0) + member_roll(centred, -offsets) * block(offsets)
    for d in range(1, offsets):
        move = move + member_roll(centred, -d) * block(d)
        move = move + member_roll(centred * block(d), d)
    shift = jnp.sum(centred * block(offsets + 1), axis=0, keepdims=True)
    return state + (shift - move)


def update_kernel(
    mask_ref, recv_ref, info_ref, pair_hi_ref, pair_lo_ref, cell_hi_ref, cell_lo_ref,
    out_ref, fac_buf, *, members,
):
    n_obs = info_ref.shape[1]
    batch = n_obs // BATCHES
    n_fields = mask_ref.shape[0]
    chunk = recv_ref.shape[0] // members
    per_chunk = n_obs // LANES
    lead = chunk - per_chunk
    pieces = cell_hi_ref.shape[1] // LANES
    size = fac_buf.shape[0] // 2

    def member_row(i):
        return recv_ref[pl.ds(i, members, stride=chunk), :]

    state = [
        jnp.concatenate([member_row(f * pieces + h) for h in range(pieces)], axis=1)
        for f in range(n_fields)
    ]
    priors = jnp.concatenate([member_row(lead + q) for q in range(per_chunk)], axis=1)
    upcoming = priors[:, batch:]
    current = priors[:, :batch]
    for b in range(BATCHES):
        span = slice(b * batch, (b + 1) * batch)
        rows = factors(current, info_ref[3:4, span], info_ref[4:5, span])
        for i, r in enumerate(rows):
            high, low = split_two(r)
            fac_buf[i * members : (i + 1) * members, :] = high
            fac_buf[size + i * members : size + (i + 1) * members, :] = low
        if b == 0:
            first = bdot(fac_buf[...], pair_hi_ref[...])
            sums = (first[:size] + first[size:]) + bdot(fac_buf[:size, :], pair_lo_ref[...])
            current = combined(upcoming, sums)
        obs_field = info_ref[0:1, span].astype(jnp.int32)
        for f in range(n_fields):
            open_to = jnp.zeros((1, batch), jnp.float32)
            for a in range(n_fields):
                open_to = jnp.where(obs_field == a, mask_ref[f, a].astype(jnp.float32), open_to)
            masked = fac_buf[...] * open_to.astype(jnp.bfloat16)
            first = bdot(masked, cell_hi_ref[span, :])
            sums = (first[:size] + first[size:]) + bdot(masked[:size], cell_lo_ref[span, :])
            state[f] = combined(state[f], sums)
    for f in range(n_fields):
        out_ref[:, f, :] = state[f]


def vmem_spec():
    return pl.BlockSpec(memory_space=pltpu.VMEM)


def smem_spec():
    return pl.BlockSpec(memory_space=pltpu.SMEM)


def quick_device(
    realization_stack, velocity, diffusion, obs_cell, obs_order, obs_value, obs_var, field_mask
):
    _, n_fields, rows_here, n_cols = realization_stack.shape
    n_mem = lax.axis_size("mem")
    total_rows = 2 * rows_here
    n_obs = obs_cell.shape[0]
    batch = n_obs // BATCHES
    slab_index = lax.axis_index("row")
    own_row = slab_index * rows_here + lax.axis_index("mem")
    place = jnp.stack([slab_index, own_row]).astype(jnp.int32)
    params = pltpu.CompilerParams(vmem_limit_bytes=40 * MEGA)
    shape = jax.ShapeDtypeStruct
    swap = [(0, 1), (1, 0)]
    other = lax.ppermute(realization_stack, "row", swap)
    vel_other = lax.ppermute(velocity, "row", swap)
    table = (n_obs // LANES, LANES)
    info, infot = pl.pallas_call(
        functools.partial(prep_kernel, total_rows=total_rows, n_cols=n_cols),
        out_shape=(shape((8, n_obs), jnp.float32), shape((n_obs, 8), jnp.float32)),
        in_specs=[vmem_spec()] * 4,
        out_specs=(vmem_spec(), vmem_spec()),
        compiler_params=params,
        name="prep",
    )(
        obs_order.reshape(1, n_obs),
        obs_cell.reshape(table),
        obs_value.reshape(table),
        obs_var.reshape(table),
    )
    chunk = -(-(n_fields * n_cols + n_obs) // (8 * LANES)) * 8
    send = pl.pallas_call(
        forecast_kernel,
        out_shape=shape((n_mem * chunk, LANES), jnp.float32),
        in_specs=[smem_spec(), smem_spec()] + [vmem_spec()] * 5,
        out_specs=vmem_spec(),
        scratch_shapes=[
            pltpu.VMEM((n_fields, total_rows, n_cols), jnp.float32),
            pltpu.VMEM((2, total_rows, n_cols), jnp.float32),
            pltpu.VMEM((n_obs // LANES, LANES), jnp.float32),
        ],
        compiler_params=params,
        name="forecast",
    )(place, diffusion, realization_stack, other, velocity, vel_other, info)
    recv = lax.all_to_all(send, "mem", split_axis=0, concat_axis=0, tiled=True)
    locs = pl.pallas_call(
        loc_kernel,
        out_shape=(
            shape((batch, n_obs - batch), jnp.bfloat16),
            shape((batch, n_obs - batch), jnp.bfloat16),
            shape((n_obs, n_cols), jnp.bfloat16),
            shape((n_obs, n_cols), jnp.bfloat16),
        ),
        in_specs=[smem_spec(), smem_spec(), vmem_spec(), vmem_spec()],
        out_specs=(vmem_spec(),) * 4,
        scratch_shapes=[pltpu.VMEM((batch, n_obs - batch), jnp.float32)],
        compiler_params=params,
        name="localize",
    )(place, field_mask, info, infot)
    rows = n_mem * (n_mem // 2 + 2)
    out = pl.pallas_call(
        functools.partial(update_kernel, members=n_mem),
        out_shape=shape((n_mem, n_fields, n_cols), jnp.float32),
        in_specs=[smem_spec()] + [vmem_spec()] * 6,
        out_specs=vmem_spec(),
        scratch_shapes=[pltpu.VMEM((2 * rows, batch), jnp.bfloat16)],
        compiler_params=params,
        name="update",
    )(field_mask, recv, info, *locs)
    return out.reshape(n_mem, n_fields, 1, 1, n_cols)


def is_quick(realization_stack, obs_cell, n_mem, n_slab):
    local_members, n_fields, rows_here, n_cols = realization_stack.shape
    powers = all(n & (n - 1) == 0 for n in (rows_here, n_cols))
    return (
        n_slab == 2
        and local_members == 1
        and n_mem == rows_here == 16
        and n_fields <= 8
        and powers
        and n_cols % LANES == 0
        and obs_cell.shape[0] == 8 * n_cols
        and BATCHES == 2
    )


def per_device(
    realization_stack, velocity, diffusion, obs_cell, obs_order, obs_value, obs_var, field_mask
):
    local_members = realization_stack.shape[0]
    n_fields = realization_stack.shape[1]
    rows_here = realization_stack.shape[2]
    n_cols = realization_stack.shape[3]
    n_mem = lax.axis_size("mem")
    n_slab = lax.axis_size("row")
    total_members = local_members * n_mem
    total_rows = rows_here * n_slab
    if is_quick(realization_stack, obs_cell, n_mem, n_slab):
        return quick_device(
            realization_stack, velocity, diffusion, obs_cell, obs_order, obs_value, obs_var, field_mask
        )
    slab_index = lax.axis_index("row")
    member_index = lax.axis_index("mem")
    row_sub = rows_here // n_mem
    current = realization_stack
    for substep in range(SUBSTEPS):
        padded = extended(current, (("row", 2),), 1)
        current = advance(padded, velocity, diffusion)
    field_all, row_all, col_all = decode(obs_cell, total_rows, n_cols)
    batch_size = obs_cell.shape[0] // BATCHES
    layout = lax.all_to_all(current, "mem", split_axis=2, concat_axis=0, tiled=True)
    ensemble_now = layout.reshape(total_members, -1)
    base_row = slab_index * rows_here + member_index * row_sub
    for batch_num in range(BATCHES):
        picked = obs_order[batch_num * batch_size : (batch_num + 1) * batch_size]
        obs_field = field_all[picked]
        obs_row = row_all[picked]
        obs_col = col_all[picked]
        owned = ((obs_row >= base_row) & (obs_row < base_row + row_sub)).astype(jnp.float32)
        local_ids = (
            obs_field * row_sub * n_cols
            + jnp.clip(obs_row - base_row, 0, row_sub - 1) * n_cols
            + obs_col
        )
        partial_priors = jnp.take(ensemble_now, local_ids, axis=1) * owned[None, :]
        priors = lax.psum(partial_priors, ("mem", "row"))
        anomaly, adjust = innovations(priors, obs_value[picked], obs_var[picked])
        ensemble_now = regress(
            ensemble_now, base_row, obs_field, obs_row, obs_col, anomaly, adjust, field_mask, n_cols
        )
    return ensemble_now.reshape(total_members, n_fields, 1, row_sub, n_cols)


def solution(mesh):
    in_specs = (P("mem", None, "row", None), P(None, "row", None), P(), P(), P(), P(), P(), P())
    out_specs = P(None, None, "row", "mem", None)
    return jax.shard_map(
        per_device, mesh=mesh, in_specs=in_specs, out_specs=out_specs, check_vma=False
    )
```

```python
import functools

import jax
import jax.numpy as jnp
from jax import lax
from jax.experimental import pallas as pl
from jax.experimental.pallas import tpu as pltpu
from jax.sharding import PartitionSpec as P

SUBSTEPS = 4
BATCHES = 2
LOC_HALF = 32


precise = lax.Precision.HIGHEST


def extended(shard, sides, width):
    for axis, dim in sides:
        count, length = (lax.axis_size(axis), shard.shape[dim])
        up = [(i, (i + 1) % count) for i in range(count - 1)]
        down = [(j, i) for i, j in up]
        last = lax.slice_in_dim(shard, length - width, length, axis=dim)
        initial = lax.slice_in_dim(shard, 0, width, axis=dim)
        before = lax.ppermute(last, axis, up)
        after = lax.ppermute(initial, axis, down)
        shard = jnp.concatenate([before, shard, after], axis=dim)
    return shard


def advance(padded, velocity, diffusion):
    spec_pad = ((0, 0),) * (padded.ndim - 1) + ((1, 1),)
    col_padded = jnp.pad(padded, spec_pad)
    centre = col_padded[..., 1:-1, 1:-1]
    north_cell = col_padded[..., :-2, 1:-1]
    south_cell = col_padded[..., 2:, 1:-1]
    west_cell = col_padded[..., 1:-1, :-2]
    east_cell = col_padded[..., 1:-1, 2:]
    along_col = velocity[0]
    along_row = velocity[1]
    spread = north_cell + south_cell + west_cell + east_cell - 4.0 * centre
    carried = (
        jnp.maximum(along_col, 0.0) * (centre - west_cell)
        + jnp.minimum(along_col, 0.0) * (east_cell - centre)
        + jnp.maximum(along_row, 0.0) * (centre - north_cell)
        + jnp.minimum(along_row, 0.0) * (south_cell - centre)
    )
    return centre + diffusion[:, None, None] * spread - carried


def gaspari(dist_sq):
    scaled = jnp.sqrt(dist_sq) / LOC_HALF
    clipped = jnp.maximum(scaled, 1.0)
    inner_part = (
        ((-0.25 * scaled + 0.5) * scaled + 0.625) * scaled - 5.0 / 3.0
    ) * scaled * scaled + 1.0
    outer_part = (
        ((((scaled / 12.0 - 0.5) * scaled + 0.625) * scaled + 5.0 / 3.0) * scaled - 5.0) * scaled
        + 4.0
        - 2.0 / (3.0 * clipped)
    )
    return jnp.where(scaled <= 1.0, inner_part, jnp.where(scaled <= 2.0, outer_part, 0.0))


def decode(flat_cells, total_rows, n_cols):
    field_ids = flat_cells // (total_rows * n_cols)
    row_ids = flat_cells // n_cols % total_rows
    col_ids = flat_cells % n_cols
    return (field_ids, row_ids, col_ids)


def innovations(priors, obs_values, obs_noise):
    members = priors.shape[0]
    average = jnp.mean(priors, axis=0)
    anomaly = priors - average
    spread = jnp.sum(anomaly * anomaly, axis=0) / (members - 1)
    variance_sum = spread + obs_noise
    root_sum = jnp.sqrt(variance_sum)
    shrink = 1.0 / (root_sum * (jnp.sqrt(obs_noise) + root_sum))
    adjust = (obs_values - average) / variance_sum - shrink * anomaly
    return (anomaly, adjust)


def regress(
    ensemble_now, base_row, obs_field, obs_row, obs_col, anomaly, adjust, field_mask, n_cols
):
    members, n_cells = ensemble_now.shape
    n_fields = field_mask.shape[0]
    per_field = n_cells // n_fields
    local_ids = lax.iota(jnp.int32, per_field)
    cell_row = (base_row + local_ids // n_cols).astype(jnp.float32)
    cell_col = (local_ids % n_cols).astype(jnp.float32)
    centred = ensemble_now - jnp.mean(ensemble_now, axis=0)
    mask_float = field_mask.astype(jnp.float32)
    total_obs = obs_field.shape[0]
    obs_block = min(256, total_obs)
    increment = jnp.zeros_like(ensemble_now)
    for offset in range(0, total_obs, obs_block):
        row_gap = cell_row[:, None] - obs_row[None, offset : offset + obs_block].astype(jnp.float32)
        col_gap = cell_col[:, None] - obs_col[None, offset : offset + obs_block].astype(jnp.float32)
        closeness = gaspari(row_gap * row_gap + col_gap * col_gap)
        field_hot = (
            obs_field[None, offset : offset + obs_block] == lax.iota(jnp.int32, n_fields)[:, None]
        ).astype(jnp.float32)
        allowed = jnp.dot(mask_float, field_hot, precision=precise)
        covariance = lax.dot_general(
            centred,
            anomaly[:, offset : offset + obs_block],
            (((0,), (0,)), ((), ())),
            precision=precise,
        )
        weights = (
            covariance.reshape(n_fields, per_field, obs_block)
            * (closeness[None] * allowed[:, None, :])
            / (members - 1)
        )
        increment = increment + lax.dot_general(
            adjust[:, offset : offset + obs_block],
            weights.reshape(n_cells, obs_block),
            (((1,), (1,)), ((), ())),
            precision=precise,
        )
    return ensemble_now + increment


LANES = 128
MEGA = 1 << 20


def split_two(x):
    high = x.astype(jnp.bfloat16)
    low = (x - high.astype(jnp.float32)).astype(jnp.bfloat16)
    return high, low


def split_three(x):
    high = x.astype(jnp.bfloat16)
    rest = x - high.astype(jnp.float32)
    mid = rest.astype(jnp.bfloat16)
    low = (rest - mid.astype(jnp.float32)).astype(jnp.bfloat16)
    return high, mid, low


def bdot(a, b):
    return jnp.dot(a, b, preferred_element_type=jnp.float32)


def log2(n):
    return n.bit_length() - 1


def fetch(pairs, sems):
    copies = [pltpu.make_async_copy(src, dst, sems.at[i]) for i, (src, dst) in enumerate(pairs)]
    for copy in copies:
        copy.start()
    for copy in copies:
        copy.wait()


def prep_kernel(
    order_hbm, cell_hbm, value_hbm, var_hbm, mask_hbm, diffusion_hbm, stack_hbm, velocity_hbm,
    info_ref, own_ref, vel_ref, kappa_ref,
    order_buf, cell_buf, value_buf, var_buf, mask_buf, diffusion_buf, sems,
    *, total_rows, n_cols,
):
    fetch(
        [
            (order_hbm, order_buf), (cell_hbm, cell_buf), (value_hbm, value_buf),
            (var_hbm, var_buf), (mask_hbm, mask_buf), (diffusion_hbm, diffusion_buf),
            (stack_hbm, own_ref), (velocity_hbm, vel_ref),
        ],
        sems,
    )
    table_rows = cell_buf.shape[0]
    n_fields = mask_buf.shape[0]
    for f in range(n_fields):
        kappa_ref[f : f + 1, :] = jnp.full((1, LANES), diffusion_buf[0, f], jnp.float32)
    order = order_buf[...]
    n_obs = order.shape[1]
    table = jnp.concatenate(
        [cell_buf[...].astype(jnp.float32), value_buf[...], var_buf[...]], axis=0
    )
    parts = jnp.concatenate(split_three(table), axis=0)
    lane_hot = (
        lax.broadcasted_iota(jnp.int32, (LANES, n_obs), 0) == (order & (LANES - 1))
    ).astype(jnp.float32).astype(jnp.bfloat16)
    found = bdot(parts, lane_hot)
    size = 3 * table_rows
    found = (found[:size] + found[size : 2 * size]) + found[2 * size :]
    row_hot = lax.broadcasted_iota(jnp.int32, (table_rows, n_obs), 0) == (order >> log2(LANES))

    def take(i):
        rows = found[i * table_rows : (i + 1) * table_rows]
        return jnp.sum(jnp.where(row_hot, rows, 0.0), axis=0, keepdims=True)

    cell = take(0).astype(jnp.int32)
    strip = cell >> log2(n_cols)
    field = strip >> log2(total_rows)
    row = strip & (total_rows - 1)
    col = cell & (n_cols - 1)
    as_float = lambda x: x.astype(jnp.float32)
    zero = jnp.zeros((1, n_obs), jnp.float32)
    up = lax.broadcasted_iota(jnp.int32, (8, 8), 0)
    along = lax.broadcasted_iota(jnp.int32, (8, 8), 1)
    mask = jnp.zeros((8, 8), jnp.float32)
    for f in range(n_fields):
        for b in range(n_fields):
            mask = jnp.where((up == f) & (along == b), as_float(mask_buf[f, b]), mask)
    field_hot = as_float(lax.broadcasted_iota(jnp.int32, (8, n_obs), 0) == field)
    info = jnp.concatenate(
        [
            as_float(field), as_float(row), as_float(col), take(1), take(2), as_float(strip), zero, zero,
            bdot(mask.astype(jnp.bfloat16), field_hot.astype(jnp.bfloat16)),
        ],
        axis=0,
    )
    info_ref[...] = info


def forecast_kernel(
    place_ref, kappa_ref, own_ref, other_ref, vel_own_ref, vel_other_ref, info_ref,
    send_ref, field_buf, vel_buf, prior_buf,
):
    n_fields, n_rows, n_cols = field_buf.shape
    half = n_rows // 2
    n_dest = half
    chunk = send_ref.shape[0] // n_dest
    mine = pl.multiple_of(place_ref[0] * half, half)
    theirs = pl.multiple_of((1 - place_ref[0]) * half, half)
    vel_buf[:, pl.ds(mine, half), :] = vel_own_ref[...]
    vel_buf[:, pl.ds(theirs, half), :] = vel_other_ref[...]
    field_buf[:, pl.ds(mine, half), :] = own_ref[0]
    field_buf[:, pl.ds(theirs, half), :] = other_ref[0]
    u = vel_buf[0]
    v = vel_buf[1]
    row = lax.broadcasted_iota(jnp.int32, (n_rows, n_cols), 0)
    col = lax.broadcasted_iota(jnp.int32, (n_rows, n_cols), 1)
    u_pos, u_neg = jnp.maximum(u, 0.0), jnp.minimum(u, 0.0)
    v_pos, v_neg = jnp.maximum(v, 0.0), jnp.minimum(v, 0.0)
    outflow = (u_neg - u_pos) + (v_neg - v_pos)
    for f in range(n_fields):
        kappa = kappa_ref[f : f + 1, 0:1]
        k_c = (1.0 - 4.0 * kappa) + outflow
        k_n = jnp.where(row == 0, 0.0, kappa + v_pos)
        k_s = jnp.where(row == n_rows - 1, 0.0, kappa - v_neg)
        k_w = jnp.where(col == 0, 0.0, kappa + u_pos)
        k_e = jnp.where(col == n_cols - 1, 0.0, kappa - u_neg)
        c = field_buf[f]
        for _ in range(SUBSTEPS):
            c = (
                (c * k_c + pltpu.roll(c, 1, 0) * k_n)
                + (pltpu.roll(c, n_rows - 1, 0) * k_s + pltpu.roll(c, 1, 1) * k_w)
                + pltpu.roll(c, n_cols - 1, 1) * k_e
            )
        field_buf[f] = c
    whole = field_buf[...].reshape(n_fields * n_rows, n_cols)
    strips = n_fields * n_rows
    parts = jnp.concatenate(split_three(whole), axis=0)
    n_obs = info_ref.shape[1]
    width = 2 * LANES
    strip_ids = lax.broadcasted_iota(jnp.int32, (strips, width), 0)
    col_ids = lax.broadcasted_iota(jnp.int32, (n_cols, width), 0)
    for q in range(n_obs // width):
        cols = info_ref[2:3, q * width : (q + 1) * width].astype(jnp.int32)
        strip = info_ref[5:6, q * width : (q + 1) * width].astype(jnp.int32)
        hot = (col_ids == cols).astype(jnp.float32).astype(jnp.bfloat16)
        found = bdot(parts, hot)
        found = (found[:strips] + found[strips : 2 * strips]) + found[2 * strips :]
        values = jnp.sum(jnp.where(strip_ids == strip, found, 0.0), axis=0, keepdims=True)
        for h in range(width // LANES):
            at = q * (width // LANES) + h
            prior_buf[at : at + 1, :] = values[:, h * LANES : (h + 1) * LANES]
    priors = prior_buf[...]
    lead = chunk - n_obs // LANES
    for d in range(n_dest):
        send_ref[d * chunk + lead : (d + 1) * chunk, :] = priors
    pieces = n_cols // LANES
    for f in range(n_fields):
        rows = field_buf[f, pl.ds(mine, half), :]
        for h in range(pieces):
            send_ref[pl.ds(f * pieces + h, n_dest, stride=chunk), :] = rows[
                :, h * LANES : (h + 1) * LANES
            ]
    for i in range(n_fields * pieces, lead):
        send_ref[pl.ds(i, n_dest, stride=chunk), :] = jnp.zeros((n_dest, LANES), jnp.float32)


def closeness_of(dist_sq):
    inverse = lax.rsqrt(jnp.maximum(dist_sq, 1e-6))
    z = dist_sq * inverse
    half_sq = 0.5 * dist_sq
    inner = 1.0 + dist_sq * ((half_sq - 5.0 / 3.0) + z * (0.625 - 0.5 * half_sq))
    left = jnp.maximum(2.0 - z, 0.0)
    left = left * left
    left = left * left
    outer = left * ((dist_sq + (z + z)) - 0.5) * (inverse * (1.0 / 12.0))
    return jnp.where(dist_sq <= 1.0, inner, outer)


def loc_kernel(
    place_ref, info_ref, pair_hi_hbm, pair_lo_hbm, cell_hi_ref, cell_lo_ref,
    infot_ref, pair_hi_ref, pair_lo_ref, allow_buf, row_k_buf, col_k_buf, row_j_buf, col_j_buf, sems,
):
    n_obs = info_ref.shape[1]
    batch, n_pair = pair_hi_ref.shape
    n_cols = cell_hi_ref.shape[1]
    scale = 1.0 / LOC_HALF
    infot_ref[...] = info_ref[...].T
    hot_j = (
        lax.broadcasted_iota(jnp.int32, (8, n_pair), 0) == info_ref[0:1, batch:].astype(jnp.int32)
    ).astype(jnp.float32)
    allow_buf[...] = bdot(infot_ref[0:batch, 8:16].astype(jnp.bfloat16), hot_j.astype(jnp.bfloat16))
    row_k_buf[...] = jnp.broadcast_to(infot_ref[0:batch, 1:2] * scale, (batch, LANES))
    col_k_buf[...] = jnp.broadcast_to(infot_ref[0:batch, 2:3] * scale, (batch, LANES))
    row_j_buf[...] = jnp.broadcast_to(info_ref[1:2, batch:] * scale, (8, n_pair))
    col_j_buf[...] = jnp.broadcast_to(info_ref[2:3, batch:] * scale, (8, n_pair))
    step = 128
    tiles = (step // 8, 8, LANES)

    def copies_out(i):
        rows = pl.ds(pl.multiple_of(i * step, step), step)
        return [
            pltpu.make_async_copy(ref.at[rows, :], hbm.at[rows, :], sems.at[i, side])
            for side, (ref, hbm) in enumerate([(pair_hi_ref, pair_hi_hbm), (pair_lo_ref, pair_lo_hbm)])
        ]

    def pair_body(i, carry):
        at = pl.multiple_of(i * step, step)
        row_k = row_k_buf[pl.ds(at, step), :].reshape(tiles)
        col_k = col_k_buf[pl.ds(at, step), :].reshape(tiles)
        for h in range(n_pair // LANES):
            here = slice(h * LANES, (h + 1) * LANES)
            d_row = row_j_buf[:, here][None] - row_k
            d_col = col_j_buf[:, here][None] - col_k
            loc = closeness_of(d_row * d_row + d_col * d_col).reshape(step, LANES)
            high, low = split_two(loc * allow_buf[pl.ds(at, step), here])
            pair_hi_ref[pl.ds(at, step), here] = high
            pair_lo_ref[pl.ds(at, step), here] = low
        for copy in copies_out(i):
            copy.start()
        return carry

    lax.fori_loop(0, batch // step, pair_body, 0)

    table_rows = 32
    own_row = place_ref[1].astype(jnp.float32)
    gap_row = (lax.broadcasted_iota(jnp.int32, (table_rows, LANES), 0).astype(jnp.float32) - own_row) * scale
    gap_col = lax.broadcasted_iota(jnp.int32, (table_rows, LANES), 1).astype(jnp.float32) * scale
    high, mid, low = split_three(closeness_of(gap_row * gap_row + gap_col * gap_col))
    row_ids = lax.broadcasted_iota(jnp.int32, (1, table_rows), 1)
    for b in range(BATCHES):
        span = slice(b * batch, (b + 1) * batch)
        hot = (row_ids == infot_ref[span, 1:2].astype(jnp.int32)).astype(jnp.float32).astype(jnp.bfloat16)
        table = (bdot(hot, high) + bdot(hot, mid)) + bdot(hot, low)
        col_k = jnp.broadcast_to(infot_ref[span, 2:3], (batch, LANES)).astype(jnp.int32)
        for h in range(n_cols // LANES):
            here = slice(h * LANES, (h + 1) * LANES)
            col = lax.broadcasted_iota(jnp.int32, (batch, LANES), 1) + h * LANES
            gap = jnp.minimum(jnp.abs(col - col_k), LANES - 1)
            at_hi, at_lo = split_two(jnp.take_along_axis(table, gap, axis=1))
            cell_hi_ref[span, here] = at_hi
            cell_lo_ref[span, here] = at_lo
    for i in range(batch // step):
        for copy in copies_out(i):
            copy.wait()


def member_roll(x, shift):
    shift = shift % x.shape[0]
    return pltpu.roll(x, shift, 0) if shift else x


def factors(priors, value, var):
    members = priors.shape[0]
    average = jnp.sum(priors, axis=0, keepdims=True) * (1.0 / members)
    anomaly = priors - average
    variance = jnp.sum(anomaly * anomaly, axis=0, keepdims=True) * (1.0 / (members - 1)) + var
    root = jnp.sqrt(variance)
    shrunk = anomaly * (1.0 / ((members - 1) * (root * (jnp.sqrt(var) + root))))
    rows = [shrunk * member_roll(anomaly, -d) for d in range(members // 2 + 1)]
    rows.append(anomaly * ((value - average) / ((members - 1) * variance)))
    return rows


def combined(state, sums):
    members = state.shape[0]
    centred = state - jnp.sum(state, axis=0, keepdims=True) * (1.0 / members)
    offsets = members // 2
    block = lambda d: sums[d * members : (d + 1) * members]
    move = centred * block(0) + member_roll(centred, -offsets) * block(offsets)
    for d in range(1, offsets):
        move = move + member_roll(centred, -d) * block(d)
        move = move + member_roll(centred * block(d), d)
    shift = jnp.sum(centred * block(offsets + 1), axis=0, keepdims=True)
    return state + (shift - move)


def update_kernel(
    recv_ref, info_ref, pair_hi_hbm, pair_lo_hbm, cell_hi_ref, cell_lo_ref,
    out_ref, fac_buf, pair_hi_ref, pair_lo_ref, sems, *, members, n_fields,
):
    copies = [
        pltpu.make_async_copy(pair_hi_hbm, pair_hi_ref, sems.at[0]),
        pltpu.make_async_copy(pair_lo_hbm, pair_lo_ref, sems.at[1]),
    ]
    for copy in copies:
        copy.start()
    n_obs = info_ref.shape[1]
    batch = n_obs // BATCHES
    chunk = recv_ref.shape[0] // members
    per_chunk = n_obs // LANES
    lead = chunk - per_chunk
    pieces = cell_hi_ref.shape[1] // LANES
    size = fac_buf.shape[0] // 2

    def member_row(i):
        return recv_ref[pl.ds(i, members, stride=chunk), :]

    state = [
        jnp.concatenate([member_row(f * pieces + h) for h in range(pieces)], axis=1)
        for f in range(n_fields)
    ]
    priors = jnp.concatenate([member_row(lead + q) for q in range(per_chunk)], axis=1)
    upcoming = priors[:, batch:]
    current = priors[:, :batch]
    for b in range(BATCHES):
        span = slice(b * batch, (b + 1) * batch)
        rows = factors(current, info_ref[3:4, span], info_ref[4:5, span])
        for i, r in enumerate(rows):
            high, low = split_two(r)
            fac_buf[i * members : (i + 1) * members, :] = high
            fac_buf[size + i * members : size + (i + 1) * members, :] = low
        for f in range(n_fields):
            masked = fac_buf[...] * info_ref[8 + f : 9 + f, span].astype(jnp.bfloat16)
            first = bdot(masked, cell_hi_ref[span, :])
            sums = (first[:size] + first[size:]) + bdot(masked[:size], cell_lo_ref[span, :])
            state[f] = combined(state[f], sums)
        if b == 0:
            for copy in copies:
                copy.wait()
            first = bdot(fac_buf[...], pair_hi_ref[...])
            sums = (first[:size] + first[size:]) + bdot(fac_buf[:size, :], pair_lo_ref[...])
            current = combined(upcoming, sums)
    for f in range(n_fields):
        out_ref[:, f, 0, 0, :] = state[f]


def vmem_spec():
    return pl.BlockSpec(memory_space=pltpu.VMEM)


def smem_spec():
    return pl.BlockSpec(memory_space=pltpu.SMEM)


def hbm_spec():
    return pl.BlockSpec(memory_space=pltpu.HBM)


def in_hbm(x):
    return pltpu.with_memory_space_constraint(x, pltpu.HBM)


def quick_device(
    realization_stack, velocity, diffusion, obs_cell, obs_order, obs_value, obs_var, field_mask
):
    _, n_fields, rows_here, n_cols = realization_stack.shape
    n_mem = lax.axis_size("mem")
    total_rows = 2 * rows_here
    n_obs = obs_cell.shape[0]
    batch = n_obs // BATCHES
    slab_index = lax.axis_index("row")
    own_row = slab_index * rows_here + lax.axis_index("mem")
    place = jnp.stack([slab_index, own_row]).astype(jnp.int32)
    params = pltpu.CompilerParams(vmem_limit_bytes=16 * MEGA)
    shape = jax.ShapeDtypeStruct
    f32, i32 = jnp.float32, jnp.int32
    swap = [(0, 1), (1, 0)]
    other = lax.ppermute(realization_stack, "row", swap)
    vel_other = lax.ppermute(velocity, "row", swap)
    table = (n_obs // LANES, LANES)
    info, own, vel_own, kappa = pl.pallas_call(
        functools.partial(prep_kernel, total_rows=total_rows, n_cols=n_cols),
        out_shape=(
            shape((16, n_obs), f32),
            shape(realization_stack.shape, f32),
            shape(velocity.shape, f32),
            shape((8, LANES), f32),
        ),
        in_specs=[hbm_spec()] * 8,
        out_specs=(vmem_spec(),) * 4,
        scratch_shapes=[
            pltpu.VMEM((1, n_obs), i32),
            pltpu.VMEM(table, i32),
            pltpu.VMEM(table, f32),
            pltpu.VMEM(table, f32),
            pltpu.SMEM(field_mask.shape, i32),
            pltpu.SMEM((1, n_fields), f32),
            pltpu.SemaphoreType.DMA((8,)),
        ],
        compiler_params=params,
        name="prep",
    )(
        in_hbm(obs_order.reshape(1, n_obs)),
        in_hbm(obs_cell.reshape(table)),
        in_hbm(obs_value.reshape(table)),
        in_hbm(obs_var.reshape(table)),
        in_hbm(field_mask),
        in_hbm(diffusion.reshape(1, n_fields)),
        in_hbm(realization_stack),
        in_hbm(velocity),
    )
    chunk = -(-(n_fields * n_cols + n_obs) // (8 * LANES)) * 8
    send = pl.pallas_call(
        forecast_kernel,
        out_shape=shape((n_mem * chunk, LANES), f32),
        in_specs=[smem_spec()] + [vmem_spec()] * 6,
        out_specs=vmem_spec(),
        scratch_shapes=[
            pltpu.VMEM((n_fields, total_rows, n_cols), f32),
            pltpu.VMEM((2, total_rows, n_cols), f32),
            pltpu.VMEM((n_obs // LANES, LANES), f32),
        ],
        compiler_params=params,
        name="forecast",
    )(place, kappa, own, other, vel_own, vel_other, info)
    recv = lax.all_to_all(send, "mem", split_axis=0, concat_axis=0, tiled=True)
    n_pair = n_obs - batch
    pair = pltpu.HBM((batch, n_pair), jnp.bfloat16)
    near = shape((n_obs, n_cols), jnp.bfloat16)
    pair_hi, pair_lo, cell_hi, cell_lo = pl.pallas_call(
        loc_kernel,
        out_shape=(pair, pair, near, near),
        in_specs=[smem_spec(), vmem_spec()],
        out_specs=(hbm_spec(), hbm_spec(), vmem_spec(), vmem_spec()),
        scratch_shapes=[
            pltpu.VMEM((n_obs, 16), f32),
            pltpu.VMEM((batch, n_pair), jnp.bfloat16),
            pltpu.VMEM((batch, n_pair), jnp.bfloat16),
            pltpu.VMEM((batch, n_pair), f32),
            pltpu.VMEM((batch, LANES), f32),
            pltpu.VMEM((batch, LANES), f32),
            pltpu.VMEM((8, n_pair), f32),
            pltpu.VMEM((8, n_pair), f32),
            pltpu.SemaphoreType.DMA((batch // LANES, 2)),
        ],
        compiler_params=params,
        name="localize",
    )(place, info)
    rows = n_mem * (n_mem // 2 + 2)
    return pl.pallas_call(
        functools.partial(update_kernel, members=n_mem, n_fields=n_fields),
        out_shape=shape((n_mem, n_fields, 1, 1, n_cols), f32),
        in_specs=[vmem_spec(), vmem_spec(), hbm_spec(), hbm_spec(), vmem_spec(), vmem_spec()],
        out_specs=vmem_spec(),
        scratch_shapes=[
            pltpu.VMEM((2 * rows, batch), jnp.bfloat16),
            pltpu.VMEM((batch, n_pair), jnp.bfloat16),
            pltpu.VMEM((batch, n_pair), jnp.bfloat16),
            pltpu.SemaphoreType.DMA((2,)),
        ],
        compiler_params=params,
        name="update",
    )(recv, info, in_hbm(pair_hi), in_hbm(pair_lo), cell_hi, cell_lo)


def is_quick(realization_stack, obs_cell, n_mem, n_slab):
    local_members, n_fields, rows_here, n_cols = realization_stack.shape
    powers = all(n & (n - 1) == 0 for n in (rows_here, n_cols))
    return (
        n_slab == 2
        and local_members == 1
        and n_mem == rows_here == 16
        and n_fields <= 8
        and LOC_HALF * 2 <= LANES - 1
        and powers
        and n_cols % LANES == 0
        and obs_cell.shape[0] == 8 * n_cols
        and BATCHES == 2
    )


def per_device(
    realization_stack, velocity, diffusion, obs_cell, obs_order, obs_value, obs_var, field_mask
):
    local_members = realization_stack.shape[0]
    n_fields = realization_stack.shape[1]
    rows_here = realization_stack.shape[2]
    n_cols = realization_stack.shape[3]
    n_mem = lax.axis_size("mem")
    n_slab = lax.axis_size("row")
    total_members = local_members * n_mem
    total_rows = rows_here * n_slab
    if is_quick(realization_stack, obs_cell, n_mem, n_slab):
        return quick_device(
            realization_stack, velocity, diffusion, obs_cell, obs_order, obs_value, obs_var, field_mask
        )
    slab_index = lax.axis_index("row")
    member_index = lax.axis_index("mem")
    row_sub = rows_here // n_mem
    current = realization_stack
    for substep in range(SUBSTEPS):
        padded = extended(current, (("row", 2),), 1)
        current = advance(padded, velocity, diffusion)
    field_all, row_all, col_all = decode(obs_cell, total_rows, n_cols)
    batch_size = obs_cell.shape[0] // BATCHES
    layout = lax.all_to_all(current, "mem", split_axis=2, concat_axis=0, tiled=True)
    ensemble_now = layout.reshape(total_members, -1)
    base_row = slab_index * rows_here + member_index * row_sub
    for batch_num in range(BATCHES):
        picked = obs_order[batch_num * batch_size : (batch_num + 1) * batch_size]
        obs_field = field_all[picked]
        obs_row = row_all[picked]
        obs_col = col_all[picked]
        owned = ((obs_row >= base_row) & (obs_row < base_row + row_sub)).astype(jnp.float32)
        local_ids = (
            obs_field * row_sub * n_cols
            + jnp.clip(obs_row - base_row, 0, row_sub - 1) * n_cols
            + obs_col
        )
        partial_priors = jnp.take(ensemble_now, local_ids, axis=1) * owned[None, :]
        priors = lax.psum(partial_priors, ("mem", "row"))
        anomaly, adjust = innovations(priors, obs_value[picked], obs_var[picked])
        ensemble_now = regress(
            ensemble_now, base_row, obs_field, obs_row, obs_col, anomaly, adjust, field_mask, n_cols
        )
    return ensemble_now.reshape(total_members, n_fields, 1, row_sub, n_cols)


def solution(mesh):
    in_specs = (P("mem", None, "row", None), P(None, "row", None), P(), P(), P(), P(), P(), P())
    out_specs = P(None, None, "row", "mem", None)
    return jax.shard_map(
        per_device, mesh=mesh, in_specs=in_specs, out_specs=out_specs, check_vma=False
    )
```

```python
import functools

import jax
import jax.numpy as jnp
from jax import lax
from jax.experimental import pallas as pl
from jax.experimental.pallas import tpu as pltpu
from jax.sharding import PartitionSpec as P

SUBSTEPS = 4
BATCHES = 2
LOC_HALF = 32


precise = lax.Precision.HIGHEST


def extended(shard, sides, width):
    for axis, dim in sides:
        count, length = (lax.axis_size(axis), shard.shape[dim])
        up = [(i, (i + 1) % count) for i in range(count - 1)]
        down = [(j, i) for i, j in up]
        last = lax.slice_in_dim(shard, length - width, length, axis=dim)
        initial = lax.slice_in_dim(shard, 0, width, axis=dim)
        before = lax.ppermute(last, axis, up)
        after = lax.ppermute(initial, axis, down)
        shard = jnp.concatenate([before, shard, after], axis=dim)
    return shard


def advance(padded, velocity, diffusion):
    spec_pad = ((0, 0),) * (padded.ndim - 1) + ((1, 1),)
    col_padded = jnp.pad(padded, spec_pad)
    centre = col_padded[..., 1:-1, 1:-1]
    north_cell = col_padded[..., :-2, 1:-1]
    south_cell = col_padded[..., 2:, 1:-1]
    west_cell = col_padded[..., 1:-1, :-2]
    east_cell = col_padded[..., 1:-1, 2:]
    along_col = velocity[0]
    along_row = velocity[1]
    spread = north_cell + south_cell + west_cell + east_cell - 4.0 * centre
    carried = (
        jnp.maximum(along_col, 0.0) * (centre - west_cell)
        + jnp.minimum(along_col, 0.0) * (east_cell - centre)
        + jnp.maximum(along_row, 0.0) * (centre - north_cell)
        + jnp.minimum(along_row, 0.0) * (south_cell - centre)
    )
    return centre + diffusion[:, None, None] * spread - carried


def gaspari(dist_sq):
    scaled = jnp.sqrt(dist_sq) / LOC_HALF
    clipped = jnp.maximum(scaled, 1.0)
    inner_part = (
        ((-0.25 * scaled + 0.5) * scaled + 0.625) * scaled - 5.0 / 3.0
    ) * scaled * scaled + 1.0
    outer_part = (
        ((((scaled / 12.0 - 0.5) * scaled + 0.625) * scaled + 5.0 / 3.0) * scaled - 5.0) * scaled
        + 4.0
        - 2.0 / (3.0 * clipped)
    )
    return jnp.where(scaled <= 1.0, inner_part, jnp.where(scaled <= 2.0, outer_part, 0.0))


def decode(flat_cells, total_rows, n_cols):
    field_ids = flat_cells // (total_rows * n_cols)
    row_ids = flat_cells // n_cols % total_rows
    col_ids = flat_cells % n_cols
    return (field_ids, row_ids, col_ids)


def innovations(priors, obs_values, obs_noise):
    members = priors.shape[0]
    average = jnp.mean(priors, axis=0)
    anomaly = priors - average
    spread = jnp.sum(anomaly * anomaly, axis=0) / (members - 1)
    variance_sum = spread + obs_noise
    root_sum = jnp.sqrt(variance_sum)
    shrink = 1.0 / (root_sum * (jnp.sqrt(obs_noise) + root_sum))
    adjust = (obs_values - average) / variance_sum - shrink * anomaly
    return (anomaly, adjust)


def regress(
    ensemble_now, base_row, obs_field, obs_row, obs_col, anomaly, adjust, field_mask, n_cols
):
    members, n_cells = ensemble_now.shape
    n_fields = field_mask.shape[0]
    per_field = n_cells // n_fields
    local_ids = lax.iota(jnp.int32, per_field)
    cell_row = (base_row + local_ids // n_cols).astype(jnp.float32)
    cell_col = (local_ids % n_cols).astype(jnp.float32)
    centred = ensemble_now - jnp.mean(ensemble_now, axis=0)
    mask_float = field_mask.astype(jnp.float32)
    total_obs = obs_field.shape[0]
    obs_block = min(256, total_obs)
    increment = jnp.zeros_like(ensemble_now)
    for offset in range(0, total_obs, obs_block):
        row_gap = cell_row[:, None] - obs_row[None, offset : offset + obs_block].astype(jnp.float32)
        col_gap = cell_col[:, None] - obs_col[None, offset : offset + obs_block].astype(jnp.float32)
        closeness = gaspari(row_gap * row_gap + col_gap * col_gap)
        field_hot = (
            obs_field[None, offset : offset + obs_block] == lax.iota(jnp.int32, n_fields)[:, None]
        ).astype(jnp.float32)
        allowed = jnp.dot(mask_float, field_hot, precision=precise)
        covariance = lax.dot_general(
            centred,
            anomaly[:, offset : offset + obs_block],
            (((0,), (0,)), ((), ())),
            precision=precise,
        )
        weights = (
            covariance.reshape(n_fields, per_field, obs_block)
            * (closeness[None] * allowed[:, None, :])
            / (members - 1)
        )
        increment = increment + lax.dot_general(
            adjust[:, offset : offset + obs_block],
            weights.reshape(n_cells, obs_block),
            (((1,), (1,)), ((), ())),
            precision=precise,
        )
    return ensemble_now + increment


LANES = 128
MEGA = 1 << 20


def split_two(x):
    high = x.astype(jnp.bfloat16)
    low = (x - high.astype(jnp.float32)).astype(jnp.bfloat16)
    return high, low


def split_three(x):
    high = x.astype(jnp.bfloat16)
    rest = x - high.astype(jnp.float32)
    mid = rest.astype(jnp.bfloat16)
    low = (rest - mid.astype(jnp.float32)).astype(jnp.bfloat16)
    return high, mid, low


def bdot(a, b):
    return jnp.dot(a, b, preferred_element_type=jnp.float32)


def log2(n):
    return n.bit_length() - 1


def start_copies(pairs, sems):
    copies = [pltpu.make_async_copy(src, dst, sems.at[i]) for i, (src, dst) in enumerate(pairs)]
    for copy in copies:
        copy.start()
    return copies


def finish(copies):
    for copy in copies:
        copy.wait()


def prep_kernel(
    order_hbm, cell_hbm, value_hbm, var_hbm, mask_hbm, diffusion_hbm, stack_hbm, velocity_hbm,
    info_ref, own_ref, vel_ref, kappa_ref,
    order_buf, cell_buf, value_buf, var_buf, mask_buf, diffusion_buf, sems,
    *, total_rows, n_cols,
):
    copies = start_copies(
        [
            (order_hbm, order_buf), (cell_hbm, cell_buf), (value_hbm, value_buf), (var_hbm, var_buf),
            (mask_hbm, mask_buf), (diffusion_hbm, diffusion_buf), (velocity_hbm, vel_ref),
            (stack_hbm, own_ref),
        ],
        sems,
    )
    finish(copies[:4])
    table_rows = cell_buf.shape[0]
    n_fields = mask_buf.shape[0]
    order = order_buf[...]
    n_obs = order.shape[1]
    table = jnp.concatenate(
        [cell_buf[...].astype(jnp.float32), value_buf[...], var_buf[...]], axis=0
    )
    parts = jnp.concatenate(split_three(table), axis=0)
    lane_hot = (
        lax.broadcasted_iota(jnp.int32, (LANES, n_obs), 0) == (order & (LANES - 1))
    ).astype(jnp.float32).astype(jnp.bfloat16)
    found = bdot(parts, lane_hot)
    size = 3 * table_rows
    found = (found[:size] + found[size : 2 * size]) + found[2 * size :]
    row_hot = lax.broadcasted_iota(jnp.int32, (table_rows, n_obs), 0) == (order >> log2(LANES))

    def take(i):
        rows = found[i * table_rows : (i + 1) * table_rows]
        return jnp.sum(jnp.where(row_hot, rows, 0.0), axis=0, keepdims=True)

    cell = take(0).astype(jnp.int32)
    strip = cell >> log2(n_cols)
    field = strip >> log2(total_rows)
    row = strip & (total_rows - 1)
    col = cell & (n_cols - 1)
    as_float = lambda x: x.astype(jnp.float32)
    zero = jnp.zeros((1, n_obs), jnp.float32)
    finish(copies[4:])
    for f in range(n_fields):
        kappa_ref[f : f + 1, :] = jnp.full((1, LANES), diffusion_buf[0, f], jnp.float32)
    up = lax.broadcasted_iota(jnp.int32, (8, 8), 0)
    along = lax.broadcasted_iota(jnp.int32, (8, 8), 1)
    mask = jnp.zeros((8, 8), jnp.float32)
    for f in range(n_fields):
        for b in range(n_fields):
            mask = jnp.where((up == f) & (along == b), as_float(mask_buf[f, b]), mask)
    field_hot = as_float(lax.broadcasted_iota(jnp.int32, (8, n_obs), 0) == field)
    info = jnp.concatenate(
        [
            as_float(field), as_float(row), as_float(col), take(1), take(2), as_float(strip), zero, zero,
            bdot(mask.astype(jnp.bfloat16), field_hot.astype(jnp.bfloat16)),
        ],
        axis=0,
    )
    info_ref[...] = info


def forecast_kernel(
    place_ref, kappa_ref, own_ref, other_ref, vel_own_ref, vel_other_ref, info_ref,
    send_ref, field_buf, prior_buf,
):
    n_fields, n_rows, n_cols = field_buf.shape
    half = n_rows // 2
    n_dest = half
    chunk = send_ref.shape[0] // n_dest
    first_slab = place_ref[0:1, 0:1] < 0.5

    def whole_of(own, other):
        return jnp.concatenate([jnp.where(first_slab, own, other), jnp.where(first_slab, other, own)], axis=0)

    u = whole_of(vel_own_ref[0], vel_other_ref[0])
    v = whole_of(vel_own_ref[1], vel_other_ref[1])
    row = lax.broadcasted_iota(jnp.int32, (n_rows, n_cols), 0)
    col = lax.broadcasted_iota(jnp.int32, (n_rows, n_cols), 1)
    u_pos, u_neg = jnp.maximum(u, 0.0), jnp.minimum(u, 0.0)
    v_pos, v_neg = jnp.maximum(v, 0.0), jnp.minimum(v, 0.0)
    outflow = (u_neg - u_pos) + (v_neg - v_pos)
    for f in range(n_fields):
        kappa = kappa_ref[f : f + 1, 0:1]
        k_c = (1.0 - 4.0 * kappa) + outflow
        k_n = jnp.where(row == 0, 0.0, kappa + v_pos)
        k_s = jnp.where(row == n_rows - 1, 0.0, kappa - v_neg)
        k_w = jnp.where(col == 0, 0.0, kappa + u_pos)
        k_e = jnp.where(col == n_cols - 1, 0.0, kappa - u_neg)
        c = whole_of(own_ref[0, f], other_ref[0, f])
        for _ in range(SUBSTEPS):
            c = (
                (c * k_c + pltpu.roll(c, 1, 0) * k_n)
                + (pltpu.roll(c, n_rows - 1, 0) * k_s + pltpu.roll(c, 1, 1) * k_w)
                + pltpu.roll(c, n_cols - 1, 1) * k_e
            )
        field_buf[f] = c
    whole = field_buf[...].reshape(n_fields * n_rows, n_cols)
    strips = n_fields * n_rows
    parts = jnp.concatenate(split_three(whole), axis=0)
    n_obs = info_ref.shape[1]
    width = 2 * LANES
    strip_ids = lax.broadcasted_iota(jnp.int32, (strips, width), 0)
    col_ids = lax.broadcasted_iota(jnp.int32, (n_cols, width), 0)
    for q in range(n_obs // width):
        cols = info_ref[2:3, q * width : (q + 1) * width].astype(jnp.int32)
        strip = info_ref[5:6, q * width : (q + 1) * width].astype(jnp.int32)
        hot = (col_ids == cols).astype(jnp.float32).astype(jnp.bfloat16)
        found = bdot(parts, hot)
        found = (found[:strips] + found[strips : 2 * strips]) + found[2 * strips :]
        values = jnp.sum(jnp.where(strip_ids == strip, found, 0.0), axis=0, keepdims=True)
        for h in range(width // LANES):
            at = q * (width // LANES) + h
            prior_buf[at : at + 1, :] = values[:, h * LANES : (h + 1) * LANES]
    priors = prior_buf[...]
    lead = chunk - n_obs // LANES
    for d in range(n_dest):
        send_ref[d * chunk + lead : (d + 1) * chunk, :] = priors
    pieces = n_cols // LANES
    for f in range(n_fields):
        rows = jnp.where(first_slab, field_buf[f, :half, :], field_buf[f, half:, :])
        for h in range(pieces):
            send_ref[pl.ds(f * pieces + h, n_dest, stride=chunk), :] = rows[
                :, h * LANES : (h + 1) * LANES
            ]
    for i in range(n_fields * pieces, lead):
        send_ref[pl.ds(i, n_dest, stride=chunk), :] = jnp.zeros((n_dest, LANES), jnp.float32)


def closeness_of(dist_sq):
    inverse = lax.rsqrt(jnp.maximum(dist_sq, 1e-6))
    z = dist_sq * inverse
    half_sq = 0.5 * dist_sq
    inner = 1.0 + dist_sq * ((half_sq - 5.0 / 3.0) + z * (0.625 - 0.5 * half_sq))
    left = jnp.maximum(2.0 - z, 0.0)
    left = left * left
    left = left * left
    outer = left * ((dist_sq + (z + z)) - 0.5) * (inverse * (1.0 / 12.0))
    return jnp.where(dist_sq <= 1.0, inner, outer)


def loc_kernel(
    place_ref, info_ref, pair_hi_ref, pair_lo_ref, rest_hbm, cell_hi_hbm, cell_lo_hbm,
    infot_ref, rest_ref, cell_hi_ref, cell_lo_ref, gap_buf, sems,
):
    n_obs = info_ref.shape[1]
    batch, n_pair = pair_hi_ref.shape
    n_cols = cell_hi_ref.shape[1]
    scale = 1.0 / LOC_HALF
    far = 32.0 * LOC_HALF * LOC_HALF
    row, col = info_ref[1:2, :], info_ref[2:3, :]
    norm = [part.astype(jnp.float32) for part in split_three(row * row + col * col)]
    one = jnp.ones((1, n_obs), jnp.float32)
    hot = lax.broadcasted_iota(jnp.int32, (8, n_obs), 0) == info_ref[0:1, :].astype(jnp.int32)
    zeros = jnp.zeros((6, n_obs), jnp.float32)
    feature_k = jnp.concatenate(
        norm + [one, one, one, -2.0 * row, -2.0 * col, -far * info_ref[8:16, :], one * far, row, zeros], axis=0
    )
    feature_j = jnp.concatenate(
        [one, one, one] + norm + [row, col, hot.astype(jnp.float32), one], axis=0
    )[:, batch:]
    infot_ref[...] = feature_k.T
    terms = feature_j.shape[0]
    gap_buf[...] = bdot(
        infot_ref[0:batch, 0:terms].astype(jnp.bfloat16), (feature_j * (scale * scale)).astype(jnp.bfloat16)
    )
    table_rows = 32
    own_row = place_ref[1:2, 0:1]
    gap_row = (lax.broadcasted_iota(jnp.int32, (table_rows, LANES), 0).astype(jnp.float32) - own_row) * scale
    gap_col = lax.broadcasted_iota(jnp.int32, (table_rows, LANES), 1).astype(jnp.float32) * scale
    high, mid, low = split_three(closeness_of(gap_row * gap_row + gap_col * gap_col))
    row_ids = lax.broadcasted_iota(jnp.int32, (1, table_rows), 1)
    copies = []
    col_at, row_at = 7, terms
    for b in range(BATCHES):
        span = slice(b * batch, (b + 1) * batch)
        rows = infot_ref[span, row_at : row_at + 1].astype(jnp.int32)
        hot = (row_ids == rows).astype(jnp.float32).astype(jnp.bfloat16)
        table = (bdot(hot, high) + bdot(hot, mid)) + bdot(hot, low)
        cols = infot_ref[span, col_at : col_at + 1] * -0.5
        col_k = jnp.broadcast_to(cols, (batch, LANES)).astype(jnp.int32)
        for h in range(n_cols // LANES):
            here = slice(h * LANES, (h + 1) * LANES)
            col = lax.broadcasted_iota(jnp.int32, (batch, LANES), 1) + h * LANES
            gap = jnp.minimum(jnp.abs(col - col_k), LANES - 1)
            at_hi, at_lo = split_two(jnp.take_along_axis(table, gap, axis=1))
            cell_hi_ref[span, here] = at_hi
            cell_lo_ref[span, here] = at_lo
        copies += start_copies(
            [
                (cell_hi_ref.at[span, :], cell_hi_hbm.at[span, :]),
                (cell_lo_ref.at[span, :], cell_lo_hbm.at[span, :]),
            ],
            sems.at[2 * b :],
        )
    step = 128
    kept = pair_lo_ref.shape[0]

    def pair_rows(low_ref, first):
        def body(i, carry):
            to = pl.multiple_of(i * step, step)
            at = pl.multiple_of(first + i * step, step)
            for h in range(n_pair // LANES):
                here = slice(h * LANES, (h + 1) * LANES)
                high, low = split_two(closeness_of(gap_buf[pl.ds(at, step), here]))
                pair_hi_ref[pl.ds(at, step), here] = high
                low_ref[pl.ds(to, step), here] = low
            return carry

        lax.fori_loop(0, low_ref.shape[0] // step, body, 0)

    pair_rows(rest_ref, kept)
    copies += start_copies([(rest_ref, rest_hbm)], sems.at[2 * BATCHES :])
    pair_rows(pair_lo_ref, 0)
    finish(copies)


def member_roll(x, shift):
    shift = shift % x.shape[0]
    return pltpu.roll(x, shift, 0) if shift else x


def factors(priors, value, var):
    members = priors.shape[0]
    average = jnp.sum(priors, axis=0, keepdims=True) * (1.0 / members)
    anomaly = priors - average
    variance = jnp.sum(anomaly * anomaly, axis=0, keepdims=True) * (1.0 / (members - 1)) + var
    root = jnp.sqrt(variance)
    shrunk = anomaly * (1.0 / ((members - 1) * (root * (jnp.sqrt(var) + root))))
    rows = [shrunk * member_roll(anomaly, -d) for d in range(members // 2 + 1)]
    rows.append(anomaly * ((value - average) / ((members - 1) * variance)))
    return rows


def combined(state, sums):
    members = state.shape[0]
    centred = state - jnp.sum(state, axis=0, keepdims=True) * (1.0 / members)
    offsets = members // 2
    block = lambda d: sums[d * members : (d + 1) * members]
    move = centred * block(0) + member_roll(centred, -offsets) * block(offsets)
    for d in range(1, offsets):
        move = move + member_roll(centred, -d) * block(d)
        move = move + member_roll(centred * block(d), d)
    shift = jnp.sum(centred * block(offsets + 1), axis=0, keepdims=True)
    return state + (shift - move)


def update_kernel(
    recv_ref, info_ref, pair_hi_ref, pair_lo_ref, rest_hbm, cell_hi_hbm, cell_lo_hbm,
    out_ref, fac_buf, sums_buf, mask_buf, rest_ref, cell_hi_ref, cell_lo_ref, sems, *, members, n_fields,
):
    tables = [(rest_hbm, rest_ref), (cell_hi_hbm, cell_hi_ref), (cell_lo_hbm, cell_lo_ref)]
    copies = [pltpu.make_async_copy(src, dst, sems.at[i]) for i, (src, dst) in enumerate(tables)]
    n_obs = info_ref.shape[1]
    batch = n_obs // BATCHES
    chunk = recv_ref.shape[0] // members
    per_chunk = n_obs // LANES
    lead = chunk - per_chunk
    pieces = cell_hi_ref.shape[1] // LANES
    size = fac_buf.shape[1] // 2
    kept = pair_lo_ref.shape[0]

    def member_row(i):
        return recv_ref[pl.ds(i, members, stride=chunk), :]

    def priors_of(b):
        first = lead + b * (per_chunk // BATCHES)
        return jnp.concatenate([member_row(first + q) for q in range(per_chunk // BATCHES)], axis=1)

    def set_factors(b, priors):
        span = slice(b * batch, (b + 1) * batch)
        rows = factors(priors, info_ref[3:4, span], info_ref[4:5, span])
        for i, r in enumerate(rows):
            high, low = split_two(r)
            fac_buf[b, i * members : (i + 1) * members, :] = high
            fac_buf[b, size + i * members : size + (i + 1) * members, :] = low

    @pl.when(pl.program_id(0) == 0)
    def _():
        for copy in copies:
            copy.start()
        set_factors(0, priors_of(0))
        first = bdot(fac_buf[0], pair_hi_ref[...])
        sums_buf[...] = (first[:size] + first[size:]) + bdot(fac_buf[0, :size, :kept], pair_lo_ref[...])

    @pl.when(pl.program_id(0) == 1)
    def _():
        finish(copies[:1])
        sums = sums_buf[...] + bdot(fac_buf[0, :size, kept:], rest_ref[...])
        set_factors(1, combined(priors_of(1), sums))

    @pl.when(pl.program_id(0) == 2)
    def _():
        finish(copies[1:])
        states = [
            jnp.concatenate([member_row(f * pieces + h) for h in range(pieces)], axis=1)
            for f in range(n_fields)
        ]
        all_rows = n_fields * size
        for b in range(BATCHES):
            span = slice(b * batch, (b + 1) * batch)
            for f in range(n_fields):
                open_to = info_ref[8 + f : 9 + f, span].astype(jnp.bfloat16)
                mask_buf[f * size : (f + 1) * size, :] = fac_buf[b, :size, :] * open_to
                mask_buf[all_rows + f * size : all_rows + (f + 1) * size, :] = fac_buf[b, size:, :] * open_to
            first = bdot(mask_buf[...], cell_hi_ref[span, :])
            sums = (first[:all_rows] + first[all_rows:]) + bdot(mask_buf[:all_rows, :], cell_lo_ref[span, :])
            states = [combined(state, sums[f * size : (f + 1) * size]) for f, state in enumerate(states)]
        for f in range(n_fields):
            out_ref[:, f, 0, 0, :] = states[f]


def vmem_spec():
    return pl.BlockSpec(memory_space=pltpu.VMEM)


def smem_spec():
    return pl.BlockSpec(memory_space=pltpu.SMEM)


def hbm_spec():
    return pl.BlockSpec(memory_space=pltpu.HBM)


def in_hbm(x):
    return pltpu.with_memory_space_constraint(x, pltpu.HBM)


def quick_device(
    realization_stack, velocity, diffusion, obs_cell, obs_order, obs_value, obs_var, field_mask
):
    _, n_fields, rows_here, n_cols = realization_stack.shape
    n_mem = lax.axis_size("mem")
    total_rows = 2 * rows_here
    n_obs = obs_cell.shape[0]
    batch = n_obs // BATCHES
    slab_index = lax.axis_index("row")
    own_row = slab_index * rows_here + lax.axis_index("mem")
    place = jnp.where(
        lax.broadcasted_iota(jnp.int32, (8, LANES), 0) == 0, slab_index, own_row
    ).astype(jnp.float32)
    params = pltpu.CompilerParams(vmem_limit_bytes=16 * MEGA)
    shape = jax.ShapeDtypeStruct
    f32, i32 = jnp.float32, jnp.int32
    swap = [(0, 1), (1, 0)]
    other = lax.ppermute(realization_stack, "row", swap)
    vel_other = lax.ppermute(velocity, "row", swap)
    table = (n_obs // LANES, LANES)
    info, own, vel_own, kappa = pl.pallas_call(
        functools.partial(prep_kernel, total_rows=total_rows, n_cols=n_cols),
        out_shape=(
            shape((16, n_obs), f32),
            shape(realization_stack.shape, f32),
            shape(velocity.shape, f32),
            shape((8, LANES), f32),
        ),
        in_specs=[hbm_spec()] * 8,
        out_specs=(vmem_spec(),) * 4,
        scratch_shapes=[
            pltpu.VMEM((1, n_obs), i32),
            pltpu.VMEM(table, i32),
            pltpu.VMEM(table, f32),
            pltpu.VMEM(table, f32),
            pltpu.SMEM(field_mask.shape, i32),
            pltpu.SMEM((1, n_fields), f32),
            pltpu.SemaphoreType.DMA((8,)),
        ],
        compiler_params=params,
        name="prep",
    )(
        in_hbm(obs_order.reshape(1, n_obs)),
        in_hbm(obs_cell.reshape(table)),
        in_hbm(obs_value.reshape(table)),
        in_hbm(obs_var.reshape(table)),
        in_hbm(field_mask),
        in_hbm(diffusion.reshape(1, n_fields)),
        in_hbm(realization_stack),
        in_hbm(velocity),
    )
    chunk = (n_fields * n_cols + n_obs) // LANES
    send = pl.pallas_call(
        forecast_kernel,
        out_shape=shape((n_mem * chunk, LANES), f32),
        in_specs=[vmem_spec()] * 7,
        out_specs=vmem_spec(),
        scratch_shapes=[
            pltpu.VMEM((n_fields, total_rows, n_cols), f32),
            pltpu.VMEM((n_obs // LANES, LANES), f32),
        ],
        compiler_params=params,
        name="forecast",
    )(place, kappa, own, other, vel_own, vel_other, info)
    recv = lax.all_to_all(
        send.reshape(n_mem, chunk, 1, LANES), "mem", split_axis=0, concat_axis=0, tiled=True
    ).reshape(send.shape)
    n_pair = n_obs - batch
    bf16 = jnp.bfloat16
    kept = batch // 2
    pair_hi, pair_lo, rest, cell_hi, cell_lo = pl.pallas_call(
        loc_kernel,
        out_shape=(
            shape((batch, n_pair), bf16),
            shape((kept, n_pair), bf16),
            pltpu.HBM((batch - kept, n_pair), bf16),
            pltpu.HBM((n_obs, n_cols), bf16),
            pltpu.HBM((n_obs, n_cols), bf16),
        ),
        in_specs=[vmem_spec(), vmem_spec()],
        out_specs=(vmem_spec(), vmem_spec(), hbm_spec(), hbm_spec(), hbm_spec()),
        scratch_shapes=[
            pltpu.VMEM((n_obs, 24), f32),
            pltpu.VMEM((batch - kept, n_pair), bf16),
            pltpu.VMEM((n_obs, n_cols), bf16),
            pltpu.VMEM((n_obs, n_cols), bf16),
            pltpu.VMEM((batch, n_pair), f32),
            pltpu.SemaphoreType.DMA((2 * BATCHES + 1,)),
        ],
        compiler_params=params,
        name="localize",
    )(place, info)
    rows = n_mem * (n_mem // 2 + 2)
    return pl.pallas_call(
        functools.partial(update_kernel, members=n_mem, n_fields=n_fields),
        grid=(3,),
        out_shape=shape((n_mem, n_fields, 1, 1, n_cols), f32),
        in_specs=[vmem_spec()] * 4 + [hbm_spec()] * 3,
        out_specs=vmem_spec(),
        scratch_shapes=[
            pltpu.VMEM((BATCHES, 2 * rows, batch), bf16),
            pltpu.VMEM((rows, n_pair), f32),
            pltpu.VMEM((2 * rows * n_fields, batch), bf16),
            pltpu.VMEM((batch - kept, n_pair), bf16),
            pltpu.VMEM((n_obs, n_cols), bf16),
            pltpu.VMEM((n_obs, n_cols), bf16),
            pltpu.SemaphoreType.DMA((3,)),
        ],
        compiler_params=params,
        name="update",
    )(recv, info, pair_hi, pair_lo, in_hbm(rest), in_hbm(cell_hi), in_hbm(cell_lo))


def is_quick(realization_stack, obs_cell, n_mem, n_slab):
    local_members, n_fields, rows_here, n_cols = realization_stack.shape
    powers = all(n & (n - 1) == 0 for n in (rows_here, n_cols))
    return (
        n_slab == 2
        and local_members == 1
        and n_mem == rows_here == 16
        and n_fields <= 8
        and LOC_HALF * 2 <= LANES - 1
        and powers
        and n_cols % LANES == 0
        and obs_cell.shape[0] == 8 * n_cols
        and BATCHES == 2
    )


def per_device(
    realization_stack, velocity, diffusion, obs_cell, obs_order, obs_value, obs_var, field_mask
):
    local_members = realization_stack.shape[0]
    n_fields = realization_stack.shape[1]
    rows_here = realization_stack.shape[2]
    n_cols = realization_stack.shape[3]
    n_mem = lax.axis_size("mem")
    n_slab = lax.axis_size("row")
    total_members = local_members * n_mem
    total_rows = rows_here * n_slab
    if is_quick(realization_stack, obs_cell, n_mem, n_slab):
        return quick_device(
            realization_stack, velocity, diffusion, obs_cell, obs_order, obs_value, obs_var, field_mask
        )
    slab_index = lax.axis_index("row")
    member_index = lax.axis_index("mem")
    row_sub = rows_here // n_mem
    current = realization_stack
    for substep in range(SUBSTEPS):
        padded = extended(current, (("row", 2),), 1)
        current = advance(padded, velocity, diffusion)
    field_all, row_all, col_all = decode(obs_cell, total_rows, n_cols)
    batch_size = obs_cell.shape[0] // BATCHES
    layout = lax.all_to_all(current, "mem", split_axis=2, concat_axis=0, tiled=True)
    ensemble_now = layout.reshape(total_members, -1)
    base_row = slab_index * rows_here + member_index * row_sub
    for batch_num in range(BATCHES):
        picked = obs_order[batch_num * batch_size : (batch_num + 1) * batch_size]
        obs_field = field_all[picked]
        obs_row = row_all[picked]
        obs_col = col_all[picked]
        owned = ((obs_row >= base_row) & (obs_row < base_row + row_sub)).astype(jnp.float32)
        local_ids = (
            obs_field * row_sub * n_cols
            + jnp.clip(obs_row - base_row, 0, row_sub - 1) * n_cols
            + obs_col
        )
        partial_priors = jnp.take(ensemble_now, local_ids, axis=1) * owned[None, :]
        priors = lax.psum(partial_priors, ("mem", "row"))
        anomaly, adjust = innovations(priors, obs_value[picked], obs_var[picked])
        ensemble_now = regress(
            ensemble_now, base_row, obs_field, obs_row, obs_col, anomaly, adjust, field_mask, n_cols
        )
    return ensemble_now.reshape(total_members, n_fields, 1, row_sub, n_cols)


def solution(mesh):
    in_specs = (P("mem", None, "row", None), P(None, "row", None), P(), P(), P(), P(), P(), P())
    out_specs = P(None, None, "row", "mem", None)
    return jax.shard_map(
        per_device, mesh=mesh, in_specs=in_specs, out_specs=out_specs, check_vma=False
    )
```

```python
import functools

import jax
import jax.numpy as jnp
from jax import lax
from jax.experimental import pallas as pl
from jax.experimental.pallas import tpu as pltpu
from jax.sharding import PartitionSpec as P

SUBSTEPS = 4
BATCHES = 2
LOC_HALF = 32


precise = lax.Precision.HIGHEST


def extended(shard, sides, width):
    for axis, dim in sides:
        count, length = (lax.axis_size(axis), shard.shape[dim])
        up = [(i, (i + 1) % count) for i in range(count - 1)]
        down = [(j, i) for i, j in up]
        last = lax.slice_in_dim(shard, length - width, length, axis=dim)
        initial = lax.slice_in_dim(shard, 0, width, axis=dim)
        before = lax.ppermute(last, axis, up)
        after = lax.ppermute(initial, axis, down)
        shard = jnp.concatenate([before, shard, after], axis=dim)
    return shard


def advance(padded, velocity, diffusion):
    spec_pad = ((0, 0),) * (padded.ndim - 1) + ((1, 1),)
    col_padded = jnp.pad(padded, spec_pad)
    centre = col_padded[..., 1:-1, 1:-1]
    north_cell = col_padded[..., :-2, 1:-1]
    south_cell = col_padded[..., 2:, 1:-1]
    west_cell = col_padded[..., 1:-1, :-2]
    east_cell = col_padded[..., 1:-1, 2:]
    along_col = velocity[0]
    along_row = velocity[1]
    spread = north_cell + south_cell + west_cell + east_cell - 4.0 * centre
    carried = (
        jnp.maximum(along_col, 0.0) * (centre - west_cell)
        + jnp.minimum(along_col, 0.0) * (east_cell - centre)
        + jnp.maximum(along_row, 0.0) * (centre - north_cell)
        + jnp.minimum(along_row, 0.0) * (south_cell - centre)
    )
    return centre + diffusion[:, None, None] * spread - carried


def gaspari(dist_sq):
    scaled = jnp.sqrt(dist_sq) / LOC_HALF
    clipped = jnp.maximum(scaled, 1.0)
    inner_part = (
        ((-0.25 * scaled + 0.5) * scaled + 0.625) * scaled - 5.0 / 3.0
    ) * scaled * scaled + 1.0
    outer_part = (
        ((((scaled / 12.0 - 0.5) * scaled + 0.625) * scaled + 5.0 / 3.0) * scaled - 5.0) * scaled
        + 4.0
        - 2.0 / (3.0 * clipped)
    )
    return jnp.where(scaled <= 1.0, inner_part, jnp.where(scaled <= 2.0, outer_part, 0.0))


def decode(flat_cells, total_rows, n_cols):
    field_ids = flat_cells // (total_rows * n_cols)
    row_ids = flat_cells // n_cols % total_rows
    col_ids = flat_cells % n_cols
    return (field_ids, row_ids, col_ids)


def innovations(priors, obs_values, obs_noise):
    members = priors.shape[0]
    average = jnp.mean(priors, axis=0)
    anomaly = priors - average
    spread = jnp.sum(anomaly * anomaly, axis=0) / (members - 1)
    variance_sum = spread + obs_noise
    root_sum = jnp.sqrt(variance_sum)
    shrink = 1.0 / (root_sum * (jnp.sqrt(obs_noise) + root_sum))
    adjust = (obs_values - average) / variance_sum - shrink * anomaly
    return (anomaly, adjust)


def regress(
    ensemble_now, base_row, obs_field, obs_row, obs_col, anomaly, adjust, field_mask, n_cols
):
    members, n_cells = ensemble_now.shape
    n_fields = field_mask.shape[0]
    per_field = n_cells // n_fields
    local_ids = lax.iota(jnp.int32, per_field)
    cell_row = (base_row + local_ids // n_cols).astype(jnp.float32)
    cell_col = (local_ids % n_cols).astype(jnp.float32)
    centred = ensemble_now - jnp.mean(ensemble_now, axis=0)
    mask_float = field_mask.astype(jnp.float32)
    total_obs = obs_field.shape[0]
    obs_block = min(256, total_obs)
    increment = jnp.zeros_like(ensemble_now)
    for offset in range(0, total_obs, obs_block):
        row_gap = cell_row[:, None] - obs_row[None, offset : offset + obs_block].astype(jnp.float32)
        col_gap = cell_col[:, None] - obs_col[None, offset : offset + obs_block].astype(jnp.float32)
        closeness = gaspari(row_gap * row_gap + col_gap * col_gap)
        field_hot = (
            obs_field[None, offset : offset + obs_block] == lax.iota(jnp.int32, n_fields)[:, None]
        ).astype(jnp.float32)
        allowed = jnp.dot(mask_float, field_hot, precision=precise)
        covariance = lax.dot_general(
            centred,
            anomaly[:, offset : offset + obs_block],
            (((0,), (0,)), ((), ())),
            precision=precise,
        )
        weights = (
            covariance.reshape(n_fields, per_field, obs_block)
            * (closeness[None] * allowed[:, None, :])
            / (members - 1)
        )
        increment = increment + lax.dot_general(
            adjust[:, offset : offset + obs_block],
            weights.reshape(n_cells, obs_block),
            (((1,), (1,)), ((), ())),
            precision=precise,
        )
    return ensemble_now + increment


LANES = 128
MEGA = 1 << 20


def split_two(x):
    high = x.astype(jnp.bfloat16)
    low = (x - high.astype(jnp.float32)).astype(jnp.bfloat16)
    return high, low


def split_three(x):
    high = x.astype(jnp.bfloat16)
    rest = x - high.astype(jnp.float32)
    mid = rest.astype(jnp.bfloat16)
    low = (rest - mid.astype(jnp.float32)).astype(jnp.bfloat16)
    return high, mid, low


def bdot(a, b):
    return jnp.dot(a, b, preferred_element_type=jnp.float32)


def log2(n):
    return n.bit_length() - 1


def start_copies(pairs, sems):
    copies = [pltpu.make_async_copy(src, dst, sems.at[i]) for i, (src, dst) in enumerate(pairs)]
    for copy in copies:
        copy.start()
    return copies


def finish(copies):
    for copy in copies:
        copy.wait()


def prep_kernel(
    order_hbm, cell_hbm, value_hbm, var_hbm, mask_hbm, diffusion_hbm, stack_hbm, velocity_hbm,
    info_ref, own_ref, vel_ref, kappa_ref,
    order_buf, cell_buf, value_buf, var_buf, mask_buf, diffusion_buf, sems,
    *, total_rows, n_cols,
):
    copies = start_copies(
        [
            (order_hbm, order_buf), (cell_hbm, cell_buf), (value_hbm, value_buf), (var_hbm, var_buf),
            (mask_hbm, mask_buf), (diffusion_hbm, diffusion_buf), (velocity_hbm, vel_ref),
            (stack_hbm, own_ref),
        ],
        sems,
    )
    finish(copies[:4])
    table_rows = cell_buf.shape[0]
    n_fields = mask_buf.shape[0]
    order = order_buf[...]
    n_obs = order.shape[1]
    table = jnp.concatenate(
        [cell_buf[...].astype(jnp.float32), value_buf[...], var_buf[...]], axis=0
    )
    parts = jnp.concatenate(split_three(table), axis=0)
    lane_hot = (
        lax.broadcasted_iota(jnp.int32, (LANES, n_obs), 0) == (order & (LANES - 1))
    ).astype(jnp.float32).astype(jnp.bfloat16)
    found = bdot(parts, lane_hot)
    size = 3 * table_rows
    found = (found[:size] + found[size : 2 * size]) + found[2 * size :]
    row_hot = lax.broadcasted_iota(jnp.int32, (table_rows, n_obs), 0) == (order >> log2(LANES))

    def take(i):
        rows = found[i * table_rows : (i + 1) * table_rows]
        return jnp.sum(jnp.where(row_hot, rows, 0.0), axis=0, keepdims=True)

    cell = take(0).astype(jnp.int32)
    strip = cell >> log2(n_cols)
    field = strip >> log2(total_rows)
    row = strip & (total_rows - 1)
    col = cell & (n_cols - 1)
    as_float = lambda x: x.astype(jnp.float32)
    zero = jnp.zeros((1, n_obs), jnp.float32)
    finish(copies[4:])
    for f in range(n_fields):
        kappa_ref[f : f + 1, :] = jnp.full((1, LANES), diffusion_buf[0, f], jnp.float32)
    up = lax.broadcasted_iota(jnp.int32, (8, 8), 0)
    along = lax.broadcasted_iota(jnp.int32, (8, 8), 1)
    mask = jnp.zeros((8, 8), jnp.float32)
    for f in range(n_fields):
        for b in range(n_fields):
            mask = jnp.where((up == f) & (along == b), as_float(mask_buf[f, b]), mask)
    field_hot = as_float(lax.broadcasted_iota(jnp.int32, (8, n_obs), 0) == field)
    info = jnp.concatenate(
        [
            as_float(field), as_float(row), as_float(col), take(1), take(2), as_float(strip), zero, zero,
            bdot(mask.astype(jnp.bfloat16), field_hot.astype(jnp.bfloat16)),
        ],
        axis=0,
    )
    info_ref[...] = info


def forecast_kernel(
    place_ref, kappa_ref, own_ref, other_ref, vel_own_ref, vel_other_ref, info_ref,
    send_ref, field_buf, prior_buf,
):
    n_fields, n_rows, n_cols = field_buf.shape
    half = n_rows // 2
    n_dest = half
    chunk = send_ref.shape[0] // n_dest
    first_slab = place_ref[0:1, 0:1] < 0.5

    def whole_of(own, other):
        return jnp.concatenate([jnp.where(first_slab, own, other), jnp.where(first_slab, other, own)], axis=0)

    u = whole_of(vel_own_ref[0], vel_other_ref[0])
    v = whole_of(vel_own_ref[1], vel_other_ref[1])
    row = lax.broadcasted_iota(jnp.int32, (n_rows, n_cols), 0)
    col = lax.broadcasted_iota(jnp.int32, (n_rows, n_cols), 1)
    u_pos, u_neg = jnp.maximum(u, 0.0), jnp.minimum(u, 0.0)
    v_pos, v_neg = jnp.maximum(v, 0.0), jnp.minimum(v, 0.0)
    outflow = (u_neg - u_pos) + (v_neg - v_pos)
    cells, weights = [], []
    for f in range(n_fields):
        kappa = kappa_ref[f : f + 1, 0:1]
        weights.append((
            (1.0 - 4.0 * kappa) + outflow,
            jnp.where(row == 0, 0.0, kappa + v_pos),
            jnp.where(row == n_rows - 1, 0.0, kappa - v_neg),
            jnp.where(col == 0, 0.0, kappa + u_pos),
            jnp.where(col == n_cols - 1, 0.0, kappa - u_neg),
        ))
        cells.append(whole_of(own_ref[0, f], other_ref[0, f]))
    for _ in range(SUBSTEPS):
        for f in range(n_fields):
            c = cells[f]
            k_c, k_n, k_s, k_w, k_e = weights[f]
            cells[f] = (
                (c * k_c + pltpu.roll(c, 1, 0) * k_n)
                + (pltpu.roll(c, n_rows - 1, 0) * k_s + pltpu.roll(c, 1, 1) * k_w)
                + pltpu.roll(c, n_cols - 1, 1) * k_e
            )
    for f in range(n_fields):
        field_buf[f] = cells[f]
    whole = field_buf[...].reshape(n_fields * n_rows, n_cols)
    strips = n_fields * n_rows
    parts = jnp.concatenate(split_three(whole), axis=0)
    n_obs = info_ref.shape[1]
    width = 2 * LANES
    strip_ids = lax.broadcasted_iota(jnp.int32, (strips, width), 0)
    col_ids = lax.broadcasted_iota(jnp.int32, (n_cols, width), 0)
    for q in range(n_obs // width):
        cols = info_ref[2:3, q * width : (q + 1) * width].astype(jnp.int32)
        strip = info_ref[5:6, q * width : (q + 1) * width].astype(jnp.int32)
        hot = (col_ids == cols).astype(jnp.float32).astype(jnp.bfloat16)
        found = bdot(parts, hot)
        found = (found[:strips] + found[strips : 2 * strips]) + found[2 * strips :]
        values = jnp.sum(jnp.where(strip_ids == strip, found, 0.0), axis=0, keepdims=True)
        for h in range(width // LANES):
            at = q * (width // LANES) + h
            prior_buf[at : at + 1, :] = values[:, h * LANES : (h + 1) * LANES]
    priors = prior_buf[...]
    lead = chunk - n_obs // LANES
    for d in range(n_dest):
        send_ref[d * chunk + lead : (d + 1) * chunk, :] = priors
    pieces = n_cols // LANES
    for f in range(n_fields):
        rows = jnp.where(first_slab, field_buf[f, :half, :], field_buf[f, half:, :])
        for h in range(pieces):
            send_ref[pl.ds(f * pieces + h, n_dest, stride=chunk), :] = rows[
                :, h * LANES : (h + 1) * LANES
            ]
    for i in range(n_fields * pieces, lead):
        send_ref[pl.ds(i, n_dest, stride=chunk), :] = jnp.zeros((n_dest, LANES), jnp.float32)


def closeness_of(dist_sq):
    inverse = lax.rsqrt(jnp.maximum(dist_sq, 1e-6))
    z = dist_sq * inverse
    half_sq = 0.5 * dist_sq
    inner = 1.0 + dist_sq * ((half_sq - 5.0 / 3.0) + z * (0.625 - 0.5 * half_sq))
    left = jnp.maximum(2.0 - z, 0.0)
    left = left * left
    left = left * left
    outer = left * ((dist_sq + (z + z)) - 0.5) * (inverse * (1.0 / 12.0))
    return jnp.where(dist_sq <= 1.0, inner, outer)


def loc_kernel(
    place_ref, info_ref, pair_hi_ref, pair_lo_ref, rest_hbm, cell_hi_hbm, cell_lo_hbm,
    infot_ref, rest_ref, cell_hi_ref, cell_lo_ref, gap_buf, sems,
):
    n_obs = info_ref.shape[1]
    batch, n_pair = pair_hi_ref.shape
    n_cols = cell_hi_ref.shape[1]
    scale = 1.0 / LOC_HALF
    far = 32.0 * LOC_HALF * LOC_HALF
    row, col = info_ref[1:2, :], info_ref[2:3, :]
    norm = [part.astype(jnp.float32) for part in split_three(row * row + col * col)]
    one = jnp.ones((1, n_obs), jnp.float32)
    hot = lax.broadcasted_iota(jnp.int32, (8, n_obs), 0) == info_ref[0:1, :].astype(jnp.int32)
    zeros = jnp.zeros((6, n_obs), jnp.float32)
    feature_k = jnp.concatenate(
        norm + [one, one, one, -2.0 * row, -2.0 * col, -far * info_ref[8:16, :], one * far, row, zeros], axis=0
    )
    feature_j = jnp.concatenate(
        [one, one, one] + norm + [row, col, hot.astype(jnp.float32), one], axis=0
    )[:, batch:]
    infot_ref[...] = feature_k.T
    terms = feature_j.shape[0]
    gap_buf[...] = bdot(
        infot_ref[0:batch, 0:terms].astype(jnp.bfloat16), (feature_j * (scale * scale)).astype(jnp.bfloat16)
    )
    table_rows = 32
    own_row = place_ref[1:2, 0:1]
    gap_row = (lax.broadcasted_iota(jnp.int32, (table_rows, LANES), 0).astype(jnp.float32) - own_row) * scale
    gap_col = lax.broadcasted_iota(jnp.int32, (table_rows, LANES), 1).astype(jnp.float32) * scale
    high, mid, low = split_three(closeness_of(gap_row * gap_row + gap_col * gap_col))
    row_ids = lax.broadcasted_iota(jnp.int32, (1, table_rows), 1)
    copies = []
    col_at, row_at = 7, terms
    for b in range(BATCHES):
        span = slice(b * batch, (b + 1) * batch)
        rows = infot_ref[span, row_at : row_at + 1].astype(jnp.int32)
        hot = (row_ids == rows).astype(jnp.float32).astype(jnp.bfloat16)
        table = (bdot(hot, high) + bdot(hot, mid)) + bdot(hot, low)
        cols = infot_ref[span, col_at : col_at + 1] * -0.5
        col_k = jnp.broadcast_to(cols, (batch, LANES)).astype(jnp.int32)
        for h in range(n_cols // LANES):
            here = slice(h * LANES, (h + 1) * LANES)
            col = lax.broadcasted_iota(jnp.int32, (batch, LANES), 1) + h * LANES
            gap = jnp.minimum(jnp.abs(col - col_k), LANES - 1)
            at_hi, at_lo = split_two(jnp.take_along_axis(table, gap, axis=1))
            cell_hi_ref[span, here] = at_hi
            cell_lo_ref[span, here] = at_lo
        copies += start_copies(
            [
                (cell_hi_ref.at[span, :], cell_hi_hbm.at[span, :]),
                (cell_lo_ref.at[span, :], cell_lo_hbm.at[span, :]),
            ],
            sems.at[2 * b :],
        )
    step = 128
    kept = pair_lo_ref.shape[0]

    def pair_rows(low_ref, first):
        def body(i, carry):
            to = pl.multiple_of(i * step, step)
            at = pl.multiple_of(first + i * step, step)
            for h in range(n_pair // LANES):
                here = slice(h * LANES, (h + 1) * LANES)
                high, low = split_two(closeness_of(gap_buf[pl.ds(at, step), here]))
                pair_hi_ref[pl.ds(at, step), here] = high
                low_ref[pl.ds(to, step), here] = low
            return carry

        lax.fori_loop(0, low_ref.shape[0] // step, body, 0)

    pair_rows(rest_ref, kept)
    copies += start_copies([(rest_ref, rest_hbm)], sems.at[2 * BATCHES :])
    pair_rows(pair_lo_ref, 0)
    finish(copies)


def member_roll(x, shift):
    shift = shift % x.shape[0]
    return pltpu.roll(x, shift, 0) if shift else x


def factors(priors, value, var):
    members = priors.shape[0]
    average = jnp.sum(priors, axis=0, keepdims=True) * (1.0 / members)
    anomaly = priors - average
    variance = jnp.sum(anomaly * anomaly, axis=0, keepdims=True) * (1.0 / (members - 1)) + var
    root = jnp.sqrt(variance)
    shrunk = anomaly * (1.0 / ((members - 1) * (root * (jnp.sqrt(var) + root))))
    rows = [shrunk * member_roll(anomaly, -d) for d in range(members // 2)]
    rows.append(anomaly * ((value - average) / ((members - 1) * variance)))
    return rows


def combined(state, sums):
    members = state.shape[0]
    half = members // 2
    centred = state - jnp.sum(state, axis=0, keepdims=True) * (1.0 / members)
    block = lambda d: sums[d * members : (d + 1) * members]
    across = member_roll(centred, half)
    move = (centred - across) * block(0)
    for d in range(1, half):
        move = move + (member_roll(centred, -d) - across) * block(d)
        move = move + member_roll((centred - member_roll(across, -d)) * block(d), d)
    shift = jnp.sum(centred * block(half), axis=0, keepdims=True)
    return state + (shift - move)


def update_kernel(
    recv_ref, info_ref, pair_hi_ref, pair_lo_ref, rest_hbm, cell_hi_hbm, cell_lo_hbm,
    out_ref, fac_buf, sums_buf, mask_buf, rest_ref, cell_hi_ref, cell_lo_ref, sems, *, members, n_fields,
):
    tables = [(rest_hbm, rest_ref), (cell_hi_hbm, cell_hi_ref), (cell_lo_hbm, cell_lo_ref)]
    copies = [pltpu.make_async_copy(src, dst, sems.at[i]) for i, (src, dst) in enumerate(tables)]
    n_obs = info_ref.shape[1]
    batch = n_obs // BATCHES
    chunk = recv_ref.shape[0] // members
    per_chunk = n_obs // LANES
    lead = chunk - per_chunk
    pieces = cell_hi_ref.shape[1] // LANES
    size = fac_buf.shape[1] // 2
    kept = pair_lo_ref.shape[0]

    def member_row(i):
        return recv_ref[pl.ds(i, members, stride=chunk), :]

    def priors_of(b):
        first = lead + b * (per_chunk // BATCHES)
        return jnp.concatenate([member_row(first + q) for q in range(per_chunk // BATCHES)], axis=1)

    def set_factors(b, priors):
        span = slice(b * batch, (b + 1) * batch)
        rows = factors(priors, info_ref[3:4, span], info_ref[4:5, span])
        for i, r in enumerate(rows):
            high, low = split_two(r)
            fac_buf[b, i * members : (i + 1) * members, :] = high
            fac_buf[b, size + i * members : size + (i + 1) * members, :] = low

    def run(step, carry):
        @pl.when(step == 0)
        def _():
            for copy in copies:
                copy.start()
            set_factors(0, priors_of(0))
            first = bdot(fac_buf[0], pair_hi_ref[...])
            sums_buf[...] = (first[:size] + first[size:]) + bdot(fac_buf[0, :size, :kept], pair_lo_ref[...])

        @pl.when(step == 1)
        def _():
            finish(copies[:1])
            sums = sums_buf[...] + bdot(fac_buf[0, :size, kept:], rest_ref[...])
            set_factors(1, combined(priors_of(1), sums))

        @pl.when(step == 2)
        def _():
            finish(copies[1:])
            states = [
                jnp.concatenate([member_row(f * pieces + h) for h in range(pieces)], axis=1)
                for f in range(n_fields)
            ]
            all_rows = n_fields * size
            for b in range(BATCHES):
                span = slice(b * batch, (b + 1) * batch)
                for f in range(n_fields):
                    open_to = info_ref[8 + f : 9 + f, span].astype(jnp.bfloat16)
                    mask_buf[f * size : (f + 1) * size, :] = fac_buf[b, :size, :] * open_to
                    mask_buf[all_rows + f * size : all_rows + (f + 1) * size, :] = fac_buf[b, size:, :] * open_to
                first = bdot(mask_buf[...], cell_hi_ref[span, :])
                sums = (first[:all_rows] + first[all_rows:]) + bdot(mask_buf[:all_rows, :], cell_lo_ref[span, :])
                states = [combined(state, sums[f * size : (f + 1) * size]) for f, state in enumerate(states)]
            for f in range(n_fields):
                out_ref[:, f, 0, 0, :] = states[f]

        return carry

    lax.fori_loop(0, 3, run, 0)


def vmem_spec():
    return pl.BlockSpec(memory_space=pltpu.VMEM)


def smem_spec():
    return pl.BlockSpec(memory_space=pltpu.SMEM)


def hbm_spec():
    return pl.BlockSpec(memory_space=pltpu.HBM)


def in_hbm(x):
    return pltpu.with_memory_space_constraint(x, pltpu.HBM)


def quick_device(
    realization_stack, velocity, diffusion, obs_cell, obs_order, obs_value, obs_var, field_mask
):
    _, n_fields, rows_here, n_cols = realization_stack.shape
    n_mem = lax.axis_size("mem")
    total_rows = 2 * rows_here
    n_obs = obs_cell.shape[0]
    batch = n_obs // BATCHES
    slab_index = lax.axis_index("row")
    own_row = slab_index * rows_here + lax.axis_index("mem")
    place = jnp.where(
        lax.broadcasted_iota(jnp.int32, (8, LANES), 0) == 0, slab_index, own_row
    ).astype(jnp.float32)
    params = pltpu.CompilerParams(vmem_limit_bytes=16 * MEGA)
    shape = jax.ShapeDtypeStruct
    f32, i32 = jnp.float32, jnp.int32
    swap = [(0, 1), (1, 0)]
    other = lax.ppermute(realization_stack, "row", swap)
    vel_other = lax.ppermute(velocity, "row", swap)
    table = (n_obs // LANES, LANES)
    info, own, vel_own, kappa = pl.pallas_call(
        functools.partial(prep_kernel, total_rows=total_rows, n_cols=n_cols),
        out_shape=(
            shape((16, n_obs), f32),
            shape(realization_stack.shape, f32),
            shape(velocity.shape, f32),
            shape((8, LANES), f32),
        ),
        in_specs=[hbm_spec()] * 8,
        out_specs=(vmem_spec(),) * 4,
        scratch_shapes=[
            pltpu.VMEM((1, n_obs), i32),
            pltpu.VMEM(table, i32),
            pltpu.VMEM(table, f32),
            pltpu.VMEM(table, f32),
            pltpu.SMEM(field_mask.shape, i32),
            pltpu.SMEM((1, n_fields), f32),
            pltpu.SemaphoreType.DMA((8,)),
        ],
        compiler_params=params,
        name="prep",
    )(
        in_hbm(obs_order.reshape(1, n_obs)),
        in_hbm(obs_cell.reshape(table)),
        in_hbm(obs_value.reshape(table)),
        in_hbm(obs_var.reshape(table)),
        in_hbm(field_mask),
        in_hbm(diffusion.reshape(1, n_fields)),
        in_hbm(realization_stack),
        in_hbm(velocity),
    )
    chunk = (n_fields * n_cols + n_obs) // LANES
    send = pl.pallas_call(
        forecast_kernel,
        out_shape=shape((n_mem * chunk, LANES), f32),
        in_specs=[vmem_spec()] * 7,
        out_specs=vmem_spec(),
        scratch_shapes=[
            pltpu.VMEM((n_fields, total_rows, n_cols), f32),
            pltpu.VMEM((n_obs // LANES, LANES), f32),
        ],
        compiler_params=params,
        name="forecast",
    )(place, kappa, own, other, vel_own, vel_other, info)
    recv = lax.all_to_all(
        send.reshape(n_mem, chunk, 1, LANES), "mem", split_axis=0, concat_axis=0, tiled=True
    ).reshape(send.shape)
    n_pair = n_obs - batch
    bf16 = jnp.bfloat16
    kept = batch // 2
    pair_hi, pair_lo, rest, cell_hi, cell_lo = pl.pallas_call(
        loc_kernel,
        out_shape=(
            shape((batch, n_pair), bf16),
            shape((kept, n_pair), bf16),
            pltpu.HBM((batch - kept, n_pair), bf16),
            pltpu.HBM((n_obs, n_cols), bf16),
            pltpu.HBM((n_obs, n_cols), bf16),
        ),
        in_specs=[vmem_spec(), vmem_spec()],
        out_specs=(vmem_spec(), vmem_spec(), hbm_spec(), hbm_spec(), hbm_spec()),
        scratch_shapes=[
            pltpu.VMEM((n_obs, 24), f32),
            pltpu.VMEM((batch - kept, n_pair), bf16),
            pltpu.VMEM((n_obs, n_cols), bf16),
            pltpu.VMEM((n_obs, n_cols), bf16),
            pltpu.VMEM((batch, n_pair), f32),
            pltpu.SemaphoreType.DMA((2 * BATCHES + 1,)),
        ],
        compiler_params=params,
        name="localize",
    )(place, info)
    rows = n_mem * (n_mem // 2 + 1)
    return pl.pallas_call(
        functools.partial(update_kernel, members=n_mem, n_fields=n_fields),
        out_shape=shape((n_mem, n_fields, 1, 1, n_cols), f32),
        in_specs=[vmem_spec()] * 4 + [hbm_spec()] * 3,
        out_specs=vmem_spec(),
        scratch_shapes=[
            pltpu.VMEM((BATCHES, 2 * rows, batch), bf16),
            pltpu.VMEM((rows, n_pair), f32),
            pltpu.VMEM((2 * rows * n_fields, batch), bf16),
            pltpu.VMEM((batch - kept, n_pair), bf16),
            pltpu.VMEM((n_obs, n_cols), bf16),
            pltpu.VMEM((n_obs, n_cols), bf16),
            pltpu.SemaphoreType.DMA((3,)),
        ],
        compiler_params=params,
        name="update",
    )(recv, info, pair_hi, pair_lo, in_hbm(rest), in_hbm(cell_hi), in_hbm(cell_lo))


def is_quick(realization_stack, obs_cell, n_mem, n_slab):
    local_members, n_fields, rows_here, n_cols = realization_stack.shape
    powers = all(n & (n - 1) == 0 for n in (rows_here, n_cols))
    return (
        n_slab == 2
        and local_members == 1
        and n_mem == rows_here == 16
        and n_fields <= 8
        and LOC_HALF * 2 <= LANES - 1
        and powers
        and n_cols % LANES == 0
        and obs_cell.shape[0] == 8 * n_cols
        and BATCHES == 2
    )


def per_device(
    realization_stack, velocity, diffusion, obs_cell, obs_order, obs_value, obs_var, field_mask
):
    local_members = realization_stack.shape[0]
    n_fields = realization_stack.shape[1]
    rows_here = realization_stack.shape[2]
    n_cols = realization_stack.shape[3]
    n_mem = lax.axis_size("mem")
    n_slab = lax.axis_size("row")
    total_members = local_members * n_mem
    total_rows = rows_here * n_slab
    if is_quick(realization_stack, obs_cell, n_mem, n_slab):
        return quick_device(
            realization_stack, velocity, diffusion, obs_cell, obs_order, obs_value, obs_var, field_mask
        )
    slab_index = lax.axis_index("row")
    member_index = lax.axis_index("mem")
    row_sub = rows_here // n_mem
    current = realization_stack
    for substep in range(SUBSTEPS):
        padded = extended(current, (("row", 2),), 1)
        current = advance(padded, velocity, diffusion)
    field_all, row_all, col_all = decode(obs_cell, total_rows, n_cols)
    batch_size = obs_cell.shape[0] // BATCHES
    layout = lax.all_to_all(current, "mem", split_axis=2, concat_axis=0, tiled=True)
    ensemble_now = layout.reshape(total_members, -1)
    base_row = slab_index * rows_here + member_index * row_sub
    for batch_num in range(BATCHES):
        picked = obs_order[batch_num * batch_size : (batch_num + 1) * batch_size]
        obs_field = field_all[picked]
        obs_row = row_all[picked]
        obs_col = col_all[picked]
        owned = ((obs_row >= base_row) & (obs_row < base_row + row_sub)).astype(jnp.float32)
        local_ids = (
            obs_field * row_sub * n_cols
            + jnp.clip(obs_row - base_row, 0, row_sub - 1) * n_cols
            + obs_col
        )
        partial_priors = jnp.take(ensemble_now, local_ids, axis=1) * owned[None, :]
        priors = lax.psum(partial_priors, ("mem", "row"))
        anomaly, adjust = innovations(priors, obs_value[picked], obs_var[picked])
        ensemble_now = regress(
            ensemble_now, base_row, obs_field, obs_row, obs_col, anomaly, adjust, field_mask, n_cols
        )
    return ensemble_now.reshape(total_members, n_fields, 1, row_sub, n_cols)


def solution(mesh):
    in_specs = (P("mem", None, "row", None), P(None, "row", None), P(), P(), P(), P(), P(), P())
    out_specs = P(None, None, "row", "mem", None)
    return jax.shard_map(
        per_device, mesh=mesh, in_specs=in_specs, out_specs=out_specs, check_vma=False
    )
```

```python
import functools

import jax
import jax.numpy as jnp
from jax import lax
from jax.experimental import pallas as pl
from jax.experimental.pallas import tpu as pltpu
from jax.sharding import PartitionSpec as P

SUBSTEPS = 4
BATCHES = 2
LOC_HALF = 32


precise = lax.Precision.HIGHEST


def extended(shard, sides, width):
    for axis, dim in sides:
        count, length = (lax.axis_size(axis), shard.shape[dim])
        up = [(i, (i + 1) % count) for i in range(count - 1)]
        down = [(j, i) for i, j in up]
        last = lax.slice_in_dim(shard, length - width, length, axis=dim)
        initial = lax.slice_in_dim(shard, 0, width, axis=dim)
        before = lax.ppermute(last, axis, up)
        after = lax.ppermute(initial, axis, down)
        shard = jnp.concatenate([before, shard, after], axis=dim)
    return shard


def advance(padded, velocity, diffusion):
    spec_pad = ((0, 0),) * (padded.ndim - 1) + ((1, 1),)
    col_padded = jnp.pad(padded, spec_pad)
    centre = col_padded[..., 1:-1, 1:-1]
    north_cell = col_padded[..., :-2, 1:-1]
    south_cell = col_padded[..., 2:, 1:-1]
    west_cell = col_padded[..., 1:-1, :-2]
    east_cell = col_padded[..., 1:-1, 2:]
    along_col = velocity[0]
    along_row = velocity[1]
    spread = north_cell + south_cell + west_cell + east_cell - 4.0 * centre
    carried = (
        jnp.maximum(along_col, 0.0) * (centre - west_cell)
        + jnp.minimum(along_col, 0.0) * (east_cell - centre)
        + jnp.maximum(along_row, 0.0) * (centre - north_cell)
        + jnp.minimum(along_row, 0.0) * (south_cell - centre)
    )
    return centre + diffusion[:, None, None] * spread - carried


def gaspari(dist_sq):
    scaled = jnp.sqrt(dist_sq) / LOC_HALF
    clipped = jnp.maximum(scaled, 1.0)
    inner_part = (
        ((-0.25 * scaled + 0.5) * scaled + 0.625) * scaled - 5.0 / 3.0
    ) * scaled * scaled + 1.0
    outer_part = (
        ((((scaled / 12.0 - 0.5) * scaled + 0.625) * scaled + 5.0 / 3.0) * scaled - 5.0) * scaled
        + 4.0
        - 2.0 / (3.0 * clipped)
    )
    return jnp.where(scaled <= 1.0, inner_part, jnp.where(scaled <= 2.0, outer_part, 0.0))


def decode(flat_cells, total_rows, n_cols):
    field_ids = flat_cells // (total_rows * n_cols)
    row_ids = flat_cells // n_cols % total_rows
    col_ids = flat_cells % n_cols
    return (field_ids, row_ids, col_ids)


def innovations(priors, obs_values, obs_noise):
    members = priors.shape[0]
    average = jnp.mean(priors, axis=0)
    anomaly = priors - average
    spread = jnp.sum(anomaly * anomaly, axis=0) / (members - 1)
    variance_sum = spread + obs_noise
    root_sum = jnp.sqrt(variance_sum)
    shrink = 1.0 / (root_sum * (jnp.sqrt(obs_noise) + root_sum))
    adjust = (obs_values - average) / variance_sum - shrink * anomaly
    return (anomaly, adjust)


def regress(
    ensemble_now, base_row, obs_field, obs_row, obs_col, anomaly, adjust, field_mask, n_cols
):
    members, n_cells = ensemble_now.shape
    n_fields = field_mask.shape[0]
    per_field = n_cells // n_fields
    local_ids = lax.iota(jnp.int32, per_field)
    cell_row = (base_row + local_ids // n_cols).astype(jnp.float32)
    cell_col = (local_ids % n_cols).astype(jnp.float32)
    centred = ensemble_now - jnp.mean(ensemble_now, axis=0)
    mask_float = field_mask.astype(jnp.float32)
    total_obs = obs_field.shape[0]
    obs_block = min(256, total_obs)
    increment = jnp.zeros_like(ensemble_now)
    for offset in range(0, total_obs, obs_block):
        row_gap = cell_row[:, None] - obs_row[None, offset : offset + obs_block].astype(jnp.float32)
        col_gap = cell_col[:, None] - obs_col[None, offset : offset + obs_block].astype(jnp.float32)
        closeness = gaspari(row_gap * row_gap + col_gap * col_gap)
        field_hot = (
            obs_field[None, offset : offset + obs_block] == lax.iota(jnp.int32, n_fields)[:, None]
        ).astype(jnp.float32)
        allowed = jnp.dot(mask_float, field_hot, precision=precise)
        covariance = lax.dot_general(
            centred,
            anomaly[:, offset : offset + obs_block],
            (((0,), (0,)), ((), ())),
            precision=precise,
        )
        weights = (
            covariance.reshape(n_fields, per_field, obs_block)
            * (closeness[None] * allowed[:, None, :])
            / (members - 1)
        )
        increment = increment + lax.dot_general(
            adjust[:, offset : offset + obs_block],
            weights.reshape(n_cells, obs_block),
            (((1,), (1,)), ((), ())),
            precision=precise,
        )
    return ensemble_now + increment


LANES = 128
MEGA = 1 << 20


def split_two(x):
    high = x.astype(jnp.bfloat16)
    low = (x - high.astype(jnp.float32)).astype(jnp.bfloat16)
    return high, low


def split_three(x):
    high = x.astype(jnp.bfloat16)
    rest = x - high.astype(jnp.float32)
    mid = rest.astype(jnp.bfloat16)
    low = (rest - mid.astype(jnp.float32)).astype(jnp.bfloat16)
    return high, mid, low


def bdot(a, b):
    return jnp.dot(a, b, preferred_element_type=jnp.float32)


def log2(n):
    return n.bit_length() - 1


def start_copies(pairs, sems):
    copies = [pltpu.make_async_copy(src, dst, sems.at[i]) for i, (src, dst) in enumerate(pairs)]
    for copy in copies:
        copy.start()
    return copies


def finish(copies):
    for copy in copies:
        copy.wait()


def half_turn(x):
    half = x.shape[0] // 2
    return jnp.concatenate([x[half:], x[:half]], axis=0)


def prep_kernel(
    order_hbm, cell_hbm, value_hbm, var_hbm, mask_hbm, diffusion_hbm, stack_hbm, velocity_hbm,
    info_ref, own_ref, vel_ref, kappa_ref,
    order_buf, cell_buf, value_buf, var_buf, mask_buf, diffusion_buf, sems,
    *, total_rows, n_cols,
):
    copies = start_copies(
        [
            (order_hbm, order_buf), (cell_hbm, cell_buf), (value_hbm, value_buf), (var_hbm, var_buf),
            (mask_hbm, mask_buf), (diffusion_hbm, diffusion_buf), (velocity_hbm, vel_ref),
            (stack_hbm, own_ref),
        ],
        sems,
    )
    finish(copies[:4])
    table_rows = cell_buf.shape[0]
    n_fields = mask_buf.shape[0]
    order = order_buf[...]
    n_obs = order.shape[1]
    table = jnp.concatenate(
        [cell_buf[...].astype(jnp.float32), value_buf[...], var_buf[...]], axis=0
    )
    parts = jnp.concatenate(split_three(table), axis=0)
    lane_hot = (
        lax.broadcasted_iota(jnp.int32, (LANES, n_obs), 0) == (order & (LANES - 1))
    ).astype(jnp.float32).astype(jnp.bfloat16)
    found = bdot(parts, lane_hot)
    size = 3 * table_rows
    found = (found[:size] + found[size : 2 * size]) + found[2 * size :]
    row_hot = lax.broadcasted_iota(jnp.int32, (table_rows, n_obs), 0) == (order >> log2(LANES))

    def take(i):
        rows = found[i * table_rows : (i + 1) * table_rows]
        return jnp.sum(jnp.where(row_hot, rows, 0.0), axis=0, keepdims=True)

    cell = take(0).astype(jnp.int32)
    strip = cell >> log2(n_cols)
    field = strip >> log2(total_rows)
    row = strip & (total_rows - 1)
    col = cell & (n_cols - 1)
    as_float = lambda x: x.astype(jnp.float32)
    zero = jnp.zeros((1, n_obs), jnp.float32)
    finish(copies[4:])
    for f in range(n_fields):
        kappa_ref[f : f + 1, :] = jnp.full((1, LANES), diffusion_buf[0, f], jnp.float32)
    up = lax.broadcasted_iota(jnp.int32, (8, 8), 0)
    along = lax.broadcasted_iota(jnp.int32, (8, 8), 1)
    mask = jnp.zeros((8, 8), jnp.float32)
    for f in range(n_fields):
        for b in range(n_fields):
            mask = jnp.where((up == f) & (along == b), as_float(mask_buf[f, b]), mask)
    field_hot = as_float(lax.broadcasted_iota(jnp.int32, (8, n_obs), 0) == field)
    info = jnp.concatenate(
        [
            as_float(field), as_float(row), as_float(col), take(1), take(2), as_float(strip), zero, zero,
            bdot(mask.astype(jnp.bfloat16), field_hot.astype(jnp.bfloat16)),
        ],
        axis=0,
    )
    info_ref[...] = info


def forecast_kernel(
    place_ref, kappa_ref, own_ref, other_ref, vel_own_ref, vel_other_ref, info_ref,
    send_ref, field_buf, prior_buf,
):
    n_fields, n_rows, n_cols = field_buf.shape
    half = n_rows // 2
    n_dest = half
    chunk = send_ref.shape[0] // n_dest
    first_slab = place_ref[0:1, 0:1] < 0.5

    def whole_of(own, other):
        return jnp.concatenate([jnp.where(first_slab, own, other), jnp.where(first_slab, other, own)], axis=0)

    u = whole_of(vel_own_ref[0], vel_other_ref[0])
    v = whole_of(vel_own_ref[1], vel_other_ref[1])
    row = lax.broadcasted_iota(jnp.int32, (n_rows, n_cols), 0)
    col = lax.broadcasted_iota(jnp.int32, (n_rows, n_cols), 1)
    u_pos, u_neg = jnp.maximum(u, 0.0), jnp.minimum(u, 0.0)
    v_pos, v_neg = jnp.maximum(v, 0.0), jnp.minimum(v, 0.0)
    outflow = (u_neg - u_pos) + (v_neg - v_pos)
    cells, weights = [], []
    for f in range(n_fields):
        kappa = kappa_ref[f : f + 1, 0:1]
        weights.append((
            (1.0 - 4.0 * kappa) + outflow,
            jnp.where(row == 0, 0.0, kappa + v_pos),
            jnp.where(row == n_rows - 1, 0.0, kappa - v_neg),
            jnp.where(col == 0, 0.0, kappa + u_pos),
            jnp.where(col == n_cols - 1, 0.0, kappa - u_neg),
        ))
        cells.append(whole_of(own_ref[0, f], other_ref[0, f]))
    for _ in range(SUBSTEPS):
        for f in range(n_fields):
            c = cells[f]
            k_c, k_n, k_s, k_w, k_e = weights[f]
            cells[f] = (
                (c * k_c + pltpu.roll(c, 1, 0) * k_n)
                + (pltpu.roll(c, n_rows - 1, 0) * k_s + pltpu.roll(c, 1, 1) * k_w)
                + pltpu.roll(c, n_cols - 1, 1) * k_e
            )
    for f in range(n_fields):
        field_buf[f] = cells[f]
    whole = field_buf[...].reshape(n_fields * n_rows, n_cols)
    strips = n_fields * n_rows
    parts = jnp.concatenate(split_three(whole), axis=0)
    n_obs = info_ref.shape[1]
    width = 2 * LANES
    strip_ids = lax.broadcasted_iota(jnp.int32, (strips, width), 0)
    col_ids = lax.broadcasted_iota(jnp.int32, (n_cols, width), 0)
    for q in range(n_obs // width):
        cols = info_ref[2:3, q * width : (q + 1) * width].astype(jnp.int32)
        strip = info_ref[5:6, q * width : (q + 1) * width].astype(jnp.int32)
        hot = (col_ids == cols).astype(jnp.float32).astype(jnp.bfloat16)
        found = bdot(parts, hot)
        found = (found[:strips] + found[strips : 2 * strips]) + found[2 * strips :]
        values = jnp.sum(jnp.where(strip_ids == strip, found, 0.0), axis=0, keepdims=True)
        for h in range(width // LANES):
            at = q * (width // LANES) + h
            prior_buf[at : at + 1, :] = values[:, h * LANES : (h + 1) * LANES]
    priors = prior_buf[...]
    lead = chunk - n_obs // LANES
    for d in range(n_dest):
        send_ref[d * chunk + lead : (d + 1) * chunk, :] = priors
    pieces = n_cols // LANES
    for f in range(n_fields):
        rows = half_turn(jnp.where(first_slab, field_buf[f, :half, :], field_buf[f, half:, :]))
        for h in range(pieces):
            send_ref[pl.ds(f * pieces + h, n_dest, stride=chunk), :] = rows[
                :, h * LANES : (h + 1) * LANES
            ]
    for i in range(n_fields * pieces, lead):
        send_ref[pl.ds(i, n_dest, stride=chunk), :] = jnp.zeros((n_dest, LANES), jnp.float32)


def closeness_of(dist_sq):
    inverse = lax.rsqrt(jnp.maximum(dist_sq, 1e-6))
    z = dist_sq * inverse
    half_sq = 0.5 * dist_sq
    inner = 1.0 + dist_sq * ((half_sq - 5.0 / 3.0) + z * (0.625 - 0.5 * half_sq))
    left = jnp.maximum(2.0 - z, 0.0)
    left = left * left
    left = left * left
    outer = left * ((dist_sq + (z + z)) - 0.5) * (inverse * (1.0 / 12.0))
    return jnp.where(dist_sq <= 1.0, inner, outer)


def loc_kernel(
    place_ref, info_ref, pair_hi_ref, pair_lo_ref, rest_hbm, cell_hi_hbm, cell_lo_hbm,
    infot_ref, rest_ref, cell_hi_ref, cell_lo_ref, gap_buf, sems,
):
    n_obs = info_ref.shape[1]
    batch, n_pair = pair_hi_ref.shape
    n_cols = cell_hi_ref.shape[1]
    scale = 1.0 / LOC_HALF
    far = 32.0 * LOC_HALF * LOC_HALF
    row, col = info_ref[1:2, :], info_ref[2:3, :]
    norm = [part.astype(jnp.float32) for part in split_three(row * row + col * col)]
    one = jnp.ones((1, n_obs), jnp.float32)
    hot = lax.broadcasted_iota(jnp.int32, (8, n_obs), 0) == info_ref[0:1, :].astype(jnp.int32)
    zeros = jnp.zeros((6, n_obs), jnp.float32)
    feature_k = jnp.concatenate(
        norm + [one, one, one, -2.0 * row, -2.0 * col, -far * info_ref[8:16, :], one * far, row, zeros], axis=0
    )
    feature_j = jnp.concatenate(
        [one, one, one] + norm + [row, col, hot.astype(jnp.float32), one], axis=0
    )[:, batch:]
    infot_ref[...] = feature_k.T
    terms = feature_j.shape[0]
    gap_buf[...] = bdot(
        infot_ref[0:batch, 0:terms].astype(jnp.bfloat16), (feature_j * (scale * scale)).astype(jnp.bfloat16)
    )
    table_rows = 32
    own_row = place_ref[1:2, 0:1]
    gap_row = (lax.broadcasted_iota(jnp.int32, (table_rows, LANES), 0).astype(jnp.float32) - own_row) * scale
    gap_col = lax.broadcasted_iota(jnp.int32, (table_rows, LANES), 1).astype(jnp.float32) * scale
    high, mid, low = split_three(closeness_of(gap_row * gap_row + gap_col * gap_col))
    row_ids = lax.broadcasted_iota(jnp.int32, (1, table_rows), 1)
    copies = []
    col_at, row_at = 7, terms
    for b in range(BATCHES):
        span = slice(b * batch, (b + 1) * batch)
        rows = infot_ref[span, row_at : row_at + 1].astype(jnp.int32)
        hot = (row_ids == rows).astype(jnp.float32).astype(jnp.bfloat16)
        table = (bdot(hot, high) + bdot(hot, mid)) + bdot(hot, low)
        cols = infot_ref[span, col_at : col_at + 1] * -0.5
        col_k = jnp.broadcast_to(cols, (batch, LANES)).astype(jnp.int32)
        for h in range(n_cols // LANES):
            here = slice(h * LANES, (h + 1) * LANES)
            col = lax.broadcasted_iota(jnp.int32, (batch, LANES), 1) + h * LANES
            gap = jnp.minimum(jnp.abs(col - col_k), LANES - 1)
            at_hi, at_lo = split_two(jnp.take_along_axis(table, gap, axis=1))
            cell_hi_ref[span, here] = at_hi
            cell_lo_ref[span, here] = at_lo
        copies += start_copies(
            [
                (cell_hi_ref.at[span, :], cell_hi_hbm.at[span, :]),
                (cell_lo_ref.at[span, :], cell_lo_hbm.at[span, :]),
            ],
            sems.at[2 * b :],
        )
    step = 128
    kept = pair_lo_ref.shape[0]

    def pair_rows(low_ref, first):
        def body(i, carry):
            to = pl.multiple_of(i * step, step)
            at = pl.multiple_of(first + i * step, step)
            for h in range(n_pair // LANES):
                here = slice(h * LANES, (h + 1) * LANES)
                high, low = split_two(closeness_of(gap_buf[pl.ds(at, step), here]))
                pair_hi_ref[pl.ds(at, step), here] = high
                low_ref[pl.ds(to, step), here] = low
            return carry

        lax.fori_loop(0, low_ref.shape[0] // step, body, 0)

    pair_rows(rest_ref, kept)
    copies += start_copies([(rest_ref, rest_hbm)], sems.at[2 * BATCHES :])
    pair_rows(pair_lo_ref, 0)
    finish(copies)


def member_roll(x, shift):
    shift = shift % x.shape[0]
    return pltpu.roll(x, shift, 0) if shift else x


def factors(priors, value, var):
    members = priors.shape[0]
    average = jnp.sum(priors, axis=0, keepdims=True) * (1.0 / members)
    anomaly = priors - average
    variance = jnp.sum(anomaly * anomaly, axis=0, keepdims=True) * (1.0 / (members - 1)) + var
    root = jnp.sqrt(variance)
    shrunk = anomaly * (1.0 / ((members - 1) * (root * (jnp.sqrt(var) + root))))
    rows = [shrunk * member_roll(anomaly, -d) for d in range(members // 2)]
    rows.append(anomaly * ((value - average) / ((members - 1) * variance)))
    return rows


def combined(state, sums):
    members = state.shape[0]
    half = members // 2
    centred = state - jnp.sum(state, axis=0, keepdims=True) * (1.0 / members)
    block = lambda d: sums[d * members : (d + 1) * members]
    across = member_roll(centred, half)
    move = (centred - across) * block(0)
    for d in range(1, half):
        move = move + (member_roll(centred, -d) - across) * block(d)
        move = move + member_roll((centred - member_roll(across, -d)) * block(d), d)
    shift = jnp.sum(centred * block(half), axis=0, keepdims=True)
    return state + (shift - move)


def update_kernel(
    recv_ref, info_ref, pair_hi_ref, pair_lo_ref, rest_hbm, cell_hi_hbm, cell_lo_hbm,
    out_ref, fac_buf, sums_buf, mask_buf, rest_ref, cell_hi_ref, cell_lo_ref, sems, *, members, n_fields,
):
    tables = [(rest_hbm, rest_ref), (cell_hi_hbm, cell_hi_ref), (cell_lo_hbm, cell_lo_ref)]
    copies = [pltpu.make_async_copy(src, dst, sems.at[i]) for i, (src, dst) in enumerate(tables)]
    n_obs = info_ref.shape[1]
    batch = n_obs // BATCHES
    chunk = recv_ref.shape[0] // members
    per_chunk = n_obs // LANES
    lead = chunk - per_chunk
    pieces = cell_hi_ref.shape[1] // LANES
    size = fac_buf.shape[1] // 2
    kept = pair_lo_ref.shape[0]

    def member_row(i):
        return recv_ref[pl.ds(i, members, stride=chunk), :]

    def priors_of(b):
        first = lead + b * (per_chunk // BATCHES)
        return jnp.concatenate([member_row(first + q) for q in range(per_chunk // BATCHES)], axis=1)

    def set_factors(b, priors):
        span = slice(b * batch, (b + 1) * batch)
        rows = factors(priors, info_ref[3:4, span], info_ref[4:5, span])
        for i, r in enumerate(rows):
            high, low = split_two(r)
            fac_buf[b, i * members : (i + 1) * members, :] = high
            fac_buf[b, size + i * members : size + (i + 1) * members, :] = low

    def run(step, carry):
        @pl.when(step == 0)
        def _():
            for copy in copies:
                copy.start()
            set_factors(0, priors_of(0))
            first = bdot(fac_buf[0], pair_hi_ref[...])
            sums_buf[...] = (first[:size] + first[size:]) + bdot(fac_buf[0, :size, :kept], pair_lo_ref[...])

        @pl.when(step == 1)
        def _():
            finish(copies[:1])
            sums = sums_buf[...] + bdot(fac_buf[0, :size, kept:], rest_ref[...])
            set_factors(1, combined(priors_of(1), sums))

        @pl.when(step == 2)
        def _():
            finish(copies[1:])
            states = [
                jnp.concatenate([member_row(f * pieces + h) for h in range(pieces)], axis=1)
                for f in range(n_fields)
            ]
            all_rows = n_fields * size
            for b in range(BATCHES):
                span = slice(b * batch, (b + 1) * batch)
                for f in range(n_fields):
                    open_to = info_ref[8 + f : 9 + f, span].astype(jnp.bfloat16)
                    mask_buf[f * size : (f + 1) * size, :] = fac_buf[b, :size, :] * open_to
                    mask_buf[all_rows + f * size : all_rows + (f + 1) * size, :] = fac_buf[b, size:, :] * open_to
                first = bdot(mask_buf[...], cell_hi_ref[span, :])
                sums = (first[:all_rows] + first[all_rows:]) + bdot(mask_buf[:all_rows, :], cell_lo_ref[span, :])
                states = [combined(state, sums[f * size : (f + 1) * size]) for f, state in enumerate(states)]
            for f in range(n_fields):
                out_ref[:, f, 0, 0, :] = half_turn(states[f])

        return carry

    lax.fori_loop(0, 3, run, 0)


def vmem_spec():
    return pl.BlockSpec(memory_space=pltpu.VMEM)


def smem_spec():
    return pl.BlockSpec(memory_space=pltpu.SMEM)


def hbm_spec():
    return pl.BlockSpec(memory_space=pltpu.HBM)


def in_hbm(x):
    return pltpu.with_memory_space_constraint(x, pltpu.HBM)


def quick_device(
    realization_stack, velocity, diffusion, obs_cell, obs_order, obs_value, obs_var, field_mask
):
    _, n_fields, rows_here, n_cols = realization_stack.shape
    n_mem = lax.axis_size("mem")
    total_rows = 2 * rows_here
    n_obs = obs_cell.shape[0]
    batch = n_obs // BATCHES
    slab_index = lax.axis_index("row")
    own_row = slab_index * rows_here + lax.axis_index("mem")
    place = jnp.where(
        lax.broadcasted_iota(jnp.int32, (8, LANES), 0) == 0, slab_index, own_row
    ).astype(jnp.float32)
    params = pltpu.CompilerParams(vmem_limit_bytes=16 * MEGA)
    shape = jax.ShapeDtypeStruct
    f32, i32 = jnp.float32, jnp.int32
    swap = [(0, 1), (1, 0)]
    other = lax.ppermute(realization_stack, "row", swap)
    vel_other = lax.ppermute(velocity, "row", swap)
    table = (n_obs // LANES, LANES)
    info, own, vel_own, kappa = pl.pallas_call(
        functools.partial(prep_kernel, total_rows=total_rows, n_cols=n_cols),
        out_shape=(
            shape((16, n_obs), f32),
            shape(realization_stack.shape, f32),
            shape(velocity.shape, f32),
            shape((8, LANES), f32),
        ),
        in_specs=[hbm_spec()] * 8,
        out_specs=(vmem_spec(),) * 4,
        scratch_shapes=[
            pltpu.VMEM((1, n_obs), i32),
            pltpu.VMEM(table, i32),
            pltpu.VMEM(table, f32),
            pltpu.VMEM(table, f32),
            pltpu.SMEM(field_mask.shape, i32),
            pltpu.SMEM((1, n_fields), f32),
            pltpu.SemaphoreType.DMA((8,)),
        ],
        compiler_params=params,
        name="prep",
    )(
        in_hbm(obs_order.reshape(1, n_obs)),
        in_hbm(obs_cell.reshape(table)),
        in_hbm(obs_value.reshape(table)),
        in_hbm(obs_var.reshape(table)),
        in_hbm(field_mask),
        in_hbm(diffusion.reshape(1, n_fields)),
        in_hbm(realization_stack),
        in_hbm(velocity),
    )
    chunk = (n_fields * n_cols + n_obs) // LANES
    send = pl.pallas_call(
        forecast_kernel,
        out_shape=shape((n_mem * chunk, LANES), f32),
        in_specs=[vmem_spec()] * 7,
        out_specs=vmem_spec(),
        scratch_shapes=[
            pltpu.VMEM((n_fields, total_rows, n_cols), f32),
            pltpu.VMEM((n_obs // LANES, LANES), f32),
        ],
        compiler_params=params,
        name="forecast",
    )(place, kappa, own, other, vel_own, vel_other, info)
    recv = lax.all_to_all(
        send.reshape(n_mem, chunk, 1, LANES),
        "mem",
        split_axis=0,
        concat_axis=0,
        axis_index_groups=[[(i + n_mem // 2) % n_mem for i in range(n_mem)]],
        tiled=True,
    ).reshape(send.shape)
    n_pair = n_obs - batch
    bf16 = jnp.bfloat16
    kept = batch // 2
    pair_hi, pair_lo, rest, cell_hi, cell_lo = pl.pallas_call(
        loc_kernel,
        out_shape=(
            shape((batch, n_pair), bf16),
            shape((kept, n_pair), bf16),
            pltpu.HBM((batch - kept, n_pair), bf16),
            pltpu.HBM((n_obs, n_cols), bf16),
            pltpu.HBM((n_obs, n_cols), bf16),
        ),
        in_specs=[vmem_spec(), vmem_spec()],
        out_specs=(vmem_spec(), vmem_spec(), hbm_spec(), hbm_spec(), hbm_spec()),
        scratch_shapes=[
            pltpu.VMEM((n_obs, 24), f32),
            pltpu.VMEM((batch - kept, n_pair), bf16),
            pltpu.VMEM((n_obs, n_cols), bf16),
            pltpu.VMEM((n_obs, n_cols), bf16),
            pltpu.VMEM((batch, n_pair), f32),
            pltpu.SemaphoreType.DMA((2 * BATCHES + 1,)),
        ],
        compiler_params=params,
        name="localize",
    )(place, info)
    rows = n_mem * (n_mem // 2 + 1)
    return pl.pallas_call(
        functools.partial(update_kernel, members=n_mem, n_fields=n_fields),
        out_shape=shape((n_mem, n_fields, 1, 1, n_cols), f32),
        in_specs=[vmem_spec()] * 4 + [hbm_spec()] * 3,
        out_specs=vmem_spec(),
        scratch_shapes=[
            pltpu.VMEM((BATCHES, 2 * rows, batch), bf16),
            pltpu.VMEM((rows, n_pair), f32),
            pltpu.VMEM((2 * rows * n_fields, batch), bf16),
            pltpu.VMEM((batch - kept, n_pair), bf16),
            pltpu.VMEM((n_obs, n_cols), bf16),
            pltpu.VMEM((n_obs, n_cols), bf16),
            pltpu.SemaphoreType.DMA((3,)),
        ],
        compiler_params=params,
        name="update",
    )(recv, info, pair_hi, pair_lo, in_hbm(rest), in_hbm(cell_hi), in_hbm(cell_lo))


def is_quick(realization_stack, obs_cell, n_mem, n_slab):
    local_members, n_fields, rows_here, n_cols = realization_stack.shape
    powers = all(n & (n - 1) == 0 for n in (rows_here, n_cols))
    return (
        n_slab == 2
        and local_members == 1
        and n_mem == rows_here == 16
        and n_fields <= 8
        and LOC_HALF * 2 <= LANES - 1
        and powers
        and n_cols % LANES == 0
        and obs_cell.shape[0] == 8 * n_cols
        and BATCHES == 2
    )


def per_device(
    realization_stack, velocity, diffusion, obs_cell, obs_order, obs_value, obs_var, field_mask
):
    local_members = realization_stack.shape[0]
    n_fields = realization_stack.shape[1]
    rows_here = realization_stack.shape[2]
    n_cols = realization_stack.shape[3]
    n_mem = lax.axis_size("mem")
    n_slab = lax.axis_size("row")
    total_members = local_members * n_mem
    total_rows = rows_here * n_slab
    if is_quick(realization_stack, obs_cell, n_mem, n_slab):
        return quick_device(
            realization_stack, velocity, diffusion, obs_cell, obs_order, obs_value, obs_var, field_mask
        )
    slab_index = lax.axis_index("row")
    member_index = lax.axis_index("mem")
    row_sub = rows_here // n_mem
    current = realization_stack
    for substep in range(SUBSTEPS):
        padded = extended(current, (("row", 2),), 1)
        current = advance(padded, velocity, diffusion)
    field_all, row_all, col_all = decode(obs_cell, total_rows, n_cols)
    batch_size = obs_cell.shape[0] // BATCHES
    layout = lax.all_to_all(current, "mem", split_axis=2, concat_axis=0, tiled=True)
    ensemble_now = layout.reshape(total_members, -1)
    base_row = slab_index * rows_here + member_index * row_sub
    for batch_num in range(BATCHES):
        picked = obs_order[batch_num * batch_size : (batch_num + 1) * batch_size]
        obs_field = field_all[picked]
        obs_row = row_all[picked]
        obs_col = col_all[picked]
        owned = ((obs_row >= base_row) & (obs_row < base_row + row_sub)).astype(jnp.float32)
        local_ids = (
            obs_field * row_sub * n_cols
            + jnp.clip(obs_row - base_row, 0, row_sub - 1) * n_cols
            + obs_col
        )
        partial_priors = jnp.take(ensemble_now, local_ids, axis=1) * owned[None, :]
        priors = lax.psum(partial_priors, ("mem", "row"))
        anomaly, adjust = innovations(priors, obs_value[picked], obs_var[picked])
        ensemble_now = regress(
            ensemble_now, base_row, obs_field, obs_row, obs_col, anomaly, adjust, field_mask, n_cols
        )
    return ensemble_now.reshape(total_members, n_fields, 1, row_sub, n_cols)


def solution(mesh):
    in_specs = (P("mem", None, "row", None), P(None, "row", None), P(), P(), P(), P(), P(), P())
    out_specs = P(None, None, "row", "mem", None)
    return jax.shard_map(
        per_device, mesh=mesh, in_specs=in_specs, out_specs=out_specs, check_vma=False
    )
```

```python
import functools

import jax
import jax.numpy as jnp
from jax import lax
from jax.experimental import pallas as pl
from jax.experimental.pallas import tpu as pltpu
from jax.sharding import PartitionSpec as P

SUBSTEPS = 4
BATCHES = 2
LOC_HALF = 32


precise = lax.Precision.HIGHEST


def extended(shard, sides, width):
    for axis, dim in sides:
        count, length = (lax.axis_size(axis), shard.shape[dim])
        up = [(i, (i + 1) % count) for i in range(count - 1)]
        down = [(j, i) for i, j in up]
        last = lax.slice_in_dim(shard, length - width, length, axis=dim)
        initial = lax.slice_in_dim(shard, 0, width, axis=dim)
        before = lax.ppermute(last, axis, up)
        after = lax.ppermute(initial, axis, down)
        shard = jnp.concatenate([before, shard, after], axis=dim)
    return shard


def advance(padded, velocity, diffusion):
    spec_pad = ((0, 0),) * (padded.ndim - 1) + ((1, 1),)
    col_padded = jnp.pad(padded, spec_pad)
    centre = col_padded[..., 1:-1, 1:-1]
    north_cell = col_padded[..., :-2, 1:-1]
    south_cell = col_padded[..., 2:, 1:-1]
    west_cell = col_padded[..., 1:-1, :-2]
    east_cell = col_padded[..., 1:-1, 2:]
    along_col = velocity[0]
    along_row = velocity[1]
    spread = north_cell + south_cell + west_cell + east_cell - 4.0 * centre
    carried = (
        jnp.maximum(along_col, 0.0) * (centre - west_cell)
        + jnp.minimum(along_col, 0.0) * (east_cell - centre)
        + jnp.maximum(along_row, 0.0) * (centre - north_cell)
        + jnp.minimum(along_row, 0.0) * (south_cell - centre)
    )
    return centre + diffusion[:, None, None] * spread - carried


def gaspari(dist_sq):
    scaled = jnp.sqrt(dist_sq) / LOC_HALF
    clipped = jnp.maximum(scaled, 1.0)
    inner_part = (
        ((-0.25 * scaled + 0.5) * scaled + 0.625) * scaled - 5.0 / 3.0
    ) * scaled * scaled + 1.0
    outer_part = (
        ((((scaled / 12.0 - 0.5) * scaled + 0.625) * scaled + 5.0 / 3.0) * scaled - 5.0) * scaled
        + 4.0
        - 2.0 / (3.0 * clipped)
    )
    return jnp.where(scaled <= 1.0, inner_part, jnp.where(scaled <= 2.0, outer_part, 0.0))


def decode(flat_cells, total_rows, n_cols):
    field_ids = flat_cells // (total_rows * n_cols)
    row_ids = flat_cells // n_cols % total_rows
    col_ids = flat_cells % n_cols
    return (field_ids, row_ids, col_ids)


def innovations(priors, obs_values, obs_noise):
    members = priors.shape[0]
    average = jnp.mean(priors, axis=0)
    anomaly = priors - average
    spread = jnp.sum(anomaly * anomaly, axis=0) / (members - 1)
    variance_sum = spread + obs_noise
    root_sum = jnp.sqrt(variance_sum)
    shrink = 1.0 / (root_sum * (jnp.sqrt(obs_noise) + root_sum))
    adjust = (obs_values - average) / variance_sum - shrink * anomaly
    return (anomaly, adjust)


def regress(
    ensemble_now, base_row, obs_field, obs_row, obs_col, anomaly, adjust, field_mask, n_cols
):
    members, n_cells = ensemble_now.shape
    n_fields = field_mask.shape[0]
    per_field = n_cells // n_fields
    local_ids = lax.iota(jnp.int32, per_field)
    cell_row = (base_row + local_ids // n_cols).astype(jnp.float32)
    cell_col = (local_ids % n_cols).astype(jnp.float32)
    centred = ensemble_now - jnp.mean(ensemble_now, axis=0)
    mask_float = field_mask.astype(jnp.float32)
    total_obs = obs_field.shape[0]
    obs_block = min(256, total_obs)
    increment = jnp.zeros_like(ensemble_now)
    for offset in range(0, total_obs, obs_block):
        row_gap = cell_row[:, None] - obs_row[None, offset : offset + obs_block].astype(jnp.float32)
        col_gap = cell_col[:, None] - obs_col[None, offset : offset + obs_block].astype(jnp.float32)
        closeness = gaspari(row_gap * row_gap + col_gap * col_gap)
        field_hot = (
            obs_field[None, offset : offset + obs_block] == lax.iota(jnp.int32, n_fields)[:, None]
        ).astype(jnp.float32)
        allowed = jnp.dot(mask_float, field_hot, precision=precise)
        covariance = lax.dot_general(
            centred,
            anomaly[:, offset : offset + obs_block],
            (((0,), (0,)), ((), ())),
            precision=precise,
        )
        weights = (
            covariance.reshape(n_fields, per_field, obs_block)
            * (closeness[None] * allowed[:, None, :])
            / (members - 1)
        )
        increment = increment + lax.dot_general(
            adjust[:, offset : offset + obs_block],
            weights.reshape(n_cells, obs_block),
            (((1,), (1,)), ((), ())),
            precision=precise,
        )
    return ensemble_now + increment


LANES = 128
MEGA = 1 << 20


def split_two(x):
    high = x.astype(jnp.bfloat16)
    low = (x - high.astype(jnp.float32)).astype(jnp.bfloat16)
    return high, low


def split_three(x):
    high = x.astype(jnp.bfloat16)
    rest = x - high.astype(jnp.float32)
    mid = rest.astype(jnp.bfloat16)
    low = (rest - mid.astype(jnp.float32)).astype(jnp.bfloat16)
    return high, mid, low


def bdot(a, b):
    return jnp.dot(a, b, preferred_element_type=jnp.float32)


def log2(n):
    return n.bit_length() - 1


def start_copies(pairs, sems):
    copies = [pltpu.make_async_copy(src, dst, sems.at[i]) for i, (src, dst) in enumerate(pairs)]
    for copy in copies:
        copy.start()
    return copies


def finish(copies):
    for copy in copies:
        copy.wait()


def exchange_order(n):
    return [(n // 2 - 1 - i) % n for i in range(n)]


def prep_kernel(
    order_hbm, cell_hbm, value_hbm, var_hbm, mask_hbm, diffusion_hbm, stack_hbm, velocity_hbm,
    info_ref, own_ref, vel_ref, kappa_ref,
    order_buf, cell_buf, value_buf, var_buf, mask_buf, diffusion_buf, sems,
    *, total_rows, n_cols,
):
    copies = start_copies(
        [
            (order_hbm, order_buf), (cell_hbm, cell_buf), (value_hbm, value_buf), (var_hbm, var_buf),
            (mask_hbm, mask_buf), (diffusion_hbm, diffusion_buf), (velocity_hbm, vel_ref),
            (stack_hbm, own_ref),
        ],
        sems,
    )
    finish(copies[:4])
    table_rows = cell_buf.shape[0]
    n_fields = mask_buf.shape[0]
    order = order_buf[...]
    n_obs = order.shape[1]
    table = jnp.concatenate(
        [cell_buf[...].astype(jnp.float32), value_buf[...], var_buf[...]], axis=0
    )
    parts = jnp.concatenate(split_three(table), axis=0)
    lane_hot = (
        lax.broadcasted_iota(jnp.int32, (LANES, n_obs), 0) == (order & (LANES - 1))
    ).astype(jnp.float32).astype(jnp.bfloat16)
    found = bdot(parts, lane_hot)
    size = 3 * table_rows
    found = (found[:size] + found[size : 2 * size]) + found[2 * size :]
    row_hot = lax.broadcasted_iota(jnp.int32, (table_rows, n_obs), 0) == (order >> log2(LANES))

    def take(i):
        rows = found[i * table_rows : (i + 1) * table_rows]
        return jnp.sum(jnp.where(row_hot, rows, 0.0), axis=0, keepdims=True)

    cell = take(0).astype(jnp.int32)
    strip = cell >> log2(n_cols)
    field = strip >> log2(total_rows)
    row = strip & (total_rows - 1)
    col = cell & (n_cols - 1)
    as_float = lambda x: x.astype(jnp.float32)
    zero = jnp.zeros((1, n_obs), jnp.float32)
    finish(copies[4:])
    for f in range(n_fields):
        kappa_ref[f : f + 1, :] = jnp.full((1, LANES), diffusion_buf[0, f], jnp.float32)
    up = lax.broadcasted_iota(jnp.int32, (8, 8), 0)
    along = lax.broadcasted_iota(jnp.int32, (8, 8), 1)
    mask = jnp.zeros((8, 8), jnp.float32)
    for f in range(n_fields):
        for b in range(n_fields):
            mask = jnp.where((up == f) & (along == b), as_float(mask_buf[f, b]), mask)
    field_hot = as_float(lax.broadcasted_iota(jnp.int32, (8, n_obs), 0) == field)
    info = jnp.concatenate(
        [
            as_float(field), as_float(row), as_float(col), take(1), take(2), as_float(strip), zero, zero,
            bdot(mask.astype(jnp.bfloat16), field_hot.astype(jnp.bfloat16)),
        ],
        axis=0,
    )
    info_ref[...] = info


def forecast_kernel(
    place_ref, kappa_ref, own_ref, other_ref, vel_own_ref, vel_other_ref, info_ref,
    send_ref, field_buf, prior_buf,
):
    n_fields, n_rows, n_cols = field_buf.shape
    half = n_rows // 2
    n_dest = half
    chunk = send_ref.shape[0] // n_dest
    first_slab = place_ref[0:1, 0:1] < 0.5

    def whole_of(own, other):
        return jnp.concatenate([jnp.where(first_slab, own, other), jnp.where(first_slab, other, own)], axis=0)

    u = whole_of(vel_own_ref[0], vel_other_ref[0])
    v = whole_of(vel_own_ref[1], vel_other_ref[1])
    row = lax.broadcasted_iota(jnp.int32, (n_rows, n_cols), 0)
    col = lax.broadcasted_iota(jnp.int32, (n_rows, n_cols), 1)
    u_pos, u_neg = jnp.maximum(u, 0.0), jnp.minimum(u, 0.0)
    v_pos, v_neg = jnp.maximum(v, 0.0), jnp.minimum(v, 0.0)
    outflow = (u_neg - u_pos) + (v_neg - v_pos)
    cells, weights = [], []
    for f in range(n_fields):
        kappa = kappa_ref[f : f + 1, 0:1]
        weights.append((
            (1.0 - 4.0 * kappa) + outflow,
            jnp.where(row == 0, 0.0, kappa + v_pos),
            jnp.where(row == n_rows - 1, 0.0, kappa - v_neg),
            jnp.where(col == 0, 0.0, kappa + u_pos),
            jnp.where(col == n_cols - 1, 0.0, kappa - u_neg),
        ))
        cells.append(whole_of(own_ref[0, f], other_ref[0, f]))
    for _ in range(SUBSTEPS):
        for f in range(n_fields):
            c = cells[f]
            k_c, k_n, k_s, k_w, k_e = weights[f]
            cells[f] = (
                (c * k_c + pltpu.roll(c, 1, 0) * k_n)
                + (pltpu.roll(c, n_rows - 1, 0) * k_s + pltpu.roll(c, 1, 1) * k_w)
                + pltpu.roll(c, n_cols - 1, 1) * k_e
            )
    for f in range(n_fields):
        field_buf[f] = cells[f]
    whole = field_buf[...].reshape(n_fields * n_rows, n_cols)
    strips = n_fields * n_rows
    parts = jnp.concatenate(split_three(whole), axis=0)
    n_obs = info_ref.shape[1]
    width = 2 * LANES
    strip_ids = lax.broadcasted_iota(jnp.int32, (strips, width), 0)
    col_ids = lax.broadcasted_iota(jnp.int32, (n_cols, width), 0)
    for q in range(n_obs // width):
        cols = info_ref[2:3, q * width : (q + 1) * width].astype(jnp.int32)
        strip = info_ref[5:6, q * width : (q + 1) * width].astype(jnp.int32)
        hot = (col_ids == cols).astype(jnp.float32).astype(jnp.bfloat16)
        found = bdot(parts, hot)
        found = (found[:strips] + found[strips : 2 * strips]) + found[2 * strips :]
        values = jnp.sum(jnp.where(strip_ids == strip, found, 0.0), axis=0, keepdims=True)
        for h in range(width // LANES):
            at = q * (width // LANES) + h
            prior_buf[at : at + 1, :] = values[:, h * LANES : (h + 1) * LANES]
    priors = prior_buf[...]
    lead = chunk - n_obs // LANES
    for d in range(n_dest):
        send_ref[d * chunk + lead : (d + 1) * chunk, :] = priors
    pieces = n_cols // LANES
    for f in range(n_fields):
        rows = jnp.where(first_slab, field_buf[f, :half, :], field_buf[f, half:, :])
        for i, dest in enumerate(exchange_order(n_dest)):
            for h in range(pieces):
                at = i * chunk + f * pieces + h
                send_ref[at : at + 1, :] = rows[dest : dest + 1, h * LANES : (h + 1) * LANES]
    for i in range(n_fields * pieces, lead):
        send_ref[pl.ds(i, n_dest, stride=chunk), :] = jnp.zeros((n_dest, LANES), jnp.float32)


def closeness_of(dist_sq):
    inverse = lax.rsqrt(jnp.maximum(dist_sq, 1e-6))
    z = dist_sq * inverse
    half_sq = 0.5 * dist_sq
    inner = 1.0 + dist_sq * ((half_sq - 5.0 / 3.0) + z * (0.625 - 0.5 * half_sq))
    left = jnp.maximum(2.0 - z, 0.0)
    left = left * left
    left = left * left
    outer = left * ((dist_sq + (z + z)) - 0.5) * (inverse * (1.0 / 12.0))
    return jnp.where(dist_sq <= 1.0, inner, outer)


def loc_kernel(
    place_ref, info_ref, pair_hi_ref, pair_lo_ref, rest_hbm, cell_hi_hbm, cell_lo_hbm,
    infot_ref, rest_ref, cell_hi_ref, cell_lo_ref, gap_buf, sems,
):
    n_obs = info_ref.shape[1]
    batch, n_pair = pair_hi_ref.shape
    n_cols = cell_hi_ref.shape[1]
    scale = 1.0 / LOC_HALF
    far = 32.0 * LOC_HALF * LOC_HALF
    row, col = info_ref[1:2, :], info_ref[2:3, :]
    norm = [part.astype(jnp.float32) for part in split_three(row * row + col * col)]
    one = jnp.ones((1, n_obs), jnp.float32)
    hot = lax.broadcasted_iota(jnp.int32, (8, n_obs), 0) == info_ref[0:1, :].astype(jnp.int32)
    zeros = jnp.zeros((6, n_obs), jnp.float32)
    feature_k = jnp.concatenate(
        norm + [one, one, one, -2.0 * row, -2.0 * col, -far * info_ref[8:16, :], one * far, row, zeros], axis=0
    )
    feature_j = jnp.concatenate(
        [one, one, one] + norm + [row, col, hot.astype(jnp.float32), one], axis=0
    )[:, batch:]
    infot_ref[...] = feature_k.T
    terms = feature_j.shape[0]
    gap_buf[...] = bdot(
        infot_ref[0:batch, 0:terms].astype(jnp.bfloat16), (feature_j * (scale * scale)).astype(jnp.bfloat16)
    )
    table_rows = 32
    own_row = place_ref[1:2, 0:1]
    gap_row = (lax.broadcasted_iota(jnp.int32, (table_rows, LANES), 0).astype(jnp.float32) - own_row) * scale
    gap_col = lax.broadcasted_iota(jnp.int32, (table_rows, LANES), 1).astype(jnp.float32) * scale
    by_row = jnp.concatenate(split_three(closeness_of(gap_row * gap_row + gap_col * gap_col)), axis=0)
    row_ids = lax.broadcasted_iota(jnp.int32, (1, 3 * table_rows), 1) & (table_rows - 1)
    copies = []
    col_at, row_at = 7, terms
    for b in range(BATCHES):
        span = slice(b * batch, (b + 1) * batch)
        rows = infot_ref[span, row_at : row_at + 1].astype(jnp.int32)
        hot = (row_ids == rows).astype(jnp.float32).astype(jnp.bfloat16)
        table = bdot(hot, by_row)
        cols = infot_ref[span, col_at : col_at + 1] * -0.5
        col_k = jnp.broadcast_to(cols, (batch, LANES)).astype(jnp.int32)
        for h in range(n_cols // LANES):
            here = slice(h * LANES, (h + 1) * LANES)
            col = lax.broadcasted_iota(jnp.int32, (batch, LANES), 1) + h * LANES
            gap = jnp.minimum(jnp.abs(col - col_k), LANES - 1)
            at_hi, at_lo = split_two(jnp.take_along_axis(table, gap, axis=1))
            cell_hi_ref[span, here] = at_hi
            cell_lo_ref[span, here] = at_lo
        copies += start_copies(
            [
                (cell_hi_ref.at[span, :], cell_hi_hbm.at[span, :]),
                (cell_lo_ref.at[span, :], cell_lo_hbm.at[span, :]),
            ],
            sems.at[2 * b :],
        )
    step = 128
    kept = pair_lo_ref.shape[0]

    def pair_rows(low_ref, first):
        def body(i, carry):
            to = pl.multiple_of(i * step, step)
            at = pl.multiple_of(first + i * step, step)
            for h in range(n_pair // LANES):
                here = slice(h * LANES, (h + 1) * LANES)
                high, low = split_two(closeness_of(gap_buf[pl.ds(at, step), here]))
                pair_hi_ref[pl.ds(at, step), here] = high
                low_ref[pl.ds(to, step), here] = low
            return carry

        lax.fori_loop(0, low_ref.shape[0] // step, body, 0)

    pair_rows(rest_ref, kept)
    copies += start_copies([(rest_ref, rest_hbm)], sems.at[2 * BATCHES :])
    pair_rows(pair_lo_ref, 0)
    finish(copies)


def member_roll(x, shift):
    shift = shift % x.shape[0]
    return pltpu.roll(x, shift, 0) if shift else x


def factors(priors, value, var):
    members = priors.shape[0]
    average = jnp.sum(priors, axis=0, keepdims=True) * (1.0 / members)
    anomaly = priors - average
    variance = jnp.sum(anomaly * anomaly, axis=0, keepdims=True) * (1.0 / (members - 1)) + var
    root = jnp.sqrt(variance)
    shrunk = anomaly * (1.0 / ((members - 1) * (root * (jnp.sqrt(var) + root))))
    rows = [shrunk * member_roll(anomaly, -d) for d in range(members // 2)]
    rows.append(anomaly * ((value - average) / ((members - 1) * variance)))
    return rows


def combined(state, sums):
    members = state.shape[0]
    half = members // 2
    centred = state - jnp.sum(state, axis=0, keepdims=True) * (1.0 / members)
    block = lambda d: sums[d * members : (d + 1) * members]
    across = member_roll(centred, half)
    move = (centred - across) * block(0)
    for d in range(1, half):
        move = move + (member_roll(centred, -d) - across) * block(d)
        move = move + member_roll((centred - member_roll(across, -d)) * block(d), d)
    shift = jnp.sum(centred * block(half), axis=0, keepdims=True)
    return state + (shift - move)


def update_kernel(
    recv_ref, info_ref, pair_hi_ref, pair_lo_ref, rest_hbm, cell_hi_hbm, cell_lo_hbm,
    out_ref, fac_buf, sums_buf, mask_buf, rest_ref, cell_hi_ref, cell_lo_ref, sems, *, members, n_fields,
):
    tables = [(rest_hbm, rest_ref), (cell_hi_hbm, cell_hi_ref), (cell_lo_hbm, cell_lo_ref)]
    copies = [pltpu.make_async_copy(src, dst, sems.at[i]) for i, (src, dst) in enumerate(tables)]
    n_obs = info_ref.shape[1]
    batch = n_obs // BATCHES
    chunk = recv_ref.shape[0] // members
    per_chunk = n_obs // LANES
    lead = chunk - per_chunk
    pieces = cell_hi_ref.shape[1] // LANES
    size = fac_buf.shape[1] // 2
    kept = pair_lo_ref.shape[0]

    def member_row(i):
        return recv_ref[pl.ds(i, members, stride=chunk), :]

    def priors_of(b):
        first = lead + b * (per_chunk // BATCHES)
        return jnp.concatenate([member_row(first + q) for q in range(per_chunk // BATCHES)], axis=1)

    def set_factors(b, priors):
        span = slice(b * batch, (b + 1) * batch)
        rows = factors(priors, info_ref[3:4, span], info_ref[4:5, span])
        for i, r in enumerate(rows):
            high, low = split_two(r)
            fac_buf[b, i * members : (i + 1) * members, :] = high
            fac_buf[b, size + i * members : size + (i + 1) * members, :] = low

    def run(step, carry):
        @pl.when(step == 0)
        def _():
            for copy in copies:
                copy.start()
            set_factors(0, priors_of(0))
            first = bdot(fac_buf[0], pair_hi_ref[...])
            sums_buf[...] = (first[:size] + first[size:]) + bdot(fac_buf[0, :size, :kept], pair_lo_ref[...])

        @pl.when(step == 1)
        def _():
            finish(copies[:1])
            sums = sums_buf[...] + bdot(fac_buf[0, :size, kept:], rest_ref[...])
            set_factors(1, combined(priors_of(1), sums))

        @pl.when(step == 2)
        def _():
            finish(copies[1:])
            states = [
                jnp.concatenate([member_row(f * pieces + h) for h in range(pieces)], axis=1)
                for f in range(n_fields)
            ]
            all_rows = n_fields * size
            for b in range(BATCHES):
                span = slice(b * batch, (b + 1) * batch)
                for f in range(n_fields):
                    open_to = info_ref[8 + f : 9 + f, span].astype(jnp.bfloat16)
                    mask_buf[f * size : (f + 1) * size, :] = fac_buf[b, :size, :] * open_to
                    mask_buf[all_rows + f * size : all_rows + (f + 1) * size, :] = fac_buf[b, size:, :] * open_to
                first = bdot(mask_buf[...], cell_hi_ref[span, :])
                sums = (first[:all_rows] + first[all_rows:]) + bdot(mask_buf[:all_rows, :], cell_lo_ref[span, :])
                states = [combined(state, sums[f * size : (f + 1) * size]) for f, state in enumerate(states)]
            for f in range(n_fields):
                for i, member in enumerate(exchange_order(members)):
                    out_ref[member, f, 0, :, :] = states[f][i : i + 1]

        return carry

    lax.fori_loop(0, 3, run, 0)


def vmem_spec():
    return pl.BlockSpec(memory_space=pltpu.VMEM)


def smem_spec():
    return pl.BlockSpec(memory_space=pltpu.SMEM)


def hbm_spec():
    return pl.BlockSpec(memory_space=pltpu.HBM)


def in_hbm(x):
    return pltpu.with_memory_space_constraint(x, pltpu.HBM)


def quick_device(
    realization_stack, velocity, diffusion, obs_cell, obs_order, obs_value, obs_var, field_mask
):
    _, n_fields, rows_here, n_cols = realization_stack.shape
    n_mem = lax.axis_size("mem")
    total_rows = 2 * rows_here
    n_obs = obs_cell.shape[0]
    batch = n_obs // BATCHES
    slab_index = lax.axis_index("row")
    own_row = slab_index * rows_here + lax.axis_index("mem")
    place = jnp.where(
        lax.broadcasted_iota(jnp.int32, (8, LANES), 0) == 0, slab_index, own_row
    ).astype(jnp.float32)
    params = pltpu.CompilerParams(vmem_limit_bytes=16 * MEGA)
    shape = jax.ShapeDtypeStruct
    f32, i32 = jnp.float32, jnp.int32
    swap = [(0, 1), (1, 0)]
    other = lax.ppermute(realization_stack, "row", swap)
    vel_other = lax.ppermute(velocity, "row", swap)
    table = (n_obs // LANES, LANES)
    info, own, vel_own, kappa = pl.pallas_call(
        functools.partial(prep_kernel, total_rows=total_rows, n_cols=n_cols),
        out_shape=(
            shape((16, n_obs), f32),
            shape(realization_stack.shape, f32),
            shape(velocity.shape, f32),
            shape((8, LANES), f32),
        ),
        in_specs=[hbm_spec()] * 8,
        out_specs=(vmem_spec(),) * 4,
        scratch_shapes=[
            pltpu.VMEM((1, n_obs), i32),
            pltpu.VMEM(table, i32),
            pltpu.VMEM(table, f32),
            pltpu.VMEM(table, f32),
            pltpu.SMEM(field_mask.shape, i32),
            pltpu.SMEM((1, n_fields), f32),
            pltpu.SemaphoreType.DMA((8,)),
        ],
        compiler_params=params,
        name="prep",
    )(
        in_hbm(obs_order.reshape(1, n_obs)),
        in_hbm(obs_cell.reshape(table)),
        in_hbm(obs_value.reshape(table)),
        in_hbm(obs_var.reshape(table)),
        in_hbm(field_mask),
        in_hbm(diffusion.reshape(1, n_fields)),
        in_hbm(realization_stack),
        in_hbm(velocity),
    )
    chunk = (n_fields * n_cols + n_obs) // LANES
    send = pl.pallas_call(
        forecast_kernel,
        out_shape=shape((n_mem * chunk, LANES), f32),
        in_specs=[vmem_spec()] * 7,
        out_specs=vmem_spec(),
        scratch_shapes=[
            pltpu.VMEM((n_fields, total_rows, n_cols), f32),
            pltpu.VMEM((n_obs // LANES, LANES), f32),
        ],
        compiler_params=params,
        name="forecast",
    )(place, kappa, own, other, vel_own, vel_other, info)
    recv = lax.all_to_all(
        send.reshape(n_mem, chunk, 1, LANES),
        "mem",
        split_axis=0,
        concat_axis=0,
        axis_index_groups=[exchange_order(n_mem)],
        tiled=True,
    ).reshape(send.shape)
    n_pair = n_obs - batch
    bf16 = jnp.bfloat16
    kept = batch // 2
    pair_hi, pair_lo, rest, cell_hi, cell_lo = pl.pallas_call(
        loc_kernel,
        out_shape=(
            shape((batch, n_pair), bf16),
            shape((kept, n_pair), bf16),
            pltpu.HBM((batch - kept, n_pair), bf16),
            pltpu.HBM((n_obs, n_cols), bf16),
            pltpu.HBM((n_obs, n_cols), bf16),
        ),
        in_specs=[vmem_spec(), vmem_spec()],
        out_specs=(vmem_spec(), vmem_spec(), hbm_spec(), hbm_spec(), hbm_spec()),
        scratch_shapes=[
            pltpu.VMEM((n_obs, 24), f32),
            pltpu.VMEM((batch - kept, n_pair), bf16),
            pltpu.VMEM((n_obs, n_cols), bf16),
            pltpu.VMEM((n_obs, n_cols), bf16),
            pltpu.VMEM((batch, n_pair), f32),
            pltpu.SemaphoreType.DMA((2 * BATCHES + 1,)),
        ],
        compiler_params=params,
        name="localize",
    )(place, info)
    rows = n_mem * (n_mem // 2 + 1)
    return pl.pallas_call(
        functools.partial(update_kernel, members=n_mem, n_fields=n_fields),
        out_shape=shape((n_mem, n_fields, 1, 1, n_cols), f32),
        in_specs=[vmem_spec()] * 4 + [hbm_spec()] * 3,
        out_specs=vmem_spec(),
        scratch_shapes=[
            pltpu.VMEM((BATCHES, 2 * rows, batch), bf16),
            pltpu.VMEM((rows, n_pair), f32),
            pltpu.VMEM((2 * rows * n_fields, batch), bf16),
            pltpu.VMEM((batch - kept, n_pair), bf16),
            pltpu.VMEM((n_obs, n_cols), bf16),
            pltpu.VMEM((n_obs, n_cols), bf16),
            pltpu.SemaphoreType.DMA((3,)),
        ],
        compiler_params=params,
        name="update",
    )(recv, info, pair_hi, pair_lo, in_hbm(rest), in_hbm(cell_hi), in_hbm(cell_lo))


def is_quick(realization_stack, obs_cell, n_mem, n_slab):
    local_members, n_fields, rows_here, n_cols = realization_stack.shape
    powers = all(n & (n - 1) == 0 for n in (rows_here, n_cols))
    return (
        n_slab == 2
        and local_members == 1
        and n_mem == rows_here == 16
        and n_fields <= 8
        and LOC_HALF * 2 <= LANES - 1
        and powers
        and n_cols % LANES == 0
        and obs_cell.shape[0] == 8 * n_cols
        and BATCHES == 2
    )


def per_device(
    realization_stack, velocity, diffusion, obs_cell, obs_order, obs_value, obs_var, field_mask
):
    local_members = realization_stack.shape[0]
    n_fields = realization_stack.shape[1]
    rows_here = realization_stack.shape[2]
    n_cols = realization_stack.shape[3]
    n_mem = lax.axis_size("mem")
    n_slab = lax.axis_size("row")
    total_members = local_members * n_mem
    total_rows = rows_here * n_slab
    if is_quick(realization_stack, obs_cell, n_mem, n_slab):
        return quick_device(
            realization_stack, velocity, diffusion, obs_cell, obs_order, obs_value, obs_var, field_mask
        )
    slab_index = lax.axis_index("row")
    member_index = lax.axis_index("mem")
    row_sub = rows_here // n_mem
    current = realization_stack
    for substep in range(SUBSTEPS):
        padded = extended(current, (("row", 2),), 1)
        current = advance(padded, velocity, diffusion)
    field_all, row_all, col_all = decode(obs_cell, total_rows, n_cols)
    batch_size = obs_cell.shape[0] // BATCHES
    layout = lax.all_to_all(current, "mem", split_axis=2, concat_axis=0, tiled=True)
    ensemble_now = layout.reshape(total_members, -1)
    base_row = slab_index * rows_here + member_index * row_sub
    for batch_num in range(BATCHES):
        picked = obs_order[batch_num * batch_size : (batch_num + 1) * batch_size]
        obs_field = field_all[picked]
        obs_row = row_all[picked]
        obs_col = col_all[picked]
        owned = ((obs_row >= base_row) & (obs_row < base_row + row_sub)).astype(jnp.float32)
        local_ids = (
            obs_field * row_sub * n_cols
            + jnp.clip(obs_row - base_row, 0, row_sub - 1) * n_cols
            + obs_col
        )
        partial_priors = jnp.take(ensemble_now, local_ids, axis=1) * owned[None, :]
        priors = lax.psum(partial_priors, ("mem", "row"))
        anomaly, adjust = innovations(priors, obs_value[picked], obs_var[picked])
        ensemble_now = regress(
            ensemble_now, base_row, obs_field, obs_row, obs_col, anomaly, adjust, field_mask, n_cols
        )
    return ensemble_now.reshape(total_members, n_fields, 1, row_sub, n_cols)


def solution(mesh):
    in_specs = (P("mem", None, "row", None), P(None, "row", None), P(), P(), P(), P(), P(), P())
    out_specs = P(None, None, "row", "mem", None)
    return jax.shard_map(
        per_device, mesh=mesh, in_specs=in_specs, out_specs=out_specs, check_vma=False
    )
```

```python
import functools

import jax
import jax.numpy as jnp
from jax import lax
from jax.experimental import pallas as pl
from jax.experimental.pallas import tpu as pltpu
from jax.sharding import PartitionSpec as P

SUBSTEPS = 4
BATCHES = 2
LOC_HALF = 32


precise = lax.Precision.HIGHEST


def extended(shard, sides, width):
    for axis, dim in sides:
        count, length = (lax.axis_size(axis), shard.shape[dim])
        up = [(i, (i + 1) % count) for i in range(count - 1)]
        down = [(j, i) for i, j in up]
        last = lax.slice_in_dim(shard, length - width, length, axis=dim)
        initial = lax.slice_in_dim(shard, 0, width, axis=dim)
        before = lax.ppermute(last, axis, up)
        after = lax.ppermute(initial, axis, down)
        shard = jnp.concatenate([before, shard, after], axis=dim)
    return shard


def advance(padded, velocity, diffusion):
    spec_pad = ((0, 0),) * (padded.ndim - 1) + ((1, 1),)
    col_padded = jnp.pad(padded, spec_pad)
    centre = col_padded[..., 1:-1, 1:-1]
    north_cell = col_padded[..., :-2, 1:-1]
    south_cell = col_padded[..., 2:, 1:-1]
    west_cell = col_padded[..., 1:-1, :-2]
    east_cell = col_padded[..., 1:-1, 2:]
    along_col = velocity[0]
    along_row = velocity[1]
    spread = north_cell + south_cell + west_cell + east_cell - 4.0 * centre
    carried = (
        jnp.maximum(along_col, 0.0) * (centre - west_cell)
        + jnp.minimum(along_col, 0.0) * (east_cell - centre)
        + jnp.maximum(along_row, 0.0) * (centre - north_cell)
        + jnp.minimum(along_row, 0.0) * (south_cell - centre)
    )
    return centre + diffusion[:, None, None] * spread - carried


def gaspari(dist_sq):
    scaled = jnp.sqrt(dist_sq) / LOC_HALF
    clipped = jnp.maximum(scaled, 1.0)
    inner_part = (
        ((-0.25 * scaled + 0.5) * scaled + 0.625) * scaled - 5.0 / 3.0
    ) * scaled * scaled + 1.0
    outer_part = (
        ((((scaled / 12.0 - 0.5) * scaled + 0.625) * scaled + 5.0 / 3.0) * scaled - 5.0) * scaled
        + 4.0
        - 2.0 / (3.0 * clipped)
    )
    return jnp.where(scaled <= 1.0, inner_part, jnp.where(scaled <= 2.0, outer_part, 0.0))


def decode(flat_cells, total_rows, n_cols):
    field_ids = flat_cells // (total_rows * n_cols)
    row_ids = flat_cells // n_cols % total_rows
    col_ids = flat_cells % n_cols
    return (field_ids, row_ids, col_ids)


def innovations(priors, obs_values, obs_noise):
    members = priors.shape[0]
    average = jnp.mean(priors, axis=0)
    anomaly = priors - average
    spread = jnp.sum(anomaly * anomaly, axis=0) / (members - 1)
    variance_sum = spread + obs_noise
    root_sum = jnp.sqrt(variance_sum)
    shrink = 1.0 / (root_sum * (jnp.sqrt(obs_noise) + root_sum))
    adjust = (obs_values - average) / variance_sum - shrink * anomaly
    return (anomaly, adjust)


def regress(
    ensemble_now, base_row, obs_field, obs_row, obs_col, anomaly, adjust, field_mask, n_cols
):
    members, n_cells = ensemble_now.shape
    n_fields = field_mask.shape[0]
    per_field = n_cells // n_fields
    local_ids = lax.iota(jnp.int32, per_field)
    cell_row = (base_row + local_ids // n_cols).astype(jnp.float32)
    cell_col = (local_ids % n_cols).astype(jnp.float32)
    centred = ensemble_now - jnp.mean(ensemble_now, axis=0)
    mask_float = field_mask.astype(jnp.float32)
    total_obs = obs_field.shape[0]
    obs_block = min(256, total_obs)
    increment = jnp.zeros_like(ensemble_now)
    for offset in range(0, total_obs, obs_block):
        row_gap = cell_row[:, None] - obs_row[None, offset : offset + obs_block].astype(jnp.float32)
        col_gap = cell_col[:, None] - obs_col[None, offset : offset + obs_block].astype(jnp.float32)
        closeness = gaspari(row_gap * row_gap + col_gap * col_gap)
        field_hot = (
            obs_field[None, offset : offset + obs_block] == lax.iota(jnp.int32, n_fields)[:, None]
        ).astype(jnp.float32)
        allowed = jnp.dot(mask_float, field_hot, precision=precise)
        covariance = lax.dot_general(
            centred,
            anomaly[:, offset : offset + obs_block],
            (((0,), (0,)), ((), ())),
            precision=precise,
        )
        weights = (
            covariance.reshape(n_fields, per_field, obs_block)
            * (closeness[None] * allowed[:, None, :])
            / (members - 1)
        )
        increment = increment + lax.dot_general(
            adjust[:, offset : offset + obs_block],
            weights.reshape(n_cells, obs_block),
            (((1,), (1,)), ((), ())),
            precision=precise,
        )
    return ensemble_now + increment


LANES = 128
MEGA = 1 << 20


def split_two(x):
    high = x.astype(jnp.bfloat16)
    low = (x - high.astype(jnp.float32)).astype(jnp.bfloat16)
    return high, low


def split_three(x):
    high = x.astype(jnp.bfloat16)
    rest = x - high.astype(jnp.float32)
    mid = rest.astype(jnp.bfloat16)
    low = (rest - mid.astype(jnp.float32)).astype(jnp.bfloat16)
    return high, mid, low


def bdot(a, b):
    return jnp.dot(a, b, preferred_element_type=jnp.float32)


def log2(n):
    return n.bit_length() - 1


def start_copies(pairs, sems):
    copies = [pltpu.make_async_copy(src, dst, sems.at[i]) for i, (src, dst) in enumerate(pairs)]
    for copy in copies:
        copy.start()
    return copies


def finish(copies):
    for copy in copies:
        copy.wait()


def exchange_order(n):
    return [(i % 4 * (n // 4) + i // 4 + n // 2) % n for i in range(n)]


def prep_kernel(
    order_hbm, cell_hbm, value_hbm, var_hbm, mask_hbm, diffusion_hbm, stack_hbm, velocity_hbm,
    info_ref, own_ref, vel_ref, kappa_ref,
    order_buf, cell_buf, value_buf, var_buf, mask_buf, diffusion_buf, sems,
    *, total_rows, n_cols,
):
    copies = start_copies(
        [
            (order_hbm, order_buf), (cell_hbm, cell_buf), (value_hbm, value_buf), (var_hbm, var_buf),
            (mask_hbm, mask_buf), (diffusion_hbm, diffusion_buf), (velocity_hbm, vel_ref),
            (stack_hbm, own_ref),
        ],
        sems,
    )
    finish(copies[:4])
    table_rows = cell_buf.shape[0]
    n_fields = mask_buf.shape[0]
    order = order_buf[...]
    n_obs = order.shape[1]
    table = jnp.concatenate(
        [cell_buf[...].astype(jnp.float32), value_buf[...], var_buf[...]], axis=0
    )
    parts = jnp.concatenate(split_three(table), axis=0)
    lane_hot = (
        lax.broadcasted_iota(jnp.int32, (LANES, n_obs), 0) == (order & (LANES - 1))
    ).astype(jnp.float32).astype(jnp.bfloat16)
    found = bdot(parts, lane_hot)
    size = 3 * table_rows
    found = (found[:size] + found[size : 2 * size]) + found[2 * size :]
    row_hot = lax.broadcasted_iota(jnp.int32, (table_rows, n_obs), 0) == (order >> log2(LANES))

    def take(i):
        rows = found[i * table_rows : (i + 1) * table_rows]
        return jnp.sum(jnp.where(row_hot, rows, 0.0), axis=0, keepdims=True)

    cell = take(0).astype(jnp.int32)
    strip = cell >> log2(n_cols)
    field = strip >> log2(total_rows)
    row = strip & (total_rows - 1)
    col = cell & (n_cols - 1)
    as_float = lambda x: x.astype(jnp.float32)
    zero = jnp.zeros((1, n_obs), jnp.float32)
    finish(copies[4:])
    for f in range(n_fields):
        kappa_ref[f : f + 1, :] = jnp.full((1, LANES), diffusion_buf[0, f], jnp.float32)
    up = lax.broadcasted_iota(jnp.int32, (8, 8), 0)
    along = lax.broadcasted_iota(jnp.int32, (8, 8), 1)
    mask = jnp.zeros((8, 8), jnp.float32)
    for f in range(n_fields):
        for b in range(n_fields):
            mask = jnp.where((up == f) & (along == b), as_float(mask_buf[f, b]), mask)
    field_hot = as_float(lax.broadcasted_iota(jnp.int32, (8, n_obs), 0) == field)
    info = jnp.concatenate(
        [
            as_float(field), as_float(row), as_float(col), take(1), take(2), as_float(strip), zero, zero,
            bdot(mask.astype(jnp.bfloat16), field_hot.astype(jnp.bfloat16)),
        ],
        axis=0,
    )
    info_ref[...] = info


def forecast_kernel(
    place_ref, kappa_ref, own_ref, other_ref, vel_own_ref, vel_other_ref, info_ref,
    send_ref, field_buf, prior_buf,
):
    n_fields, n_rows, n_cols = field_buf.shape
    half = n_rows // 2
    n_dest = half
    chunk = send_ref.shape[0] // n_dest
    first_slab = place_ref[0:1, 0:1] < 0.5

    def whole_of(own, other):
        return jnp.concatenate([jnp.where(first_slab, own, other), jnp.where(first_slab, other, own)], axis=0)

    u = whole_of(vel_own_ref[0], vel_other_ref[0])
    v = whole_of(vel_own_ref[1], vel_other_ref[1])
    row = lax.broadcasted_iota(jnp.int32, (n_rows, n_cols), 0)
    col = lax.broadcasted_iota(jnp.int32, (n_rows, n_cols), 1)
    u_pos, u_neg = jnp.maximum(u, 0.0), jnp.minimum(u, 0.0)
    v_pos, v_neg = jnp.maximum(v, 0.0), jnp.minimum(v, 0.0)
    outflow = (u_neg - u_pos) + (v_neg - v_pos)
    cells, weights = [], []
    for f in range(n_fields):
        kappa = kappa_ref[f : f + 1, 0:1]
        weights.append((
            (1.0 - 4.0 * kappa) + outflow,
            jnp.where(row == 0, 0.0, kappa + v_pos),
            jnp.where(row == n_rows - 1, 0.0, kappa - v_neg),
            jnp.where(col == 0, 0.0, kappa + u_pos),
            jnp.where(col == n_cols - 1, 0.0, kappa - u_neg),
        ))
        cells.append(whole_of(own_ref[0, f], other_ref[0, f]))
    for _ in range(SUBSTEPS):
        for f in range(n_fields):
            c = cells[f]
            k_c, k_n, k_s, k_w, k_e = weights[f]
            cells[f] = (
                (c * k_c + pltpu.roll(c, 1, 0) * k_n)
                + (pltpu.roll(c, n_rows - 1, 0) * k_s + pltpu.roll(c, 1, 1) * k_w)
                + pltpu.roll(c, n_cols - 1, 1) * k_e
            )
    for f in range(n_fields):
        field_buf[f] = cells[f]
    whole = field_buf[...].reshape(n_fields * n_rows, n_cols)
    strips = n_fields * n_rows
    parts = jnp.concatenate(split_three(whole), axis=0)
    n_obs = info_ref.shape[1]
    width = 2 * LANES
    strip_ids = lax.broadcasted_iota(jnp.int32, (strips, width), 0)
    col_ids = lax.broadcasted_iota(jnp.int32, (n_cols, width), 0)
    for q in range(n_obs // width):
        cols = info_ref[2:3, q * width : (q + 1) * width].astype(jnp.int32)
        strip = info_ref[5:6, q * width : (q + 1) * width].astype(jnp.int32)
        hot = (col_ids == cols).astype(jnp.float32).astype(jnp.bfloat16)
        found = bdot(parts, hot)
        found = (found[:strips] + found[strips : 2 * strips]) + found[2 * strips :]
        values = jnp.sum(jnp.where(strip_ids == strip, found, 0.0), axis=0, keepdims=True)
        for h in range(width // LANES):
            at = q * (width // LANES) + h
            prior_buf[at : at + 1, :] = values[:, h * LANES : (h + 1) * LANES]
    priors = prior_buf[...]
    lead = chunk - n_obs // LANES
    for d in range(n_dest):
        send_ref[d * chunk + lead : (d + 1) * chunk, :] = priors
    pieces = n_cols // LANES
    for f in range(n_fields):
        rows = jnp.where(first_slab, field_buf[f, :half, :], field_buf[f, half:, :])
        for i, dest in enumerate(exchange_order(n_dest)):
            for h in range(pieces):
                at = i * chunk + f * pieces + h
                send_ref[at : at + 1, :] = rows[dest : dest + 1, h * LANES : (h + 1) * LANES]
    for i in range(n_fields * pieces, lead):
        send_ref[pl.ds(i, n_dest, stride=chunk), :] = jnp.zeros((n_dest, LANES), jnp.float32)


def closeness_of(dist_sq):
    inverse = lax.rsqrt(jnp.maximum(dist_sq, 1e-6))
    z = dist_sq * inverse
    half_sq = 0.5 * dist_sq
    inner = 1.0 + dist_sq * ((half_sq - 5.0 / 3.0) + z * (0.625 - 0.5 * half_sq))
    left = jnp.maximum(2.0 - z, 0.0)
    left = left * left
    left = left * left
    outer = left * ((dist_sq + (z + z)) - 0.5) * (inverse * (1.0 / 12.0))
    return jnp.where(dist_sq <= 1.0, inner, outer)


def loc_kernel(
    place_ref, info_ref, pair_hi_ref, pair_lo_ref, rest_hbm, cell_hi_hbm, cell_lo_hbm,
    infot_ref, rest_ref, cell_hi_ref, cell_lo_ref, gap_buf, sems,
):
    n_obs = info_ref.shape[1]
    batch, n_pair = pair_hi_ref.shape
    n_cols = cell_hi_ref.shape[1]
    scale = 1.0 / LOC_HALF
    far = 32.0 * LOC_HALF * LOC_HALF
    row, col = info_ref[1:2, :], info_ref[2:3, :]
    norm = [part.astype(jnp.float32) for part in split_three(row * row + col * col)]
    one = jnp.ones((1, n_obs), jnp.float32)
    hot = lax.broadcasted_iota(jnp.int32, (8, n_obs), 0) == info_ref[0:1, :].astype(jnp.int32)
    zeros = jnp.zeros((6, n_obs), jnp.float32)
    feature_k = jnp.concatenate(
        norm + [one, one, one, -2.0 * row, -2.0 * col, -far * info_ref[8:16, :], one * far, row, zeros], axis=0
    )
    feature_j = jnp.concatenate(
        [one, one, one] + norm + [row, col, hot.astype(jnp.float32), one], axis=0
    )[:, batch:]
    infot_ref[...] = feature_k.T
    terms = feature_j.shape[0]
    gap_buf[...] = bdot(
        infot_ref[0:batch, 0:terms].astype(jnp.bfloat16), (feature_j * (scale * scale)).astype(jnp.bfloat16)
    )
    table_rows = 32
    own_row = place_ref[1:2, 0:1]
    gap_row = (lax.broadcasted_iota(jnp.int32, (table_rows, LANES), 0).astype(jnp.float32) - own_row) * scale
    gap_col = lax.broadcasted_iota(jnp.int32, (table_rows, LANES), 1).astype(jnp.float32) * scale
    by_row = jnp.concatenate(split_three(closeness_of(gap_row * gap_row + gap_col * gap_col)), axis=0)
    row_ids = lax.broadcasted_iota(jnp.int32, (1, 3 * table_rows), 1) & (table_rows - 1)
    copies = []
    col_at, row_at = 7, terms
    for b in range(BATCHES):
        span = slice(b * batch, (b + 1) * batch)
        rows = infot_ref[span, row_at : row_at + 1].astype(jnp.int32)
        hot = (row_ids == rows).astype(jnp.float32).astype(jnp.bfloat16)
        table = bdot(hot, by_row)
        cols = infot_ref[span, col_at : col_at + 1] * -0.5
        col_k = jnp.broadcast_to(cols, (batch, LANES)).astype(jnp.int32)
        for h in range(n_cols // LANES):
            here = slice(h * LANES, (h + 1) * LANES)
            col = lax.broadcasted_iota(jnp.int32, (batch, LANES), 1) + h * LANES
            gap = jnp.minimum(jnp.abs(col - col_k), LANES - 1)
            at_hi, at_lo = split_two(jnp.take_along_axis(table, gap, axis=1))
            cell_hi_ref[span, here] = at_hi
            cell_lo_ref[span, here] = at_lo
        copies += start_copies(
            [
                (cell_hi_ref.at[span, :], cell_hi_hbm.at[span, :]),
                (cell_lo_ref.at[span, :], cell_lo_hbm.at[span, :]),
            ],
            sems.at[2 * b :],
        )
    step = 128
    kept = pair_lo_ref.shape[0]

    def pair_rows(low_ref, first):
        def body(i, carry):
            to = pl.multiple_of(i * step, step)
            at = pl.multiple_of(first + i * step, step)
            for h in range(n_pair // LANES):
                here = slice(h * LANES, (h + 1) * LANES)
                high, low = split_two(closeness_of(gap_buf[pl.ds(at, step), here]))
                pair_hi_ref[pl.ds(at, step), here] = high
                low_ref[pl.ds(to, step), here] = low
            return carry

        lax.fori_loop(0, low_ref.shape[0] // step, body, 0)

    pair_rows(rest_ref, kept)
    copies += start_copies([(rest_ref, rest_hbm)], sems.at[2 * BATCHES :])
    pair_rows(pair_lo_ref, 0)
    finish(copies)


def member_roll(x, shift):
    shift = shift % x.shape[0]
    return pltpu.roll(x, shift, 0) if shift else x


def factors(priors, value, var):
    members = priors.shape[0]
    average = jnp.sum(priors, axis=0, keepdims=True) * (1.0 / members)
    anomaly = priors - average
    variance = jnp.sum(anomaly * anomaly, axis=0, keepdims=True) * (1.0 / (members - 1)) + var
    root = jnp.sqrt(variance)
    shrunk = anomaly * (1.0 / ((members - 1) * (root * (jnp.sqrt(var) + root))))
    rows = [shrunk * member_roll(anomaly, -d) for d in range(members // 2)]
    rows.append(anomaly * ((value - average) / ((members - 1) * variance)))
    return rows


def combined(state, sums):
    members = state.shape[0]
    half = members // 2
    centred = state - jnp.sum(state, axis=0, keepdims=True) * (1.0 / members)
    block = lambda d: sums[d * members : (d + 1) * members]
    across = member_roll(centred, half)
    move = (centred - across) * block(0)
    for d in range(1, half):
        move = move + (member_roll(centred, -d) - across) * block(d)
        move = move + member_roll((centred - member_roll(across, -d)) * block(d), d)
    shift = jnp.sum(centred * block(half), axis=0, keepdims=True)
    return state + (shift - move)


def update_kernel(
    recv_ref, info_ref, pair_hi_ref, pair_lo_ref, rest_hbm, cell_hi_hbm, cell_lo_hbm,
    out_ref, fac_buf, sums_buf, mask_buf, rest_ref, cell_hi_ref, cell_lo_ref, sems, *, members, n_fields,
):
    tables = [(rest_hbm, rest_ref), (cell_hi_hbm, cell_hi_ref), (cell_lo_hbm, cell_lo_ref)]
    copies = [pltpu.make_async_copy(src, dst, sems.at[i]) for i, (src, dst) in enumerate(tables)]
    n_obs = info_ref.shape[1]
    batch = n_obs // BATCHES
    chunk = recv_ref.shape[0] // members
    per_chunk = n_obs // LANES
    lead = chunk - per_chunk
    pieces = cell_hi_ref.shape[1] // LANES
    size = fac_buf.shape[1] // 2
    kept = pair_lo_ref.shape[0]

    def member_row(i):
        return recv_ref[pl.ds(i, members, stride=chunk), :]

    def priors_of(b):
        first = lead + b * (per_chunk // BATCHES)
        return jnp.concatenate([member_row(first + q) for q in range(per_chunk // BATCHES)], axis=1)

    def set_factors(b, priors):
        span = slice(b * batch, (b + 1) * batch)
        rows = factors(priors, info_ref[3:4, span], info_ref[4:5, span])
        for i, r in enumerate(rows):
            high, low = split_two(r)
            fac_buf[b, i * members : (i + 1) * members, :] = high
            fac_buf[b, size + i * members : size + (i + 1) * members, :] = low

    def run(step, carry):
        @pl.when(step == 0)
        def _():
            for copy in copies:
                copy.start()
            set_factors(0, priors_of(0))
            first = bdot(fac_buf[0], pair_hi_ref[...])
            sums_buf[...] = (first[:size] + first[size:]) + bdot(fac_buf[0, :size, :kept], pair_lo_ref[...])

        @pl.when(step == 1)
        def _():
            finish(copies[:1])
            sums = sums_buf[...] + bdot(fac_buf[0, :size, kept:], rest_ref[...])
            set_factors(1, combined(priors_of(1), sums))

        @pl.when(step == 2)
        def _():
            finish(copies[1:])
            states = [
                jnp.concatenate([member_row(f * pieces + h) for h in range(pieces)], axis=1)
                for f in range(n_fields)
            ]
            all_rows = n_fields * size
            for b in range(BATCHES):
                span = slice(b * batch, (b + 1) * batch)
                for f in range(n_fields):
                    open_to = info_ref[8 + f : 9 + f, span].astype(jnp.bfloat16)
                    mask_buf[f * size : (f + 1) * size, :] = fac_buf[b, :size, :] * open_to
                    mask_buf[all_rows + f * size : all_rows + (f + 1) * size, :] = fac_buf[b, size:, :] * open_to
                first = bdot(mask_buf[...], cell_hi_ref[span, :])
                sums = (first[:all_rows] + first[all_rows:]) + bdot(mask_buf[:all_rows, :], cell_lo_ref[span, :])
                states = [combined(state, sums[f * size : (f + 1) * size]) for f, state in enumerate(states)]
            for f in range(n_fields):
                for i, member in enumerate(exchange_order(members)):
                    out_ref[member, f, 0, :, :] = states[f][i : i + 1]

        return carry

    lax.fori_loop(0, 3, run, 0)


def vmem_spec():
    return pl.BlockSpec(memory_space=pltpu.VMEM)


def smem_spec():
    return pl.BlockSpec(memory_space=pltpu.SMEM)


def hbm_spec():
    return pl.BlockSpec(memory_space=pltpu.HBM)


def in_hbm(x):
    return pltpu.with_memory_space_constraint(x, pltpu.HBM)


def quick_device(
    realization_stack, velocity, diffusion, obs_cell, obs_order, obs_value, obs_var, field_mask
):
    _, n_fields, rows_here, n_cols = realization_stack.shape
    n_mem = lax.axis_size("mem")
    total_rows = 2 * rows_here
    n_obs = obs_cell.shape[0]
    batch = n_obs // BATCHES
    slab_index = lax.axis_index("row")
    own_row = slab_index * rows_here + lax.axis_index("mem")
    place = jnp.where(
        lax.broadcasted_iota(jnp.int32, (8, LANES), 0) == 0, slab_index, own_row
    ).astype(jnp.float32)
    params = pltpu.CompilerParams(vmem_limit_bytes=16 * MEGA)
    shape = jax.ShapeDtypeStruct
    f32, i32 = jnp.float32, jnp.int32
    swap = [(0, 1), (1, 0)]
    other = lax.ppermute(realization_stack, "row", swap)
    vel_other = lax.ppermute(velocity, "row", swap)
    table = (n_obs // LANES, LANES)
    info, own, vel_own, kappa = pl.pallas_call(
        functools.partial(prep_kernel, total_rows=total_rows, n_cols=n_cols),
        out_shape=(
            shape((16, n_obs), f32),
            shape(realization_stack.shape, f32),
            shape(velocity.shape, f32),
            shape((8, LANES), f32),
        ),
        in_specs=[hbm_spec()] * 8,
        out_specs=(vmem_spec(),) * 4,
        scratch_shapes=[
            pltpu.VMEM((1, n_obs), i32),
            pltpu.VMEM(table, i32),
            pltpu.VMEM(table, f32),
            pltpu.VMEM(table, f32),
            pltpu.SMEM(field_mask.shape, i32),
            pltpu.SMEM((1, n_fields), f32),
            pltpu.SemaphoreType.DMA((8,)),
        ],
        compiler_params=params,
        name="prep",
    )(
        in_hbm(obs_order.reshape(1, n_obs)),
        in_hbm(obs_cell.reshape(table)),
        in_hbm(obs_value.reshape(table)),
        in_hbm(obs_var.reshape(table)),
        in_hbm(field_mask),
        in_hbm(diffusion.reshape(1, n_fields)),
        in_hbm(realization_stack),
        in_hbm(velocity),
    )
    chunk = (n_fields * n_cols + n_obs) // LANES
    send = pl.pallas_call(
        forecast_kernel,
        out_shape=shape((n_mem * chunk, LANES), f32),
        in_specs=[vmem_spec()] * 7,
        out_specs=vmem_spec(),
        scratch_shapes=[
            pltpu.VMEM((n_fields, total_rows, n_cols), f32),
            pltpu.VMEM((n_obs // LANES, LANES), f32),
        ],
        compiler_params=params,
        name="forecast",
    )(place, kappa, own, other, vel_own, vel_other, info)
    recv = lax.all_to_all(
        send.reshape(n_mem, chunk, 1, LANES),
        "mem",
        split_axis=0,
        concat_axis=0,
        axis_index_groups=[exchange_order(n_mem)],
        tiled=True,
    ).reshape(send.shape)
    n_pair = n_obs - batch
    bf16 = jnp.bfloat16
    kept = batch // 2
    pair_hi, pair_lo, rest, cell_hi, cell_lo = pl.pallas_call(
        loc_kernel,
        out_shape=(
            shape((batch, n_pair), bf16),
            shape((kept, n_pair), bf16),
            pltpu.HBM((batch - kept, n_pair), bf16),
            pltpu.HBM((n_obs, n_cols), bf16),
            pltpu.HBM((n_obs, n_cols), bf16),
        ),
        in_specs=[vmem_spec(), vmem_spec()],
        out_specs=(vmem_spec(), vmem_spec(), hbm_spec(), hbm_spec(), hbm_spec()),
        scratch_shapes=[
            pltpu.VMEM((n_obs, 24), f32),
            pltpu.VMEM((batch - kept, n_pair), bf16),
            pltpu.VMEM((n_obs, n_cols), bf16),
            pltpu.VMEM((n_obs, n_cols), bf16),
            pltpu.VMEM((batch, n_pair), f32),
            pltpu.SemaphoreType.DMA((2 * BATCHES + 1,)),
        ],
        compiler_params=params,
        name="localize",
    )(place, info)
    rows = n_mem * (n_mem // 2 + 1)
    return pl.pallas_call(
        functools.partial(update_kernel, members=n_mem, n_fields=n_fields),
        out_shape=shape((n_mem, n_fields, 1, 1, n_cols), f32),
        in_specs=[vmem_spec()] * 4 + [hbm_spec()] * 3,
        out_specs=vmem_spec(),
        scratch_shapes=[
            pltpu.VMEM((BATCHES, 2 * rows, batch), bf16),
            pltpu.VMEM((rows, n_pair), f32),
            pltpu.VMEM((2 * rows * n_fields, batch), bf16),
            pltpu.VMEM((batch - kept, n_pair), bf16),
            pltpu.VMEM((n_obs, n_cols), bf16),
            pltpu.VMEM((n_obs, n_cols), bf16),
            pltpu.SemaphoreType.DMA((3,)),
        ],
        compiler_params=params,
        name="update",
    )(recv, info, pair_hi, pair_lo, in_hbm(rest), in_hbm(cell_hi), in_hbm(cell_lo))


def is_quick(realization_stack, obs_cell, n_mem, n_slab):
    local_members, n_fields, rows_here, n_cols = realization_stack.shape
    powers = all(n & (n - 1) == 0 for n in (rows_here, n_cols))
    return (
        n_slab == 2
        and local_members == 1
        and n_mem == rows_here == 16
        and n_fields <= 8
        and LOC_HALF * 2 <= LANES - 1
        and powers
        and n_cols % LANES == 0
        and obs_cell.shape[0] == 8 * n_cols
        and BATCHES == 2
    )


def per_device(
    realization_stack, velocity, diffusion, obs_cell, obs_order, obs_value, obs_var, field_mask
):
    local_members = realization_stack.shape[0]
    n_fields = realization_stack.shape[1]
    rows_here = realization_stack.shape[2]
    n_cols = realization_stack.shape[3]
    n_mem = lax.axis_size("mem")
    n_slab = lax.axis_size("row")
    total_members = local_members * n_mem
    total_rows = rows_here * n_slab
    if is_quick(realization_stack, obs_cell, n_mem, n_slab):
        return quick_device(
            realization_stack, velocity, diffusion, obs_cell, obs_order, obs_value, obs_var, field_mask
        )
    slab_index = lax.axis_index("row")
    member_index = lax.axis_index("mem")
    row_sub = rows_here // n_mem
    current = realization_stack
    for substep in range(SUBSTEPS):
        padded = extended(current, (("row", 2),), 1)
        current = advance(padded, velocity, diffusion)
    field_all, row_all, col_all = decode(obs_cell, total_rows, n_cols)
    batch_size = obs_cell.shape[0] // BATCHES
    layout = lax.all_to_all(current, "mem", split_axis=2, concat_axis=0, tiled=True)
    ensemble_now = layout.reshape(total_members, -1)
    base_row = slab_index * rows_here + member_index * row_sub
    for batch_num in range(BATCHES):
        picked = obs_order[batch_num * batch_size : (batch_num + 1) * batch_size]
        obs_field = field_all[picked]
        obs_row = row_all[picked]
        obs_col = col_all[picked]
        owned = ((obs_row >= base_row) & (obs_row < base_row + row_sub)).astype(jnp.float32)
        local_ids = (
            obs_field * row_sub * n_cols
            + jnp.clip(obs_row - base_row, 0, row_sub - 1) * n_cols
            + obs_col
        )
        partial_priors = jnp.take(ensemble_now, local_ids, axis=1) * owned[None, :]
        priors = lax.psum(partial_priors, ("mem", "row"))
        anomaly, adjust = innovations(priors, obs_value[picked], obs_var[picked])
        ensemble_now = regress(
            ensemble_now, base_row, obs_field, obs_row, obs_col, anomaly, adjust, field_mask, n_cols
        )
    return ensemble_now.reshape(total_members, n_fields, 1, row_sub, n_cols)


def solution(mesh):
    in_specs = (P("mem", None, "row", None), P(None, "row", None), P(), P(), P(), P(), P(), P())
    out_specs = P(None, None, "row", "mem", None)
    return jax.shard_map(
        per_device, mesh=mesh, in_specs=in_specs, out_specs=out_specs, check_vma=False
    )
```

```python
import functools

import jax
import jax.numpy as jnp
from jax import lax
from jax.experimental import pallas as pl
from jax.experimental.pallas import tpu as pltpu
from jax.sharding import PartitionSpec as P

SUBSTEPS = 4
BATCHES = 2
LOC_HALF = 32


precise = lax.Precision.HIGHEST


def extended(shard, sides, width):
    for axis, dim in sides:
        count, length = (lax.axis_size(axis), shard.shape[dim])
        up = [(i, (i + 1) % count) for i in range(count - 1)]
        down = [(j, i) for i, j in up]
        last = lax.slice_in_dim(shard, length - width, length, axis=dim)
        initial = lax.slice_in_dim(shard, 0, width, axis=dim)
        before = lax.ppermute(last, axis, up)
        after = lax.ppermute(initial, axis, down)
        shard = jnp.concatenate([before, shard, after], axis=dim)
    return shard


def advance(padded, velocity, diffusion):
    spec_pad = ((0, 0),) * (padded.ndim - 1) + ((1, 1),)
    col_padded = jnp.pad(padded, spec_pad)
    centre = col_padded[..., 1:-1, 1:-1]
    north_cell = col_padded[..., :-2, 1:-1]
    south_cell = col_padded[..., 2:, 1:-1]
    west_cell = col_padded[..., 1:-1, :-2]
    east_cell = col_padded[..., 1:-1, 2:]
    along_col = velocity[0]
    along_row = velocity[1]
    spread = north_cell + south_cell + west_cell + east_cell - 4.0 * centre
    carried = (
        jnp.maximum(along_col, 0.0) * (centre - west_cell)
        + jnp.minimum(along_col, 0.0) * (east_cell - centre)
        + jnp.maximum(along_row, 0.0) * (centre - north_cell)
        + jnp.minimum(along_row, 0.0) * (south_cell - centre)
    )
    return centre + diffusion[:, None, None] * spread - carried


def gaspari(dist_sq):
    scaled = jnp.sqrt(dist_sq) / LOC_HALF
    clipped = jnp.maximum(scaled, 1.0)
    inner_part = (
        ((-0.25 * scaled + 0.5) * scaled + 0.625) * scaled - 5.0 / 3.0
    ) * scaled * scaled + 1.0
    outer_part = (
        ((((scaled / 12.0 - 0.5) * scaled + 0.625) * scaled + 5.0 / 3.0) * scaled - 5.0) * scaled
        + 4.0
        - 2.0 / (3.0 * clipped)
    )
    return jnp.where(scaled <= 1.0, inner_part, jnp.where(scaled <= 2.0, outer_part, 0.0))


def decode(flat_cells, total_rows, n_cols):
    field_ids = flat_cells // (total_rows * n_cols)
    row_ids = flat_cells // n_cols % total_rows
    col_ids = flat_cells % n_cols
    return (field_ids, row_ids, col_ids)


def innovations(priors, obs_values, obs_noise):
    members = priors.shape[0]
    average = jnp.mean(priors, axis=0)
    anomaly = priors - average
    spread = jnp.sum(anomaly * anomaly, axis=0) / (members - 1)
    variance_sum = spread + obs_noise
    root_sum = jnp.sqrt(variance_sum)
    shrink = 1.0 / (root_sum * (jnp.sqrt(obs_noise) + root_sum))
    adjust = (obs_values - average) / variance_sum - shrink * anomaly
    return (anomaly, adjust)


def regress(
    ensemble_now, base_row, obs_field, obs_row, obs_col, anomaly, adjust, field_mask, n_cols
):
    members, n_cells = ensemble_now.shape
    n_fields = field_mask.shape[0]
    per_field = n_cells // n_fields
    local_ids = lax.iota(jnp.int32, per_field)
    cell_row = (base_row + local_ids // n_cols).astype(jnp.float32)
    cell_col = (local_ids % n_cols).astype(jnp.float32)
    centred = ensemble_now - jnp.mean(ensemble_now, axis=0)
    mask_float = field_mask.astype(jnp.float32)
    total_obs = obs_field.shape[0]
    obs_block = min(256, total_obs)
    increment = jnp.zeros_like(ensemble_now)
    for offset in range(0, total_obs, obs_block):
        row_gap = cell_row[:, None] - obs_row[None, offset : offset + obs_block].astype(jnp.float32)
        col_gap = cell_col[:, None] - obs_col[None, offset : offset + obs_block].astype(jnp.float32)
        closeness = gaspari(row_gap * row_gap + col_gap * col_gap)
        field_hot = (
            obs_field[None, offset : offset + obs_block] == lax.iota(jnp.int32, n_fields)[:, None]
        ).astype(jnp.float32)
        allowed = jnp.dot(mask_float, field_hot, precision=precise)
        covariance = lax.dot_general(
            centred,
            anomaly[:, offset : offset + obs_block],
            (((0,), (0,)), ((), ())),
            precision=precise,
        )
        weights = (
            covariance.reshape(n_fields, per_field, obs_block)
            * (closeness[None] * allowed[:, None, :])
            / (members - 1)
        )
        increment = increment + lax.dot_general(
            adjust[:, offset : offset + obs_block],
            weights.reshape(n_cells, obs_block),
            (((1,), (1,)), ((), ())),
            precision=precise,
        )
    return ensemble_now + increment


LANES = 128
MEGA = 1 << 20


def split_two(x):
    high = x.astype(jnp.bfloat16)
    low = (x - high.astype(jnp.float32)).astype(jnp.bfloat16)
    return high, low


def split_three(x):
    high = x.astype(jnp.bfloat16)
    rest = x - high.astype(jnp.float32)
    mid = rest.astype(jnp.bfloat16)
    low = (rest - mid.astype(jnp.float32)).astype(jnp.bfloat16)
    return high, mid, low


def bdot(a, b):
    return jnp.dot(a, b, preferred_element_type=jnp.float32)


def log2(n):
    return n.bit_length() - 1


def start_copies(pairs, sems):
    copies = [pltpu.make_async_copy(src, dst, sems.at[i]) for i, (src, dst) in enumerate(pairs)]
    for copy in copies:
        copy.start()
    return copies


def finish(copies):
    for copy in copies:
        copy.wait()


def exchange_order(n):
    return [(i % 4 * (n // 4) + i // 4 + n // 2) % n for i in range(n)]


def prep_kernel(
    order_hbm, cell_hbm, value_hbm, var_hbm, mask_hbm, diffusion_hbm, stack_hbm, velocity_hbm,
    info_ref, own_ref, vel_ref, kappa_ref,
    order_buf, cell_buf, value_buf, var_buf, mask_buf, diffusion_buf, sems,
    *, total_rows, n_cols,
):
    copies = start_copies(
        [
            (order_hbm, order_buf), (cell_hbm, cell_buf), (value_hbm, value_buf), (var_hbm, var_buf),
            (mask_hbm, mask_buf), (diffusion_hbm, diffusion_buf), (velocity_hbm, vel_ref),
            (stack_hbm, own_ref),
        ],
        sems,
    )
    finish(copies[:4])
    table_rows = cell_buf.shape[0]
    n_fields = mask_buf.shape[0]
    order = order_buf[...]
    n_obs = order.shape[1]
    table = jnp.concatenate(
        [cell_buf[...].astype(jnp.float32), value_buf[...], var_buf[...]], axis=0
    )
    parts = jnp.concatenate(split_three(table), axis=0)
    lane_hot = (
        lax.broadcasted_iota(jnp.int32, (LANES, n_obs), 0) == (order & (LANES - 1))
    ).astype(jnp.float32).astype(jnp.bfloat16)
    found = bdot(parts, lane_hot)
    size = 3 * table_rows
    found = (found[:size] + found[size : 2 * size]) + found[2 * size :]
    row_hot = lax.broadcasted_iota(jnp.int32, (table_rows, n_obs), 0) == (order >> log2(LANES))

    def take(i):
        rows = found[i * table_rows : (i + 1) * table_rows]
        return jnp.sum(jnp.where(row_hot, rows, 0.0), axis=0, keepdims=True)

    cell = take(0).astype(jnp.int32)
    strip = cell >> log2(n_cols)
    field = strip >> log2(total_rows)
    row = strip & (total_rows - 1)
    col = cell & (n_cols - 1)
    as_float = lambda x: x.astype(jnp.float32)
    zero = jnp.zeros((1, n_obs), jnp.float32)
    finish(copies[4:])
    for f in range(n_fields):
        kappa_ref[f : f + 1, :] = jnp.full((1, LANES), diffusion_buf[0, f], jnp.float32)
    up = lax.broadcasted_iota(jnp.int32, (8, 8), 0)
    along = lax.broadcasted_iota(jnp.int32, (8, 8), 1)
    mask = jnp.zeros((8, 8), jnp.float32)
    for f in range(n_fields):
        for b in range(n_fields):
            mask = jnp.where((up == f) & (along == b), as_float(mask_buf[f, b]), mask)
    field_hot = as_float(lax.broadcasted_iota(jnp.int32, (8, n_obs), 0) == field)
    info = jnp.concatenate(
        [
            as_float(field), as_float(row), as_float(col), take(1), take(2), as_float(strip), zero, zero,
            bdot(mask.astype(jnp.bfloat16), field_hot.astype(jnp.bfloat16)),
        ],
        axis=0,
    )
    info_ref[...] = info


def forecast_kernel(
    place_ref, kappa_ref, own_ref, other_ref, vel_own_ref, vel_other_ref, info_ref,
    send_ref, field_buf, prior_buf,
):
    n_fields, n_rows, n_cols = field_buf.shape
    half = n_rows // 2
    n_dest = half
    chunk = send_ref.shape[0] // n_dest
    first_slab = place_ref[0:1, 0:1] < 0.5

    def whole_of(own, other):
        return jnp.concatenate([jnp.where(first_slab, own, other), jnp.where(first_slab, other, own)], axis=0)

    u = whole_of(vel_own_ref[0], vel_other_ref[0])
    v = whole_of(vel_own_ref[1], vel_other_ref[1])
    row = lax.broadcasted_iota(jnp.int32, (n_rows, n_cols), 0)
    col = lax.broadcasted_iota(jnp.int32, (n_rows, n_cols), 1)
    u_pos, u_neg = jnp.maximum(u, 0.0), jnp.minimum(u, 0.0)
    v_pos, v_neg = jnp.maximum(v, 0.0), jnp.minimum(v, 0.0)
    outflow = (u_neg - u_pos) + (v_neg - v_pos)
    cells, weights = [], []
    for f in range(n_fields):
        kappa = kappa_ref[f : f + 1, 0:1]
        weights.append((
            (1.0 - 4.0 * kappa) + outflow,
            jnp.where(row == 0, 0.0, kappa + v_pos),
            jnp.where(row == n_rows - 1, 0.0, kappa - v_neg),
            jnp.where(col == 0, 0.0, kappa + u_pos),
            jnp.where(col == n_cols - 1, 0.0, kappa - u_neg),
        ))
        cells.append(whole_of(own_ref[0, f], other_ref[0, f]))
    for _ in range(SUBSTEPS):
        for f in range(n_fields):
            c = cells[f]
            k_c, k_n, k_s, k_w, k_e = weights[f]
            cells[f] = (
                (c * k_c + pltpu.roll(c, 1, 0) * k_n)
                + (pltpu.roll(c, n_rows - 1, 0) * k_s + pltpu.roll(c, 1, 1) * k_w)
                + pltpu.roll(c, n_cols - 1, 1) * k_e
            )
    for f in range(n_fields):
        field_buf[f] = cells[f]
    whole = field_buf[...].reshape(n_fields * n_rows, n_cols)
    strips = n_fields * n_rows
    parts = jnp.concatenate(split_two(whole), axis=0)
    n_obs = info_ref.shape[1]
    width = 2 * LANES
    strip_ids = lax.broadcasted_iota(jnp.int32, (strips, width), 0)
    col_ids = lax.broadcasted_iota(jnp.int32, (n_cols, width), 0)
    for q in range(n_obs // width):
        cols = info_ref[2:3, q * width : (q + 1) * width].astype(jnp.int32)
        strip = info_ref[5:6, q * width : (q + 1) * width].astype(jnp.int32)
        hot = (col_ids == cols).astype(jnp.float32).astype(jnp.bfloat16)
        found = bdot(parts, hot)
        found = found[:strips] + found[strips:]
        values = jnp.sum(jnp.where(strip_ids == strip, found, 0.0), axis=0, keepdims=True)
        for h in range(width // LANES):
            at = q * (width // LANES) + h
            prior_buf[at : at + 1, :] = values[:, h * LANES : (h + 1) * LANES]
    priors = prior_buf[...]
    lead = chunk - n_obs // LANES
    for d in range(n_dest):
        send_ref[d * chunk + lead : (d + 1) * chunk, :] = priors
    pieces = n_cols // LANES
    for f in range(n_fields):
        rows = jnp.where(first_slab, field_buf[f, :half, :], field_buf[f, half:, :])
        for i, dest in enumerate(exchange_order(n_dest)):
            for h in range(pieces):
                at = i * chunk + f * pieces + h
                send_ref[at : at + 1, :] = rows[dest : dest + 1, h * LANES : (h + 1) * LANES]
    for i in range(n_fields * pieces, lead):
        send_ref[pl.ds(i, n_dest, stride=chunk), :] = jnp.zeros((n_dest, LANES), jnp.float32)


def closeness_of(dist_sq):
    inverse = lax.rsqrt(jnp.maximum(dist_sq, 1e-6))
    z = dist_sq * inverse
    half_sq = 0.5 * dist_sq
    inner = 1.0 + dist_sq * ((half_sq - 5.0 / 3.0) + z * (0.625 - 0.5 * half_sq))
    left = jnp.maximum(2.0 - z, 0.0)
    left = left * left
    left = left * left
    outer = left * ((dist_sq + (z + z)) - 0.5) * (inverse * (1.0 / 12.0))
    return jnp.where(dist_sq <= 1.0, inner, outer)


def loc_kernel(
    place_ref, info_ref, pair_hi_ref, pair_lo_ref, rest_hbm, cell_hi_hbm, cell_lo_hbm,
    infot_ref, rest_ref, cell_hi_ref, cell_lo_ref, gap_buf, sems,
):
    n_obs = info_ref.shape[1]
    batch, n_pair = pair_hi_ref.shape
    n_cols = cell_hi_ref.shape[1]
    scale = 1.0 / LOC_HALF
    far = 32.0 * LOC_HALF * LOC_HALF
    row, col = info_ref[1:2, :], info_ref[2:3, :]
    norm = [part.astype(jnp.float32) for part in split_three(row * row + col * col)]
    one = jnp.ones((1, n_obs), jnp.float32)
    hot = lax.broadcasted_iota(jnp.int32, (8, n_obs), 0) == info_ref[0:1, :].astype(jnp.int32)
    zeros = jnp.zeros((6, n_obs), jnp.float32)
    feature_k = jnp.concatenate(
        norm + [one, one, one, -2.0 * row, -2.0 * col, -far * info_ref[8:16, :], one * far, row, zeros], axis=0
    )
    feature_j = jnp.concatenate(
        [one, one, one] + norm + [row, col, hot.astype(jnp.float32), one], axis=0
    )[:, batch:]
    infot_ref[...] = feature_k.T
    terms = feature_j.shape[0]
    gap_buf[...] = bdot(
        infot_ref[0:batch, 0:terms].astype(jnp.bfloat16), (feature_j * (scale * scale)).astype(jnp.bfloat16)
    )
    table_rows = 32
    own_row = place_ref[1:2, 0:1]
    gap_row = (lax.broadcasted_iota(jnp.int32, (table_rows, LANES), 0).astype(jnp.float32) - own_row) * scale
    gap_col = lax.broadcasted_iota(jnp.int32, (table_rows, LANES), 1).astype(jnp.float32) * scale
    by_row = jnp.concatenate(split_three(closeness_of(gap_row * gap_row + gap_col * gap_col)), axis=0)
    row_ids = lax.broadcasted_iota(jnp.int32, (1, 3 * table_rows), 1) & (table_rows - 1)
    copies = []
    col_at, row_at = 7, terms
    for b in range(BATCHES):
        span = slice(b * batch, (b + 1) * batch)
        rows = infot_ref[span, row_at : row_at + 1].astype(jnp.int32)
        hot = (row_ids == rows).astype(jnp.float32).astype(jnp.bfloat16)
        table = bdot(hot, by_row)
        cols = infot_ref[span, col_at : col_at + 1] * -0.5
        col_k = jnp.broadcast_to(cols, (batch, LANES)).astype(jnp.int32)
        for h in range(n_cols // LANES):
            here = slice(h * LANES, (h + 1) * LANES)
            col = lax.broadcasted_iota(jnp.int32, (batch, LANES), 1) + h * LANES
            gap = jnp.minimum(jnp.abs(col - col_k), LANES - 1)
            at_hi, at_lo = split_two(jnp.take_along_axis(table, gap, axis=1))
            cell_hi_ref[span, here] = at_hi
            cell_lo_ref[span, here] = at_lo
        copies += start_copies(
            [
                (cell_hi_ref.at[span, :], cell_hi_hbm.at[span, :]),
                (cell_lo_ref.at[span, :], cell_lo_hbm.at[span, :]),
            ],
            sems.at[2 * b :],
        )
    step = 128
    kept = pair_lo_ref.shape[0]

    def pair_rows(low_ref, first):
        def body(i, carry):
            to = pl.multiple_of(i * step, step)
            at = pl.multiple_of(first + i * step, step)
            for h in range(n_pair // LANES):
                here = slice(h * LANES, (h + 1) * LANES)
                high, low = split_two(closeness_of(gap_buf[pl.ds(at, step), here]))
                pair_hi_ref[pl.ds(at, step), here] = high
                low_ref[pl.ds(to, step), here] = low
            return carry

        lax.fori_loop(0, low_ref.shape[0] // step, body, 0)

    pair_rows(rest_ref, kept)
    copies += start_copies([(rest_ref, rest_hbm)], sems.at[2 * BATCHES :])
    pair_rows(pair_lo_ref, 0)
    finish(copies)


def member_roll(x, shift):
    shift = shift % x.shape[0]
    return pltpu.roll(x, shift, 0) if shift else x


def factors(priors, value, var):
    members = priors.shape[0]
    average = jnp.sum(priors, axis=0, keepdims=True) * (1.0 / members)
    anomaly = priors - average
    variance = jnp.sum(anomaly * anomaly, axis=0, keepdims=True) * (1.0 / (members - 1)) + var
    root = jnp.sqrt(variance)
    shrunk = anomaly * (1.0 / ((members - 1) * (root * (jnp.sqrt(var) + root))))
    rows = [shrunk * member_roll(anomaly, -d) for d in range(members // 2)]
    rows.append(anomaly * ((value - average) / ((members - 1) * variance)))
    return rows


def combined(state, sums):
    members = state.shape[0]
    half = members // 2
    centred = state - jnp.sum(state, axis=0, keepdims=True) * (1.0 / members)
    block = lambda d: sums[d * members : (d + 1) * members]
    across = member_roll(centred, half)
    move = (centred - across) * block(0)
    for d in range(1, half):
        move = move + (member_roll(centred, -d) - across) * block(d)
        move = move + member_roll((centred - member_roll(across, -d)) * block(d), d)
    shift = jnp.sum(centred * block(half), axis=0, keepdims=True)
    return state + (shift - move)


def update_kernel(
    recv_ref, info_ref, pair_hi_ref, pair_lo_ref, rest_hbm, cell_hi_hbm, cell_lo_hbm,
    out_ref, fac_buf, sums_buf, mask_buf, rest_ref, cell_hi_ref, cell_lo_ref, sems, *, members, n_fields,
):
    tables = [(rest_hbm, rest_ref), (cell_hi_hbm, cell_hi_ref), (cell_lo_hbm, cell_lo_ref)]
    copies = [pltpu.make_async_copy(src, dst, sems.at[i]) for i, (src, dst) in enumerate(tables)]
    n_obs = info_ref.shape[1]
    batch = n_obs // BATCHES
    chunk = recv_ref.shape[0] // members
    per_chunk = n_obs // LANES
    lead = chunk - per_chunk
    pieces = cell_hi_ref.shape[1] // LANES
    size = fac_buf.shape[1] // 2
    kept = pair_lo_ref.shape[0]

    def member_row(i):
        return recv_ref[pl.ds(i, members, stride=chunk), :]

    def priors_of(b):
        first = lead + b * (per_chunk // BATCHES)
        return jnp.concatenate([member_row(first + q) for q in range(per_chunk // BATCHES)], axis=1)

    def set_factors(b, priors):
        span = slice(b * batch, (b + 1) * batch)
        rows = factors(priors, info_ref[3:4, span], info_ref[4:5, span])
        for i, r in enumerate(rows):
            high, low = split_two(r)
            fac_buf[b, i * members : (i + 1) * members, :] = high
            fac_buf[b, size + i * members : size + (i + 1) * members, :] = low

    def run(step, carry):
        @pl.when(step == 0)
        def _():
            for copy in copies:
                copy.start()
            set_factors(0, priors_of(0))
            first = bdot(fac_buf[0], pair_hi_ref[...])
            sums_buf[...] = (first[:size] + first[size:]) + bdot(fac_buf[0, :size, :kept], pair_lo_ref[...])

        @pl.when(step == 1)
        def _():
            finish(copies[:1])
            sums = sums_buf[...] + bdot(fac_buf[0, :size, kept:], rest_ref[...])
            set_factors(1, combined(priors_of(1), sums))

        @pl.when(step == 2)
        def _():
            finish(copies[1:])
            states = [
                jnp.concatenate([member_row(f * pieces + h) for h in range(pieces)], axis=1)
                for f in range(n_fields)
            ]
            all_rows = n_fields * size
            for b in range(BATCHES):
                span = slice(b * batch, (b + 1) * batch)
                for f in range(n_fields):
                    open_to = info_ref[8 + f : 9 + f, span].astype(jnp.bfloat16)
                    mask_buf[f * size : (f + 1) * size, :] = fac_buf[b, :size, :] * open_to
                    mask_buf[all_rows + f * size : all_rows + (f + 1) * size, :] = fac_buf[b, size:, :] * open_to
                first = bdot(mask_buf[...], cell_hi_ref[span, :])
                sums = (first[:all_rows] + first[all_rows:]) + bdot(mask_buf[:all_rows, :], cell_lo_ref[span, :])
                states = [combined(state, sums[f * size : (f + 1) * size]) for f, state in enumerate(states)]
            for f in range(n_fields):
                for i, member in enumerate(exchange_order(members)):
                    out_ref[member, f, 0, :, :] = states[f][i : i + 1]

        return carry

    lax.fori_loop(0, 3, run, 0)


def vmem_spec():
    return pl.BlockSpec(memory_space=pltpu.VMEM)


def smem_spec():
    return pl.BlockSpec(memory_space=pltpu.SMEM)


def hbm_spec():
    return pl.BlockSpec(memory_space=pltpu.HBM)


def in_hbm(x):
    return pltpu.with_memory_space_constraint(x, pltpu.HBM)


def quick_device(
    realization_stack, velocity, diffusion, obs_cell, obs_order, obs_value, obs_var, field_mask
):
    _, n_fields, rows_here, n_cols = realization_stack.shape
    n_mem = lax.axis_size("mem")
    total_rows = 2 * rows_here
    n_obs = obs_cell.shape[0]
    batch = n_obs // BATCHES
    slab_index = lax.axis_index("row")
    own_row = slab_index * rows_here + lax.axis_index("mem")
    place = jnp.where(
        lax.broadcasted_iota(jnp.int32, (8, LANES), 0) == 0, slab_index, own_row
    ).astype(jnp.float32)
    params = pltpu.CompilerParams(vmem_limit_bytes=16 * MEGA)
    shape = jax.ShapeDtypeStruct
    f32, i32 = jnp.float32, jnp.int32
    swap = [(0, 1), (1, 0)]
    other = lax.ppermute(realization_stack, "row", swap)
    vel_other = lax.ppermute(velocity, "row", swap)
    table = (n_obs // LANES, LANES)
    info, own, vel_own, kappa = pl.pallas_call(
        functools.partial(prep_kernel, total_rows=total_rows, n_cols=n_cols),
        out_shape=(
            shape((16, n_obs), f32),
            shape(realization_stack.shape, f32),
            shape(velocity.shape, f32),
            shape((8, LANES), f32),
        ),
        in_specs=[hbm_spec()] * 8,
        out_specs=(vmem_spec(),) * 4,
        scratch_shapes=[
            pltpu.VMEM((1, n_obs), i32),
            pltpu.VMEM(table, i32),
            pltpu.VMEM(table, f32),
            pltpu.VMEM(table, f32),
            pltpu.SMEM(field_mask.shape, i32),
            pltpu.SMEM((1, n_fields), f32),
            pltpu.SemaphoreType.DMA((8,)),
        ],
        compiler_params=params,
        name="prep",
    )(
        in_hbm(obs_order.reshape(1, n_obs)),
        in_hbm(obs_cell.reshape(table)),
        in_hbm(obs_value.reshape(table)),
        in_hbm(obs_var.reshape(table)),
        in_hbm(field_mask),
        in_hbm(diffusion.reshape(1, n_fields)),
        in_hbm(realization_stack),
        in_hbm(velocity),
    )
    chunk = (n_fields * n_cols + n_obs) // LANES
    send = pl.pallas_call(
        forecast_kernel,
        out_shape=shape((n_mem * chunk, LANES), f32),
        in_specs=[vmem_spec()] * 7,
        out_specs=vmem_spec(),
        scratch_shapes=[
            pltpu.VMEM((n_fields, total_rows, n_cols), f32),
            pltpu.VMEM((n_obs // LANES, LANES), f32),
        ],
        compiler_params=params,
        name="forecast",
    )(place, kappa, own, other, vel_own, vel_other, info)
    recv = lax.all_to_all(
        send.reshape(n_mem, chunk, 1, LANES),
        "mem",
        split_axis=0,
        concat_axis=0,
        axis_index_groups=[exchange_order(n_mem)],
        tiled=True,
    ).reshape(send.shape)
    n_pair = n_obs - batch
    bf16 = jnp.bfloat16
    kept = batch // 2
    pair_hi, pair_lo, rest, cell_hi, cell_lo = pl.pallas_call(
        loc_kernel,
        out_shape=(
            shape((batch, n_pair), bf16),
            shape((kept, n_pair), bf16),
            pltpu.HBM((batch - kept, n_pair), bf16),
            pltpu.HBM((n_obs, n_cols), bf16),
            pltpu.HBM((n_obs, n_cols), bf16),
        ),
        in_specs=[vmem_spec(), vmem_spec()],
        out_specs=(vmem_spec(), vmem_spec(), hbm_spec(), hbm_spec(), hbm_spec()),
        scratch_shapes=[
            pltpu.VMEM((n_obs, 24), f32),
            pltpu.VMEM((batch - kept, n_pair), bf16),
            pltpu.VMEM((n_obs, n_cols), bf16),
            pltpu.VMEM((n_obs, n_cols), bf16),
            pltpu.VMEM((batch, n_pair), f32),
            pltpu.SemaphoreType.DMA((2 * BATCHES + 1,)),
        ],
        compiler_params=params,
        name="localize",
    )(place, info)
    rows = n_mem * (n_mem // 2 + 1)
    return pl.pallas_call(
        functools.partial(update_kernel, members=n_mem, n_fields=n_fields),
        out_shape=shape((n_mem, n_fields, 1, 1, n_cols), f32),
        in_specs=[vmem_spec()] * 4 + [hbm_spec()] * 3,
        out_specs=vmem_spec(),
        scratch_shapes=[
            pltpu.VMEM((BATCHES, 2 * rows, batch), bf16),
            pltpu.VMEM((rows, n_pair), f32),
            pltpu.VMEM((2 * rows * n_fields, batch), bf16),
            pltpu.VMEM((batch - kept, n_pair), bf16),
            pltpu.VMEM((n_obs, n_cols), bf16),
            pltpu.VMEM((n_obs, n_cols), bf16),
            pltpu.SemaphoreType.DMA((3,)),
        ],
        compiler_params=params,
        name="update",
    )(recv, info, pair_hi, pair_lo, in_hbm(rest), in_hbm(cell_hi), in_hbm(cell_lo))


def is_quick(realization_stack, obs_cell, n_mem, n_slab):
    local_members, n_fields, rows_here, n_cols = realization_stack.shape
    powers = all(n & (n - 1) == 0 for n in (rows_here, n_cols))
    return (
        n_slab == 2
        and local_members == 1
        and n_mem == rows_here == 16
        and n_fields <= 8
        and LOC_HALF * 2 <= LANES - 1
        and powers
        and n_cols % LANES == 0
        and obs_cell.shape[0] == 8 * n_cols
        and BATCHES == 2
    )


def per_device(
    realization_stack, velocity, diffusion, obs_cell, obs_order, obs_value, obs_var, field_mask
):
    local_members = realization_stack.shape[0]
    n_fields = realization_stack.shape[1]
    rows_here = realization_stack.shape[2]
    n_cols = realization_stack.shape[3]
    n_mem = lax.axis_size("mem")
    n_slab = lax.axis_size("row")
    total_members = local_members * n_mem
    total_rows = rows_here * n_slab
    if is_quick(realization_stack, obs_cell, n_mem, n_slab):
        return quick_device(
            realization_stack, velocity, diffusion, obs_cell, obs_order, obs_value, obs_var, field_mask
        )
    slab_index = lax.axis_index("row")
    member_index = lax.axis_index("mem")
    row_sub = rows_here // n_mem
    current = realization_stack
    for substep in range(SUBSTEPS):
        padded = extended(current, (("row", 2),), 1)
        current = advance(padded, velocity, diffusion)
    field_all, row_all, col_all = decode(obs_cell, total_rows, n_cols)
    batch_size = obs_cell.shape[0] // BATCHES
    layout = lax.all_to_all(current, "mem", split_axis=2, concat_axis=0, tiled=True)
    ensemble_now = layout.reshape(total_members, -1)
    base_row = slab_index * rows_here + member_index * row_sub
    for batch_num in range(BATCHES):
        picked = obs_order[batch_num * batch_size : (batch_num + 1) * batch_size]
        obs_field = field_all[picked]
        obs_row = row_all[picked]
        obs_col = col_all[picked]
        owned = ((obs_row >= base_row) & (obs_row < base_row + row_sub)).astype(jnp.float32)
        local_ids = (
            obs_field * row_sub * n_cols
            + jnp.clip(obs_row - base_row, 0, row_sub - 1) * n_cols
            + obs_col
        )
        partial_priors = jnp.take(ensemble_now, local_ids, axis=1) * owned[None, :]
        priors = lax.psum(partial_priors, ("mem", "row"))
        anomaly, adjust = innovations(priors, obs_value[picked], obs_var[picked])
        ensemble_now = regress(
            ensemble_now, base_row, obs_field, obs_row, obs_col, anomaly, adjust, field_mask, n_cols
        )
    return ensemble_now.reshape(total_members, n_fields, 1, row_sub, n_cols)


def solution(mesh):
    in_specs = (P("mem", None, "row", None), P(None, "row", None), P(), P(), P(), P(), P(), P())
    out_specs = P(None, None, "row", "mem", None)
    return jax.shard_map(
        per_device, mesh=mesh, in_specs=in_specs, out_specs=out_specs, check_vma=False
    )
```
